32 devices in a mesh: groups: 2 (over y), tm: 4 (over z), lon: 2 (over x), probe: 2 (over core).
Axes of the slice: x: 2, y: 2, z: 4, core: 2. Of those that a mesh axis runs over, the one named last changes fastest.
Arguments:
- winds: bfloat16 [2, 8, 2, 36, 72, 192], P(None, ('groups', 'tm'), None, None, 'lon'), parts along dimension 1, may hold values from -0.44921875 to 0.44921875
- mixing: float32 [36, 36], replicated, as said below
- obs_cell: int32 [8, 2, 2048], P(('groups', 'tm'), 'lon'), parts along dimension 0, may hold values from 0 to 248831
- obs_weight: float32 [8, 2, 2048], P(('groups', 'tm'), 'lon'), parts along dimension 0, may hold values from 0.5 to 4
- probe_sign: int32 [4, 8, 2, 2048], P('probe', ('groups', 'tm'), 'lon'), parts along dimension 1, may hold values from 0 to 1
- week_map: int32 [8, 2], P(('groups', 'tm')), parts along dimension 0, may hold values from 0 to 1
- prior_precision: float32 [4, 72, 192], P('groups', 'lon', 'tm'), parts along dimension 0, may hold values from 0.1 to 1
Outputs:
- hessian_diag: float32 [2, 4, 72, 192], P('probe', 'groups', 'lon', 'tm'), parts along dimension 1
The draws below stay inside these ranges and needn't reach their ends.
There are 2 independent parts, one for each index of `groups`. The reference program is written for one: setup_inputs(seed, part) draws one part's arguments, and reference() takes and returns one part's arrays. A program takes and returns all parts, laid end to end along the dimension named above; an argument that names none is the same for every part. Nothing has to cross between parts.
Inputs may be any that keep to these rules, and one draw needn't show every extreme that they name: mixing = 0.55 on the diagonal plus 0.45 / 36 times a factor between 0.5 and 1.4 in every entry.
All inputs are finite; a program needn't handle non-finite values.
Results may differ from the reference program's by a relative error of at most 0.0003.
Values may be sent and summed in bfloat16 or wider, within the bound.
A program may use at most 128 MiB of HBM per device.

```python
import math
import jax
import jax.numpy as jnp
from jax import lax

LEV = 36
LAT = 192
LON_DEV = 36
HOURS = 2
PROBE_DEV = 2
OBS_DEV = 2048
WEEKS = 2
SECTIONS = 4
BANDS = 2
LONS = 72
PROBE_SETS = 2
PROBES = 4


def draw_mixing(key, part):
    spread = jax.random.uniform(key, (LEV, LEV), jnp.float32, 0.5, 1.4)
    diagonal = (jnp.arange(LEV)[:, None] == jnp.arange(LEV)[None, :]).astype(jnp.float32)
    return 0.55 * diagonal + 0.45 * spread / LEV


def plant(drawn, key, least, high):
    extent = drawn.shape
    index_at = [jax.random.randint(jax.random.fold_in(key, axis), (), 0, extent[axis]) for axis in range(len(extent))]
    drawn = drawn.at[tuple(index_at)].set(least)
    longest = extent.index(max(extent))
    index_at[longest] = (index_at[longest] + 1) % extent[longest]
    return drawn.at[tuple(index_at)].set(high)


def block_levels(key, extent, cuts, low, largest):
    gain = 1.0
    for axis_at, parts in cuts:
        steps = jax.random.uniform(jax.random.fold_in(jax.random.fold_in(key, 6), axis_at), (parts,), jnp.float32, low / len(cuts), largest / len(cuts))
        gain = gain * jnp.repeat(jnp.exp(steps), extent[axis_at] // parts).reshape((-1,) + (1,) * (len(extent) - 1 - axis_at))
    return gain


def setup_inputs(seed: int = 0, part: int = 0) -> dict:
    key_of = jax.random.split(jax.random.key(seed), 8)
    part_splits = jax.random.split(jax.random.fold_in(key_of[7], part), 8)
    return {
        "winds": jnp.clip(jax.random.uniform(part_splits[0], (2, SECTIONS, HOURS, LEV, LONS, LAT), jnp.float32, -0.44921875, 0.44921875) * block_levels(part_splits[0], (2, SECTIONS, HOURS, LEV, LONS, LAT), ((1, 4), (4, 2)), -0.4, 0.0), -0.44921875, 0.44921875).astype(jnp.bfloat16),
        "mixing": draw_mixing(jax.random.fold_in(key_of[7], 71), part),
        "obs_cell": plant(jax.random.randint(part_splits[2], (SECTIONS, BANDS, OBS_DEV), 0, LEV * LON_DEV * LAT), jax.random.fold_in(part_splits[2], 1), 0, (LEV * LON_DEV * LAT) - 1).astype(jnp.int32),
        "obs_weight": jnp.clip(jnp.exp(math.log(4.0) - 2.0794415 * jax.random.uniform(part_splits[3], (SECTIONS, BANDS, OBS_DEV), jnp.float32) ** block_levels(part_splits[3], (SECTIONS, BANDS, OBS_DEV), ((0, 4), (1, 2)), -0.2, 0.2)), 0.5, 4.0),
        "probe_sign": plant(jax.random.randint(part_splits[4], (PROBES, SECTIONS, BANDS, OBS_DEV), 0, 2), jax.random.fold_in(part_splits[4], 1), 0, 1).astype(jnp.int32),
        "week_map": plant(jax.random.randint(part_splits[5], (SECTIONS, HOURS), 0, WEEKS), jax.random.fold_in(part_splits[5], 1), 0, WEEKS - 1).astype(jnp.int32),
        "prior_precision": jnp.clip(jnp.exp(math.log(1.0) - 2.3025851 * jax.random.uniform(part_splits[6], (WEEKS, LONS, LAT), jnp.float32) ** block_levels(part_splits[6], (WEEKS, LONS, LAT), ((1, 2), (2, 4)), -0.2, 0.2)), 0.1, 1.0),
    }


def adjoint_step(adjoint, east_face, north_face, mixing):
    adjoint = jnp.einsum('lk,...lxy->...kxy', mixing, adjoint, precision=lax.Precision.HIGHEST)
    east_pos = jnp.maximum(east_face, 0.0)
    west_neg = jnp.minimum(jnp.roll(east_face, 1, axis=-2), 0.0)
    adjoint = adjoint + east_pos * (jnp.roll(adjoint, -1, axis=-2) - adjoint) + west_neg * (adjoint - jnp.roll(adjoint, 1, axis=-2))
    lat_count = north_face.shape[-1]
    row_keep = (jnp.arange(lat_count) < lat_count - 1).astype(north_face.dtype)
    north_cut = north_face * row_keep
    north_pos = jnp.maximum(north_cut, 0.0)
    south_neg = jnp.minimum(jnp.concatenate([jnp.zeros_like(north_cut[..., :1]), north_cut[..., :-1]], axis=-1), 0.0)
    above_row = jnp.concatenate([adjoint[..., 1:], jnp.zeros_like(adjoint[..., :1])], axis=-1)
    below_row = jnp.concatenate([jnp.zeros_like(adjoint[..., :1]), adjoint[..., :-1]], axis=-1)
    return adjoint + north_pos * (above_row - adjoint) + south_neg * (adjoint - below_row)


def reference(winds, mixing, obs_cell, obs_weight, probe_sign, week_map, prior_precision):
    sign_vals = (2 * probe_sign - 1).astype(jnp.float32)
    value = sign_vals * obs_weight[None]
    level_id = obs_cell // (LON_DEV * LAT)
    remainder = obs_cell % (LON_DEV * LAT)
    column = remainder // LAT
    lat_id = remainder % LAT
    global_col = column + (jnp.arange(BANDS, dtype=jnp.int32) * LON_DEV)[None, :, None]
    flat_index = ((level_id * LONS + global_col) * LAT + lat_id).astype(jnp.int32)
    hour_count = SECTIONS * HOURS

    def per_hour(state_pair, step_id):
        adjoint, flux_adj = state_pair
        section_id = step_id // HOURS
        hour_id = step_id % HOURS
        places = lax.dynamic_index_in_dim(flat_index, section_id, 0, keepdims=False).reshape(-1)
        hour_gate = (hour_id == 0).astype(jnp.float32)
        injected = lax.dynamic_index_in_dim(value, section_id, 1, keepdims=False) * hour_gate
        adjoint = adjoint.reshape(PROBES, -1).at[:, places].add(injected.reshape(PROBES, -1)).reshape(PROBES, LEV, LONS, LAT)
        week_id = week_map[section_id, hour_id]
        onehot = (jnp.arange(WEEKS) == week_id).astype(jnp.float32)
        flux_adj = flux_adj + onehot[None, :, None, None] * adjoint[:, None, 0]
        east_face = winds[0, section_id, hour_id].astype(jnp.float32)
        north_face = winds[1, section_id, hour_id].astype(jnp.float32)
        adjoint = adjoint_step(adjoint, east_face, north_face, mixing)
        return (adjoint, flux_adj), None

    start = (jnp.zeros((PROBES, LEV, LONS, LAT), jnp.float32), jnp.zeros((PROBES, WEEKS, LONS, LAT), jnp.float32))
    (adjoint, flux_adj), unused = lax.scan(per_hour, start, jnp.arange(hour_count - 1, -1, -1, dtype=jnp.int32))
    squares = (flux_adj * flux_adj).reshape(PROBE_SETS, PROBE_DEV, WEEKS, LONS, LAT)
    return prior_precision[None] + jnp.mean(squares, axis=1)
```

```python
import functools

import jax
import jax.numpy as jnp
from jax import lax
from jax.experimental import pallas as pl
from jax.experimental.pallas import tpu as pltpu
from jax.sharding import PartitionSpec as P

WIDE = 4
PAD = 40


def split2(x):
    high = x.astype(jnp.bfloat16)
    low = (x - high.astype(jnp.float32)).astype(jnp.bfloat16)
    return high, low


def plan(sections, bands, hours_sec, cols, levels, lat_rows, own, probes, weeks, count):
    hours = sections * hours_sec
    halo = -(-hours // WIDE) * WIDE
    window = -(-(own + 2 * hours) // 64) * 64
    d = dict(
        sections=sections, bands=bands, hours_sec=hours_sec, cols=cols, levels=levels,
        lat_rows=lat_rows, own=own, probes=probes, weeks=weeks, count=count, hours=hours,
        halo=halo, left=hours, window=window, lanes=window * probes,
        half=cols // 4, halo_pairs=halo // 2, pairs=(cols + 2 * halo) // 2,
        blocks=(cols + 2 * halo) // WIDE,
    )
    d["stride"] = levels if d["lanes"] == 128 else -(-levels // 8) * 8
    d["block"] = WIDE * d["stride"]
    d["rows"] = PAD + (d["blocks"] + 1) * d["block"]
    d["early"] = hours <= 8
    return d


def fused_kernel(d, winds, mixing, cell, weight, sign, week, *refs):
    sections, bands, hours_sec, hours = d["sections"], d["bands"], d["hours_sec"], d["hours"]
    cols, levels, lat_rows, own = d["cols"], d["levels"], d["lat_rows"], d["own"]
    probes, count, halo, left = d["probes"], d["count"], d["halo"], d["left"]
    window, lanes, half, halo_pairs = d["window"], d["lanes"], d["half"], d["halo_pairs"]
    block, early, stride = d["block"], d["early"], d["stride"]
    if early:
        est, land, refs = refs[0], refs[1], refs[2:]
        stage = None
    else:
        est, land, stage, refs = refs[0], refs[1], refs[2], refs[3:]
    (pack, flat, obs, lhs, state, mixed, inj, ep, wm, npos, sneg, flux,
     zs, zr, hs, hr, xs, xr, os, orr, us, ur, local) = refs
    own_pairs = 2 * half
    me = lax.axis_index("tm")
    band = lax.axis_index("lon")
    core = lax.axis_index("probe")
    sides = [lax.rem(band + bands - 1, bands), lax.rem(band + 1, bands)]
    if bands == 2:
        greet = sides[:1]
    else:
        greet = sides

    def remote(src, dst, send, recv, tm, lon, probe):
        return pltpu.make_async_remote_copy(
            src_ref=src, dst_ref=dst, send_sem=send, recv_sem=recv,
            device_id={"tm": tm, "lon": lon, "probe": probe},
            device_id_type=pl.DeviceIdType.MESH,
        )

    barrier = pltpu.get_barrier_semaphore()

    def hello(tm, lon, probe):
        pl.semaphore_signal(
            barrier, inc=1, device_id={"tm": tm, "lon": lon, "probe": probe},
            device_id_type=pl.DeviceIdType.MESH,
        )

    for k in range(1, sections):
        hello(lax.rem(me + k, sections), band, core)
    for lon in greet:
        for q in range(2):
            hello(me, lon, q)
    hello(me, band, 1 - core)

    obs[me, 0, 0:1, :] = cell[...].astype(jnp.float32)
    value = (2 * sign[...] - 1).astype(jnp.float32) * weight[...]
    obs[me, 0, 1 : 1 + probes, :] = value
    lane_row = lax.broadcasted_iota(jnp.int32, (1, count), 1)
    weeks_row = jnp.zeros((1, count), jnp.float32)
    for h in range(hours_sec):
        weeks_row = jnp.where(lane_row == h, week[0:1, h : h + 1].astype(jnp.float32), weeks_row)
    obs[me, 0, 1 + probes : 2 + probes, :] = weeks_row

    pl.semaphore_wait(barrier, sections - 1 + 2 * len(greet) + 1)

    for k in range(1, sections):
        tm = lax.rem(me + k, sections)
        mine = obs.at[me, 0]
        remote(mine, mine, os.at[k], orr.at[me], tm, band, core).start()

    if stride != levels:
        flat[...] = jnp.zeros_like(flat)
    wl = 2 * window
    lat_tiles = -(-lat_rows // 128)

    def packed_column(h, column, start):
        tiles = []
        for comp in range(2):
            row = []
            for k in range(lat_tiles):
                x = winds[comp, 0, h, column, :, k * 128 : min(k * 128 + 128, lat_rows)]
                x = x.astype(jnp.float32)
                if x.shape[1] < 128:
                    x = jnp.concatenate(
                        [x, jnp.zeros((levels, 128 - x.shape[1]), jnp.float32)], axis=1
                    )
                row.append(x)
            tiles.append(row)
        lane = lax.broadcasted_iota(jnp.int32, (levels, 128), 1)
        parts = []
        for v in range(wl // 128):
            out = jnp.zeros((levels, 128), jnp.float32)
            for comp in range(2):
                begin = comp * window - v * 128
                if begin >= 128 or begin + window <= 0:
                    continue
                shift = lax.rem(begin - start + 512, 128)
                at = lane - begin
                row = at + start
                for k in range(lat_tiles):
                    inside = (
                        (at >= 0) & (at < window) & (row >= k * 128)
                        & (row < min(k * 128 + 128, lat_rows))
                    )
                    out = jnp.where(inside, pltpu.roll(tiles[comp][k], shift, 1), out)
            parts.append(out)
        return parts[0] if len(parts) == 1 else jnp.concatenate(parts, axis=1)

    def fill(h, target, first_column, put):
        start = target * own - left

        def body(i, carry):
            for c in range(2):
                at = pl.multiple_of(i * 2 * stride, 8) + c * stride
                flat[pl.ds(at, levels), :] = packed_column(h, first_column + 2 * i + c, start)
            return carry

        lax.fori_loop(0, half, body, 0, unroll=3)

        def cast(i, carry):
            x = flat[pl.ds(pl.multiple_of(i * 2 * stride, 8), 2 * stride), :]
            put(i, x.astype(jnp.bfloat16))
            return carry

        lax.fori_loop(0, half, cast, 0, unroll=3)

    least = jnp.where(me == 0, 1, 0)
    my_pairs = halo_pairs + half * core

    def z_copy(h, target):
        t = me * hours_sec + h
        return remote(
            pack.at[h, target], land.at[t, pl.ds(my_pairs, half)], zs.at[h, target], zr.at[t],
            target, band, core,
        )

    def job(h, target):
        def put(i, x):
            pack[h, target, i] = x

        fill(h, target, 2 * half * core, put)
        z_copy(h, target).start()

    def every_job(run):
        def upper(i, carry):
            h = hours_sec - 1 - i

            def target(k, inner):
                run(h, sections - 1 - k)
                return inner

            return lax.fori_loop(0, sections - 1 - me, target, carry)

        lax.fori_loop(0, hours_sec - least, upper, 0)

        def lower(i, carry):
            h = hours_sec - 1 - i

            def target(k, inner):
                run(h, k)
                return inner

            return lax.fori_loop(0, me, target, carry)

        lax.fori_loop(0, hours_sec - least, lower, 0)

    every_job(job)

    def at_home(i, carry):
        h = hours_sec - 1 - i
        t = me * hours_sec + h
        for c in range(2):
            if early:

                def put(i, x):
                    land[t, halo_pairs + half * c + i] = x

                fill(h, me, 2 * half * c, put)
            else:

                def put(i, x):
                    pack[h, me, i] = x

                fill(h, me, 2 * half * c, put)
                copy = pltpu.make_async_copy(
                    pack.at[h, me], land.at[t, pl.ds(halo_pairs + half * c, half)], local.at[0]
                )
                copy.start()
                copy.wait()
        return carry

    lax.fori_loop(0, hours_sec - least, at_home, 0)

    zero = jnp.zeros((PAD, lanes), jnp.float32)

    def clear(i, carry):
        at = pl.multiple_of(i * 8, 8)
        state[pl.ds(at, 8), :] = zero[:8]
        mixed[pl.ds(at, 8), :] = zero[:8]
        return carry

    lax.fori_loop(0, d["rows"] // 8, clear, 0, unroll=8)
    flux[...] = jnp.zeros_like(flux)
    lhs[...] = jnp.zeros_like(lhs)
    lhs[0:levels, 0:levels] = mixing[...]
    turned_mix = jnp.transpose(lhs[:, 0:128])
    both = turned_mix + pltpu.roll(pltpu.roll(turned_mix, stride, 0), stride, 1)
    high = both.astype(jnp.bfloat16).astype(jnp.float32)
    low = both - high
    none = jnp.zeros_like(both)
    high = jnp.concatenate([high, none], axis=1)
    low = jnp.concatenate([low, none], axis=1)
    deep = 2 * stride
    matrix = high + pltpu.roll(low, deep, 1) + pltpu.roll(high, 2 * deep, 1)
    lhs[...] = matrix

    def obs_copy(s, n):
        return remote(
            obs.at[s, 0], obs.at[s, 1 + n], us.at[s, n], ur.at[s, n], me, sides[1 - n], core
        )

    beside = range(1 if bands == 2 else 2)

    def hand_obs(s):
        @pl.when(me != s)
        def _():
            remote(obs.at[s, 0], obs.at[s, 0], os.at[0], orr.at[s], me, sides[0], core).wait_recv()

        @pl.when(s > 0)
        def _():
            for n in beside:
                obs_copy(s, n).start()

    def half_copy(t):
        place = land.at[t, pl.ds(my_pairs, half)]
        return remote(place, place, hs.at[t], hr.at[t], me, band, 1 - core)

    def edges(depth):
        found = []
        for side in range(2):
            begin = 0 if side == 0 else own_pairs - depth
            for c in range(2):
                a, b = max(begin, half * c), min(begin + depth, half * (c + 1))
                if a < b:
                    found.append((side, c, a, b))
        return found

    def edge_copy(t, side, c, a, b, q):
        to = halo_pairs + (own_pairs if side == 0 else -own_pairs)
        return remote(
            land.at[t, pl.ds(halo_pairs + a, b - a)], land.at[t, pl.ds(to + a, b - a)],
            xs.at[t, side, q], xr.at[t, side, c], me, sides[side], q,
        )

    def with_depth(t, act):
        @pl.when(t > halo // 2)
        def _():
            act(halo_pairs)

        @pl.when(t <= halo // 2)
        def _():
            act(halo_pairs // 2)

    def hand_winds(t):
        s = t // hours_sec

        @pl.when(me != s)
        def _():
            place = land.at[t, pl.ds(my_pairs, half)]
            remote(place, place, zs.at[0, 0], zr.at[t], me, sides[0], core).wait_recv()

        def act(depth):
            for c in range(2):

                @pl.when(core == c)
                def _():
                    for side, sender, a, b in edges(depth):
                        if sender == c:
                            for q in range(2):
                                edge_copy(t, side, sender, a, b, q).start()

        with_depth(t, act)

        @pl.when(me != s)
        def _():
            half_copy(t).start()

    def take_winds(t):
        s = t // hours_sec

        @pl.when(me != s)
        def _():
            place = land.at[t, pl.ds(halo_pairs + half * (1 - core), half)]
            remote(place, place, hs.at[t], hr.at[t], me, band, 1 - core).wait_recv()

        def act(depth):
            for side, sender, a, b in edges(depth):
                edge_copy(t, side, sender, a, b, 0).wait_recv()

        with_depth(t, act)

    first_row = me * own - left

    def observed(s, piece):
        place = obs[s, piece, 0:1, :].astype(jnp.int32)
        level = place // (cols * lat_rows)
        rest = place - level * (cols * lat_rows)
        column = rest // lat_rows
        row = rest - column * lat_rows - first_row
        hit = lax.broadcasted_iota(jnp.int32, (window, count), 0) == row
        parts = [
            split2(jnp.where(hit, obs[s, piece, 1 + p : 2 + p, :], 0.0)) for p in range(probes)
        ]
        rhs = jnp.concatenate([x[0] for x in parts] + [x[1] for x in parts], axis=0)
        return level, column, rhs

    def placed_sum(hot, rhs):
        got = lax.dot_general(
            hot.astype(jnp.float32).astype(jnp.bfloat16), rhs, (((1,), (1,)), ((), ())),
            preferred_element_type=jnp.float32,
        )
        return got[:, :lanes] + got[:, lanes:]

    def lowest(t):
        return (halo - t) // WIDE

    def highest(t):
        return (halo + cols + t + WIDE - 1) // WIDE

    edge_blocks = halo // WIDE
    own_blocks = cols // WIDE
    together = max(n for n in range(1, 4) if own_blocks % n == 0)

    def inject(s, slot):
        t = s * hours_sec
        for n in beside:
            remote(
                obs.at[s, 0], obs.at[s, 1 + n], us.at[s, n], ur.at[s, n], me, sides[0], core
            ).wait_recv()
        for piece, shift, begin, end, step in (
            (0, halo, edge_blocks, edge_blocks + own_blocks, together),
            (1, halo - cols, lowest(t), edge_blocks, 1),
            (2 if bands > 2 else 1, halo + cols, edge_blocks + own_blocks, highest(t), 1),
        ):
            level, column, rhs = observed(s, piece)
            place = (column + shift) * stride + level
            high_rows = step * block
            chunk = lax.broadcasted_iota(jnp.int32, (high_rows, count), 0)

            def body(i, carry, begin=begin, step=step, place=place, rhs=rhs, chunk=chunk, high_rows=high_rows):
                b = begin + i * step
                add = placed_sum(chunk == place - b * block, rhs)
                inj[slot, pl.ds(pl.multiple_of(PAD + b * block, 8), high_rows), :] = add
                return carry

            lax.fori_loop(0, (end - begin) // step, body, 0)

    def ground():
        start = PAD + halo * stride
        if lanes == 128:
            return state[pl.ds(start, cols, stride=stride), :]
        rows = [state[start + c * stride : start + c * stride + 1, :] for c in range(cols)]
        return jnp.concatenate(rows, axis=0)

    def add_flux(s, h, x):
        which = obs[s, 0, 1 + probes : 2 + probes, 0:128]
        lane = lax.broadcasted_iota(jnp.int32, (1, 128), 1)
        number = jnp.sum(jnp.where(lane == h, which, 0.0), axis=1, keepdims=True)
        for w in range(d["weeks"]):
            flux[w] += jnp.where(number == w, x, 0.0)

    def surface(s, slot):
        level, column, rhs = observed(0, 0)
        tall = -(-cols // 8) * 8
        chunk = lax.broadcasted_iota(jnp.int32, (tall, count), 0)
        add = placed_sum(chunk == jnp.where(level == 0, column, -1), rhs)
        add_flux(0, 0, add[:cols])

    lane = lax.broadcasted_iota(jnp.int32, (deep, lanes), 1)
    first = lane < window
    grid_row = lax.rem(lane, window) + first_row
    keep = jnp.logical_and(grid_row >= 0, grid_row < lat_rows - 1)
    slots = hours if early else 1

    def prepare(t):
        slot = t if early else 0
        if not early:
            copy = pltpu.make_async_copy(land.at[t], stage, local.at[0])
            copy.start()
            copy.wait()
        lo = lowest(t)
        wm[slot, pl.ds(pl.multiple_of(PAD + lo * block, 8), PAD), :] = zero

        def body(b, carry):
            for c in range(2):
                base = pl.multiple_of(PAD + b * block + c * deep, 8)
                packed = (land[t, 2 * b + c] if early else stage[2 * b + c]).astype(jnp.float32)
                turned = pltpu.roll(packed, window, 1)
                east = jnp.where(first, packed, turned)
                north = jnp.where(keep, jnp.where(first, turned, packed), 0.0)
                south = pltpu.roll(north, 1, 1)
                ep[slot, pl.ds(base, deep), :] = jnp.maximum(east, 0.0)
                wm[slot, pl.ds(base + stride, deep), :] = jnp.minimum(east, 0.0)
                npos[slot, pl.ds(base, deep), :] = jnp.maximum(north, 0.0)
                sneg[slot, pl.ds(base, deep), :] = jnp.minimum(south, 0.0)
            return carry

        lax.fori_loop(lo, highest(t), body, 0)

    def advance(t, slot):
        s = t // hours_sec
        h = t - s * hours_sec
        lo, hi = lowest(t), highest(t)

        @pl.when(h == 0)
        def _():
            def body(b, carry):
                at = pl.ds(pl.multiple_of(PAD + b * block, 8), block)
                state[at, :] += inj[slot, at, :]
                return carry

            lax.fori_loop(lo, hi, body, 0)

        add_flux(s, h, ground())
        mix = lhs[0:deep, 0 : 3 * deep].astype(jnp.bfloat16)
        where = t if early else 0

        def mixing_of(b):
            base = pl.multiple_of(PAD + b * block, 8)
            x = jnp.concatenate(
                [state[pl.ds(base, deep), :], state[pl.ds(base + deep, deep), :]], axis=1
            )
            low = x - x.astype(jnp.bfloat16).astype(jnp.float32)
            stack = jnp.concatenate([x, x, low], axis=0).astype(jnp.bfloat16)
            return jnp.dot(mix, stack, preferred_element_type=jnp.float32)

        def keep_mixed(b, got):
            base = pl.multiple_of(PAD + b * block, 8)
            mixed[pl.ds(base, deep), :] = got[:, :lanes]
            mixed[pl.ds(base + deep, deep), :] = got[:, lanes:]

        def advect(b):
            base = pl.multiple_of(PAD + b * block, 8)
            at = pl.ds(base, block)
            here = mixed[at, :]
            after = mixed[pl.ds(base + stride, block), :]
            before = mixed[pl.ds(base - stride, block), :]
            g = here + ep[where, at, :] * (after - here) + wm[where, at, :] * (here - before)
            above = pltpu.roll(g, lanes - 1, 1)
            below = pltpu.roll(g, 1, 1)
            return g + npos[where, at, :] * (above - g) + sneg[where, at, :] * (g - below)

        def keep_state(b, x):
            state[pl.ds(pl.multiple_of(PAD + b * block, 8), block), :] = x

        def only_mix(b, carry):
            keep_mixed(b, mixing_of(b))
            return carry

        def both(b, carry):
            got = mixing_of(b)
            new = advect(b - 2)
            keep_state(b - 2, new)
            keep_mixed(b, got)
            return carry

        def only_advect(b, carry):
            keep_state(b, advect(b))
            return carry

        lax.fori_loop(lo, lo + 2, only_mix, 0)
        lax.fori_loop(lo + 2, hi, both, 0)
        lax.fori_loop(hi - 2, hi, only_advect, 0)

    def loop(high, low, run):
        def body(i, carry):
            run(high - i)
            return carry

        lax.fori_loop(0, high - low + 1, body, 0)

    loop(sections - 1, 0, hand_obs)
    if early:
        middle = hours // 2
        hand_winds(hours - 1)
        loop(sections - 1, 1, lambda s: inject(s, s))
        surface(0, 0)

        def whole(t):
            @pl.when(t < hours - 1)
            def _():
                hand_winds(t)

            take_winds(t)
            prepare(t)
            advance(t, t // hours_sec)

        loop(hours - 1, middle + 1, whole)
        loop(middle - 1, 1, hand_winds)

        def ready(t):
            take_winds(t)
            prepare(t)

        loop(middle - 1, 1, ready)
        hand_winds(middle)
        ready(middle)
        loop(middle, 1, lambda t: advance(t, t // hours_sec))
    else:
        surface(0, 0)

        def whole(t):
            s = t // hours_sec

            @pl.when(t == s * hours_sec)
            def _():
                inject(s, 0)

            hand_winds(t)
            take_winds(t)
            prepare(t)
            advance(t, 0)

        loop(hours - 1, 1, whole)

    add_flux(0, 0, ground())
    for w in range(d["weeks"]):
        square = flux[w] * flux[w]
        est[w] = (square + pltpu.roll(square, lanes - window, 1)) * 0.5

    every_job(lambda h, target: z_copy(h, target).wait_send())
    for k in range(1, sections):
        mine = obs.at[me, 0]
        remote(mine, mine, os.at[k], orr.at[me], me, sides[0], core).wait_send()

    def sent_obs(s):
        for n in beside:
            obs_copy(s, n).wait_send()

    loop(sections - 1, 1, sent_obs)

    def sent_winds(t):
        @pl.when(me != t // hours_sec)
        def _():
            half_copy(t).wait_send()

        def act(depth):
            for c in range(2):

                @pl.when(core == c)
                def _():
                    for side, sender, a, b in edges(depth):
                        if sender == c:
                            for q in range(2):
                                edge_copy(t, side, sender, a, b, q).wait_send()

        with_depth(t, act)

    loop(hours - 1, 1, sent_winds)


def on_device(winds, mixing, obs_cell, obs_weight, probe_sign, week_map, prior_precision):
    week_count, _, own = prior_precision.shape
    d = plan(
        lax.axis_size("tm"), lax.axis_size("lon"), winds.shape[2], winds.shape[4], winds.shape[3],
        winds.shape[5], own, probe_sign.shape[0], week_count, obs_cell.shape[2],
    )
    sections, hours, hours_sec = d["sections"], d["hours"], d["hours_sec"]
    lanes, rows, cols, left = d["lanes"], d["rows"], d["cols"], d["left"]
    early = d["early"]
    wire = (d["half"], 2 * d["stride"], 2 * d["window"])
    landing = (hours, d["pairs"]) + wire[1:]
    slots = hours if early else 1
    inj_slots = sections if early else 1
    sem = pltpu.SemaphoreType.DMA
    scratch = [
        pltpu.VMEM((hours_sec, sections) + wire, jnp.bfloat16),
        pltpu.VMEM((2 * d["half"] * d["stride"], 2 * d["window"]), jnp.float32),
        pltpu.VMEM((sections, 3, 2 + d["probes"], d["count"]), jnp.float32),
        pltpu.VMEM((128, 256), jnp.float32),
        pltpu.VMEM((rows, lanes), jnp.float32),
        pltpu.VMEM((rows, lanes), jnp.float32),
        pltpu.VMEM((inj_slots, rows, lanes), jnp.float32),
    ] + [pltpu.VMEM((slots, rows, lanes), jnp.float32)] * 4 + [
        pltpu.VMEM((week_count, cols, lanes), jnp.float32),
        sem((hours_sec, sections)), sem((hours,)), sem((hours,)), sem((hours,)),
        sem((hours, 2, 2)), sem((hours, 2, 2)), sem((sections,)), sem((sections,)),
        sem((sections, 2)), sem((sections, 2)), sem((1,)),
    ]
    outs = [jax.ShapeDtypeStruct((week_count, cols, lanes), jnp.float32)]
    out_specs = [pl.BlockSpec(memory_space=pltpu.VMEM)]
    if early:
        scratch = [pltpu.VMEM(landing, jnp.bfloat16)] + scratch
    else:
        outs.append(jax.ShapeDtypeStruct(landing, jnp.bfloat16))
        out_specs.append(pl.BlockSpec(memory_space=pl.ANY))
        scratch = [pltpu.VMEM(landing[1:], jnp.bfloat16)] + scratch
    got = pl.pallas_call(
        functools.partial(fused_kernel, d),
        out_shape=tuple(outs),
        in_specs=[pl.BlockSpec(memory_space=pltpu.VMEM)] * 6,
        out_specs=tuple(out_specs),
        scratch_shapes=scratch,
        compiler_params=pltpu.CompilerParams(
            collective_id=0, has_side_effects=True, vmem_limit_bytes=56 << 20
        ),
    )(
        winds.transpose(0, 1, 2, 4, 3, 5), mixing, obs_cell[0], obs_weight[0],
        probe_sign[:, 0, 0], week_map,
    )
    return (prior_precision + got[0][..., left : left + own])[None]


def solution(mesh):
    placed = (
        P(None, ("groups", "tm"), None, None, "lon", None),
        P(),
        P(("groups", "tm"), "lon", None),
        P(("groups", "tm"), "lon", None),
        P("probe", ("groups", "tm"), "lon", None),
        P(("groups", "tm"), None),
        P("groups", "lon", "tm"),
    )
    return jax.shard_map(
        on_device,
        mesh=mesh,
        in_specs=placed,
        out_specs=P("probe", "groups", "lon", "tm"),
        check_vma=False,
    )
```

```python
import functools

import jax
import jax.numpy as jnp
from jax import lax
from jax.experimental import pallas as pl
from jax.experimental.pallas import tpu as pltpu
from jax.sharding import PartitionSpec as P

WIDE = 4
PAD = 40


def split2(x):
    high = x.astype(jnp.bfloat16)
    low = (x - high.astype(jnp.float32)).astype(jnp.bfloat16)
    return high, low


def plan(sections, bands, hours_sec, cols, levels, lat_rows, own, probes, weeks, count):
    hours = sections * hours_sec
    halo = -(-hours // WIDE) * WIDE
    window = -(-(own + 2 * hours) // 64) * 64
    d = dict(
        sections=sections, bands=bands, hours_sec=hours_sec, cols=cols, levels=levels,
        lat_rows=lat_rows, own=own, probes=probes, weeks=weeks, count=count, hours=hours,
        halo=halo, left=hours, window=window, lanes=window * probes,
        half=cols // 4, halo_pairs=halo // 2, pairs=(cols + 2 * halo) // 2,
        blocks=(cols + 2 * halo) // WIDE,
    )
    d["stride"] = levels if d["lanes"] == 128 else -(-levels // 8) * 8
    d["block"] = WIDE * d["stride"]
    d["rows"] = PAD + (d["blocks"] + 1) * d["block"]
    d["early"] = hours <= 8 and hours_sec == 2 and sections % 2 == 0
    return d


def fused_kernel(d, winds, mixing, cell, weight, sign, week, *refs):
    sections, bands, hours_sec, hours = d["sections"], d["bands"], d["hours_sec"], d["hours"]
    cols, levels, lat_rows, own = d["cols"], d["levels"], d["lat_rows"], d["own"]
    probes, count, halo, left = d["probes"], d["count"], d["halo"], d["left"]
    window, lanes, half, halo_pairs = d["window"], d["lanes"], d["half"], d["halo_pairs"]
    block, early, stride = d["block"], d["early"], d["stride"]
    if early:
        est, land, refs = refs[0], refs[1], refs[2:]
        stage = None
    else:
        est, land, stage, refs = refs[0], refs[1], refs[2], refs[3:]
    (pack, flat, obs, lhs, pick, state, mixed, inj, ep, wm, npos, sneg, flux,
     zs, zr, hs, hr, xs, xr, os, orr, us, ur, local) = refs
    own_pairs = 2 * half
    me = lax.axis_index("tm")
    band = lax.axis_index("lon")
    core = lax.axis_index("probe")
    sides = [lax.rem(band + bands - 1, bands), lax.rem(band + 1, bands)]
    if bands == 2:
        greet = sides[:1]
    else:
        greet = sides

    def remote(src, dst, send, recv, tm, lon, probe):
        return pltpu.make_async_remote_copy(
            src_ref=src, dst_ref=dst, send_sem=send, recv_sem=recv,
            device_id={"tm": tm, "lon": lon, "probe": probe},
            device_id_type=pl.DeviceIdType.MESH,
        )

    if early:
        for t in range(1, hours):
            reach = (t + 1) // 2
            for n in range((halo - t) // WIDE * WIDE // 2, halo_pairs - reach):
                land[t, n] = jnp.zeros(land.shape[2:], land.dtype)
                land[t, 2 * halo_pairs + own_pairs - 1 - n] = jnp.zeros(land.shape[2:], land.dtype)

    barrier = pltpu.get_barrier_semaphore()

    def hello(tm, lon, probe):
        pl.semaphore_signal(
            barrier, inc=1, device_id={"tm": tm, "lon": lon, "probe": probe},
            device_id_type=pl.DeviceIdType.MESH,
        )

    for k in range(1, sections):
        hello(lax.rem(me + k, sections), band, core)
    for lon in greet:
        for q in range(2):
            hello(me, lon, q)
    hello(me, band, 1 - core)

    obs[me, 0, 0:1, :] = cell[...].astype(jnp.float32)
    for p in range(probes):
        obs[me, 0, 1 + p : 2 + p, :] = (2 * sign[p] - 1).astype(jnp.float32) * weight[...]
    lane_row = lax.broadcasted_iota(jnp.int32, (1, count), 1)
    weeks_row = jnp.zeros((1, count), jnp.float32)
    for h in range(hours_sec):
        weeks_row = jnp.where(lane_row == h, week[0:1, h : h + 1].astype(jnp.float32), weeks_row)
    obs[me, 0, 1 + probes : 2 + probes, :] = weeks_row

    if stride != levels:
        flat[...] = jnp.zeros_like(flat)
    wl = 2 * window
    lat_tiles = -(-lat_rows // 128)

    def packed_column(h, column, start):
        tiles = []
        for comp in range(2):
            row = []
            for k in range(lat_tiles):
                x = winds[comp, 0, h, column, :, k * 128 : min(k * 128 + 128, lat_rows)]
                x = x.astype(jnp.float32)
                if x.shape[1] < 128:
                    x = jnp.concatenate(
                        [x, jnp.zeros((levels, 128 - x.shape[1]), jnp.float32)], axis=1
                    )
                row.append(x)
            tiles.append(row)
        lane = lax.broadcasted_iota(jnp.int32, (levels, 128), 1)
        parts = []
        for v in range(wl // 128):
            out = jnp.zeros((levels, 128), jnp.float32)
            for comp in range(2):
                begin = comp * window - v * 128
                if begin >= 128 or begin + window <= 0:
                    continue
                shift = lax.rem(begin - start + 512, 128)
                at = lane - begin
                row = at + start
                for k in range(lat_tiles):
                    inside = (
                        (at >= 0) & (at < window) & (row >= k * 128)
                        & (row < min(k * 128 + 128, lat_rows))
                    )
                    out = jnp.where(inside, pltpu.roll(tiles[comp][k], shift, 1), out)
            parts.append(out)
        return parts[0] if len(parts) == 1 else jnp.concatenate(parts, axis=1)

    def fill(h, target, first_column, put):
        start = target * own - left

        def body(i, carry):
            for c in range(2):
                at = pl.multiple_of(i * 2 * stride, 8) + c * stride
                flat[pl.ds(at, levels), :] = packed_column(h, first_column + 2 * i + c, start)
            return carry

        lax.fori_loop(0, half, body, 0, unroll=3)

        def cast(i, carry):
            x = flat[pl.ds(pl.multiple_of(i * 2 * stride, 8), 2 * stride), :]
            put(i, x.astype(jnp.bfloat16))
            return carry

        lax.fori_loop(0, half, cast, 0, unroll=3)

    least = jnp.where(me == 0, 1, 0)
    my_pairs = halo_pairs + half * core

    def z_copy(h, target):
        t = me * hours_sec + h
        return remote(
            pack.at[h, target], land.at[t, pl.ds(my_pairs, half)], zs.at[h, target], zr.at[t],
            target, band, core,
        )

    def job(h, target):
        def put(i, x):
            pack[h, target, i] = x

        fill(h, target, 2 * half * core, put)
        z_copy(h, target).start()

    def every_job(run):
        def upper(i, carry):
            h = hours_sec - 1 - i

            def target(k, inner):
                run(h, sections - 1 - k)
                return inner

            return lax.fori_loop(0, sections - 1 - me, target, carry)

        lax.fori_loop(0, hours_sec - least, upper, 0)

        def lower(i, carry):
            h = hours_sec - 1 - i

            def target(k, inner):
                run(h, k)
                return inner

            return lax.fori_loop(0, me, target, carry)

        lax.fori_loop(0, hours_sec - least, lower, 0)

    last = hours_sec - 1
    if early:
        half_way = sections // 2
        top = me == sections - 1
        beyond = jnp.where(top, 0, me + 1)

        def put_first(i, x):
            pack[last, beyond, i] = x

        fill(last, beyond, 2 * half * core, put_first)

    pl.semaphore_wait(barrier, sections - 1 + 2 * len(greet) + 1)

    for k in range(1, sections):
        tm = lax.rem(me + k, sections)
        mine = obs.at[me, 0]
        remote(mine, mine, os.at[k], orr.at[me], tm, band, core).start()

    def batch(h, low, high):
        def body(i, carry):
            job(h, low + i)
            return carry

        lax.fori_loop(0, high - low, body, 0)

    if early:
        z_copy(last, beyond).start()
        batch(last, beyond + 1, jnp.where(top, me, sections))
        batch(0, me + 1, jnp.where(me >= half_way, sections, me + 1))
    else:
        every_job(job)

    def second():
        batch(last, 0, jnp.where((me >= half_way) & (me < sections - 1), me, 0))
        batch(0, me + 1, jnp.where((me < half_way) & (me > 0), sections, me + 1))

    def third():
        batch(last, 0, jnp.where(me < half_way, me, 0))
        batch(0, 0, jnp.where(top, me, 0))

    def fourth():
        batch(0, 0, jnp.where(top, 0, me))

    def at_home(i, carry):
        h = hours_sec - 1 - i
        t = me * hours_sec + h
        for c in range(2):
            if early:

                def put(i, x):
                    land[t, halo_pairs + half * c + i] = x

                fill(h, me, 2 * half * c, put)
            else:

                def put(i, x):
                    pack[h, me, i] = x

                fill(h, me, 2 * half * c, put)
                copy = pltpu.make_async_copy(
                    pack.at[h, me], land.at[t, pl.ds(halo_pairs + half * c, half)], local.at[0]
                )
                copy.start()
                copy.wait()
        return carry

    lax.fori_loop(0, hours_sec - least, at_home, 0)

    zero = jnp.zeros((PAD, lanes), jnp.float32)

    def clear(i, carry):
        at = pl.multiple_of(i * 8, 8)
        state[pl.ds(at, 8), :] = zero[:8]
        mixed[pl.ds(at, 8), :] = zero[:8]
        return carry

    lax.fori_loop(0, d["rows"] // 8, clear, 0, unroll=8)
    flux[...] = jnp.zeros_like(flux)
    lhs[...] = jnp.zeros_like(lhs)
    lhs[0:levels, 0:levels] = mixing[...]
    turned_mix = jnp.transpose(lhs[:, 0:128])
    both = turned_mix + pltpu.roll(pltpu.roll(turned_mix, stride, 0), stride, 1)
    high = both.astype(jnp.bfloat16).astype(jnp.float32)
    low = both - high
    none = jnp.zeros_like(both)
    high = jnp.concatenate([high, none], axis=1)
    low = jnp.concatenate([low, none], axis=1)
    deep = 2 * stride
    matrix = high + pltpu.roll(low, deep, 1) + pltpu.roll(high, 2 * deep, 1)
    lhs[...] = matrix

    source = lax.broadcasted_iota(jnp.int32, (wl, lanes), 0)
    into = lax.rem(lax.broadcasted_iota(jnp.int32, (wl, lanes), 1), window)
    first_row = me * own - left
    keep = (into + first_row >= 0) & (into + first_row < lat_rows - 1)
    below = (into > 0) & (into + first_row >= 1) & (into + first_row < lat_rows)
    pick[:, :lanes] = jnp.where(source == into, 1.0, 0.0)
    pick[:, lanes : 2 * lanes] = jnp.where((source == into + window) & keep, 1.0, 0.0)
    pick[:, 2 * lanes :] = jnp.where((source == into + window - 1) & below, 1.0, 0.0)

    def obs_copy(s, n):
        return remote(
            obs.at[s, 0], obs.at[s, 1 + n], us.at[s, n], ur.at[s, n], me, sides[1 - n], core
        )

    beside = range(1 if bands == 2 else 2)

    def hand_obs(s):
        @pl.when(me != s)
        def _():
            remote(obs.at[s, 0], obs.at[s, 0], os.at[0], orr.at[s], me, sides[0], core).wait_recv()

        @pl.when(s > 0)
        def _():
            for n in beside:
                obs_copy(s, n).start()

    def half_copy(t):
        place = land.at[t, pl.ds(my_pairs, half)]
        return remote(place, place, hs.at[t], hr.at[t], me, band, 1 - core)

    def edges(depth):
        found = []
        for side in range(2):
            begin = 0 if side == 0 else own_pairs - depth
            for c in range(2):
                a, b = max(begin, half * c), min(begin + depth, half * (c + 1))
                if a < b:
                    found.append((side, c, a, b))
        return found

    def edge_copy(t, side, c, a, b, q):
        to = halo_pairs + (own_pairs if side == 0 else -own_pairs)
        return remote(
            land.at[t, pl.ds(halo_pairs + a, b - a)], land.at[t, pl.ds(to + a, b - a)],
            xs.at[t, side, q], xr.at[t, side, c], me, sides[side], q,
        )

    def with_depth(t, act):
        if early:
            for depth in range(1, halo_pairs + 1):

                @pl.when((t + 1) // 2 == depth)
                def _():
                    act(depth)

        else:

            @pl.when(t > halo // 2)
            def _():
                act(halo_pairs)

            @pl.when(t <= halo // 2)
            def _():
                act(halo_pairs // 2)

    def hand_winds(t):
        s = t // hours_sec

        @pl.when(me != s)
        def _():
            place = land.at[t, pl.ds(my_pairs, half)]
            remote(place, place, zs.at[0, 0], zr.at[t], me, sides[0], core).wait_recv()

        def act(depth):
            for c in range(2):

                @pl.when(core == c)
                def _():
                    for side, sender, a, b in edges(depth):
                        if sender == c:
                            for q in range(2):
                                edge_copy(t, side, sender, a, b, q).start()

        with_depth(t, act)

        @pl.when(me != s)
        def _():
            half_copy(t).start()

    def take_winds(t):
        s = t // hours_sec

        @pl.when(me != s)
        def _():
            place = land.at[t, pl.ds(halo_pairs + half * (1 - core), half)]
            remote(place, place, hs.at[t], hr.at[t], me, band, 1 - core).wait_recv()

        def act(depth):
            for side, sender, a, b in edges(depth):
                edge_copy(t, side, sender, a, b, 0).wait_recv()

        with_depth(t, act)

    first_row = me * own - left

    def observed(s, piece):
        place = obs[s, piece, 0:1, :].astype(jnp.int32)
        level = place // (cols * lat_rows)
        rest = place - level * (cols * lat_rows)
        column = rest // lat_rows
        row = rest - column * lat_rows - first_row
        hit = lax.broadcasted_iota(jnp.int32, (window, count), 0) == row
        parts = [
            split2(jnp.where(hit, obs[s, piece, 1 + p : 2 + p, :], 0.0)) for p in range(probes)
        ]
        rhs = jnp.concatenate([x[0] for x in parts] + [x[1] for x in parts], axis=0)
        return level, column, rhs

    def placed_sum(hot, rhs):
        got = lax.dot_general(
            hot.astype(jnp.float32).astype(jnp.bfloat16), rhs, (((1,), (1,)), ((), ())),
            preferred_element_type=jnp.float32,
        )
        return got[:, :lanes] + got[:, lanes:]

    def lowest(t):
        return (halo - t) // WIDE

    def highest(t):
        return (halo + cols + t + WIDE - 1) // WIDE

    edge_blocks = halo // WIDE
    own_blocks = cols // WIDE
    together = max(n for n in range(1, 4) if own_blocks % n == 0)

    def inject(s, slot):
        t = s * hours_sec
        for n in beside:
            remote(
                obs.at[s, 0], obs.at[s, 1 + n], us.at[s, n], ur.at[s, n], me, sides[0], core
            ).wait_recv()
        for piece, shift, begin, end, step in (
            (0, halo, edge_blocks, edge_blocks + own_blocks, together),
            (1, halo - cols, lowest(t), edge_blocks, 1),
            (2 if bands > 2 else 1, halo + cols, edge_blocks + own_blocks, highest(t), 1),
        ):
            level, column, rhs = observed(s, piece)
            place = (column + shift) * stride + level
            high_rows = step * block
            chunk = lax.broadcasted_iota(jnp.int32, (high_rows, count), 0)

            def body(i, carry, begin=begin, step=step, place=place, rhs=rhs, chunk=chunk, high_rows=high_rows):
                b = begin + i * step
                add = placed_sum(chunk == place - b * block, rhs)
                inj[slot, pl.ds(pl.multiple_of(PAD + b * block, 8), high_rows), :] = add
                return carry

            lax.fori_loop(0, (end - begin) // step, body, 0)

    def ground():
        start = PAD + halo * stride
        if lanes == 128:
            return state[pl.ds(start, cols, stride=stride), :]
        rows = [state[start + c * stride : start + c * stride + 1, :] for c in range(cols)]
        return jnp.concatenate(rows, axis=0)

    def add_flux(s, h, x):
        which = obs[s, 0, 1 + probes : 2 + probes, 0:128]
        lane = lax.broadcasted_iota(jnp.int32, (1, 128), 1)
        number = jnp.sum(jnp.where(lane == h, which, 0.0), axis=1, keepdims=True)
        for w in range(d["weeks"]):
            flux[w] += jnp.where(number == w, x, 0.0)

    def surface(s, slot):
        level, column, rhs = observed(0, 0)
        tall = -(-cols // 8) * 8
        chunk = lax.broadcasted_iota(jnp.int32, (tall, count), 0)
        add = placed_sum(chunk == jnp.where(level == 0, column, -1), rhs)
        add_flux(0, 0, add[:cols])

    middle = hours // 2

    def slot_of(t):
        return jnp.where(t > middle, 0, t) if early else 0

    def prepare(t):
        slot = slot_of(t)
        if not early:
            copy = pltpu.make_async_copy(land.at[t], stage, local.at[0])
            copy.start()
            copy.wait()
        lo, hi = lowest(t), highest(t)
        wm[slot, pl.ds(pl.multiple_of(PAD + lo * block, 8), PAD), :] = jnp.zeros((PAD, lanes), jnp.float32)
        matrix = pick[...].astype(jnp.bfloat16)

        def spread(b, n):
            base = pl.multiple_of(PAD + b * block, 8)
            at = pl.ds(b * WIDE // 2, n * WIDE // 2)
            packed = land[t, at] if early else stage[at]
            packed = packed.reshape(n * block, wl)
            got = jnp.dot(packed, matrix, preferred_element_type=jnp.float32)
            east, north, south = got[:, :lanes], got[:, lanes : 2 * lanes], got[:, 2 * lanes :]
            ep[slot, pl.ds(base, n * block), :] = jnp.maximum(east, 0.0)
            wm[slot, pl.ds(base + stride, n * block), :] = jnp.minimum(east, 0.0)
            npos[slot, pl.ds(base, n * block), :] = jnp.maximum(north, 0.0)
            sneg[slot, pl.ds(base, n * block), :] = jnp.minimum(south, 0.0)

        def one(b, carry):
            spread(b, 1)
            return carry

        def many(i, carry):
            spread(edge_blocks + i * together, together)
            return carry

        lax.fori_loop(lo, edge_blocks, one, 0)
        lax.fori_loop(0, own_blocks // together, many, 0)
        lax.fori_loop(edge_blocks + own_blocks, hi, one, 0)

    def advance(t, slot):
        s = t // hours_sec
        h = t - s * hours_sec
        lo, hi = lowest(t), highest(t)

        @pl.when(h == 0)
        def _():
            def body(b, carry):
                at = pl.ds(pl.multiple_of(PAD + b * block, 8), block)
                state[at, :] += inj[slot, at, :]
                return carry

            lax.fori_loop(lo, hi, body, 0)

        add_flux(s, h, ground())
        mix = lhs[0:deep, 0 : 3 * deep].astype(jnp.bfloat16)
        where = slot_of(t)

        def mixing_of(b):
            base = pl.multiple_of(PAD + b * block, 8)
            x = jnp.concatenate(
                [state[pl.ds(base, deep), :], state[pl.ds(base + deep, deep), :]], axis=1
            )
            low = x - x.astype(jnp.bfloat16).astype(jnp.float32)
            stack = jnp.concatenate([x, x, low], axis=0).astype(jnp.bfloat16)
            return jnp.dot(mix, stack, preferred_element_type=jnp.float32)

        def keep_mixed(b, got):
            base = pl.multiple_of(PAD + b * block, 8)
            mixed[pl.ds(base, deep), :] = got[:, :lanes]
            mixed[pl.ds(base + deep, deep), :] = got[:, lanes:]

        def advect(b):
            base = pl.multiple_of(PAD + b * block, 8)
            at = pl.ds(base, block)
            here = mixed[at, :]
            after = mixed[pl.ds(base + stride, block), :]
            before = mixed[pl.ds(base - stride, block), :]
            g = here + ep[where, at, :] * (after - here) + wm[where, at, :] * (here - before)
            above = pltpu.roll(g, lanes - 1, 1)
            below = pltpu.roll(g, 1, 1)
            return g + npos[where, at, :] * (above - g) + sneg[where, at, :] * (g - below)

        def keep_state(b, x):
            state[pl.ds(pl.multiple_of(PAD + b * block, 8), block), :] = x

        def only_mix(b, carry):
            keep_mixed(b, mixing_of(b))
            return carry

        def both(b, carry):
            got = mixing_of(b)
            new = advect(b - 2)
            keep_state(b - 2, new)
            keep_mixed(b, got)
            return carry

        def only_advect(b, carry):
            keep_state(b, advect(b))
            return carry

        lax.fori_loop(lo, lo + 2, only_mix, 0)
        lax.fori_loop(lo + 2, hi, both, 0)
        lax.fori_loop(hi - 2, hi, only_advect, 0)

    def loop(high, low, run):
        def body(i, carry):
            run(high - i)
            return carry

        lax.fori_loop(0, high - low + 1, body, 0)

    if early:

        def ready(t):
            take_winds(t)
            prepare(t)

        def step(t):
            advance(t, t // hours_sec)

        hand_obs(sections - 1)
        pieces = [second, third, fourth]
        for s in range(sections - 1, 0, -1):
            hand_obs(s - 1)
            inject(s, s)
            if pieces:
                pieces.pop(0)()
        while pieces:
            pieces.pop(0)()
        surface(0, 0)
        hand_winds(hours - 1)

        def whole(t):
            ready(t)
            hand_winds(t - 1)
            step(t)

        loop(hours - 1, middle + 2, whole)
        ready(middle + 1)
        loop(middle - 1, 1, hand_winds)
        loop(middle - 1, 1, ready)
        hand_winds(middle)
        step(middle + 1)
        ready(middle)
        loop(middle, 1, step)
    else:
        loop(sections - 1, 0, hand_obs)
        surface(0, 0)

        def whole(t):
            s = t // hours_sec

            @pl.when(t == s * hours_sec)
            def _():
                inject(s, 0)

            hand_winds(t)
            take_winds(t)
            prepare(t)
            advance(t, 0)

        loop(hours - 1, 1, whole)

    add_flux(0, 0, ground())
    for w in range(d["weeks"]):
        square = flux[w] * flux[w]
        est[w] = (square + pltpu.roll(square, lanes - window, 1)) * 0.5

    every_job(lambda h, target: z_copy(h, target).wait_send())
    for k in range(1, sections):
        mine = obs.at[me, 0]
        remote(mine, mine, os.at[k], orr.at[me], me, sides[0], core).wait_send()

    def sent_obs(s):
        for n in beside:
            obs_copy(s, n).wait_send()

    loop(sections - 1, 1, sent_obs)

    def sent_winds(t):
        @pl.when(me != t // hours_sec)
        def _():
            half_copy(t).wait_send()

        def act(depth):
            for c in range(2):

                @pl.when(core == c)
                def _():
                    for side, sender, a, b in edges(depth):
                        if sender == c:
                            for q in range(2):
                                edge_copy(t, side, sender, a, b, q).wait_send()

        with_depth(t, act)

    loop(hours - 1, 1, sent_winds)


def on_device(winds, mixing, obs_cell, obs_weight, probe_sign, week_map, prior_precision):
    week_count, _, own = prior_precision.shape
    d = plan(
        lax.axis_size("tm"), lax.axis_size("lon"), winds.shape[2], winds.shape[4], winds.shape[3],
        winds.shape[5], own, probe_sign.shape[0], week_count, obs_cell.shape[2],
    )
    sections, hours, hours_sec = d["sections"], d["hours"], d["hours_sec"]
    lanes, rows, cols, left = d["lanes"], d["rows"], d["cols"], d["left"]
    early = d["early"]
    wire = (d["half"], 2 * d["stride"], 2 * d["window"])
    landing = (hours, d["pairs"]) + wire[1:]
    slots = hours // 2 + 1 if early else 1
    inj_slots = sections if early else 1
    sem = pltpu.SemaphoreType.DMA
    scratch = [
        pltpu.VMEM((hours_sec, sections) + wire, jnp.bfloat16),
        pltpu.VMEM((2 * d["half"] * d["stride"], 2 * d["window"]), jnp.float32),
        pltpu.VMEM((sections, 3, 2 + d["probes"], d["count"]), jnp.float32),
        pltpu.VMEM((128, 256), jnp.float32),
        pltpu.VMEM((2 * d["window"], 3 * lanes), jnp.float32),
        pltpu.VMEM((rows, lanes), jnp.float32),
        pltpu.VMEM((rows, lanes), jnp.float32),
        pltpu.VMEM((inj_slots, rows, lanes), jnp.float32),
    ] + [pltpu.VMEM((slots, rows, lanes), jnp.float32)] * 4 + [
        pltpu.VMEM((week_count, cols, lanes), jnp.float32),
        sem((hours_sec, sections)), sem((hours,)), sem((hours,)), sem((hours,)),
        sem((hours, 2, 2)), sem((hours, 2, 2)), sem((sections,)), sem((sections,)),
        sem((sections, 2)), sem((sections, 2)), sem((1,)),
    ]
    outs = [jax.ShapeDtypeStruct((week_count, cols, lanes), jnp.float32)]
    out_specs = [pl.BlockSpec(memory_space=pltpu.VMEM)]
    if early:
        scratch = [pltpu.VMEM(landing, jnp.bfloat16)] + scratch
    else:
        outs.append(jax.ShapeDtypeStruct(landing, jnp.bfloat16))
        out_specs.append(pl.BlockSpec(memory_space=pl.ANY))
        scratch = [pltpu.VMEM(landing[1:], jnp.bfloat16)] + scratch
    got = pl.pallas_call(
        functools.partial(fused_kernel, d),
        out_shape=tuple(outs),
        in_specs=[pl.BlockSpec(memory_space=pltpu.VMEM)] * 6,
        out_specs=tuple(out_specs),
        scratch_shapes=scratch,
        compiler_params=pltpu.CompilerParams(
            collective_id=0, has_side_effects=True, vmem_limit_bytes=(38 if early else 56) << 20
        ),
    )(
        winds.transpose(0, 1, 2, 4, 3, 5), mixing, obs_cell[0], obs_weight[0],
        probe_sign[:, 0], week_map,
    )
    return (prior_precision + got[0][..., left : left + own])[None]


def solution(mesh):
    placed = (
        P(None, ("groups", "tm"), None, None, "lon", None),
        P(),
        P(("groups", "tm"), "lon", None),
        P(("groups", "tm"), "lon", None),
        P("probe", ("groups", "tm"), "lon", None),
        P(("groups", "tm"), None),
        P("groups", "lon", "tm"),
    )
    return jax.shard_map(
        on_device,
        mesh=mesh,
        in_specs=placed,
        out_specs=P("probe", "groups", "lon", "tm"),
        check_vma=False,
    )
```

```python
import functools

import jax
import jax.numpy as jnp
from jax import lax
from jax.experimental import pallas as pl
from jax.experimental.pallas import tpu as pltpu
from jax.sharding import PartitionSpec as P

WIDE = 4
PAD = 40


def split2(x):
    high = x.astype(jnp.bfloat16)
    low = (x - high.astype(jnp.float32)).astype(jnp.bfloat16)
    return high, low


def plan(sections, bands, hours_sec, cols, levels, lat_rows, own, probes, weeks, count):
    hours = sections * hours_sec
    halo = -(-hours // WIDE) * WIDE
    window = -(-(own + 2 * hours) // 64) * 64
    d = dict(
        sections=sections, bands=bands, hours_sec=hours_sec, cols=cols, levels=levels,
        lat_rows=lat_rows, own=own, probes=probes, weeks=weeks, count=count, hours=hours,
        halo=halo, left=hours, window=window, lanes=window * probes,
        half=cols // 4, halo_pairs=halo // 2, pairs=(cols + 2 * halo) // 2,
        blocks=(cols + 2 * halo) // WIDE,
    )
    d["stride"] = levels if d["lanes"] == 128 else -(-levels // 8) * 8
    d["block"] = WIDE * d["stride"]
    d["rows"] = PAD + (d["blocks"] + 1) * d["block"]
    d["early"] = hours <= 8 and hours_sec == 2 and sections % 2 == 0
    return d


def fused_kernel(d, winds, mixing, cell, weight, sign, week, *refs):
    sections, bands, hours_sec, hours = d["sections"], d["bands"], d["hours_sec"], d["hours"]
    cols, levels, lat_rows, own = d["cols"], d["levels"], d["lat_rows"], d["own"]
    probes, count, halo, left = d["probes"], d["count"], d["halo"], d["left"]
    window, lanes, half, halo_pairs = d["window"], d["lanes"], d["half"], d["halo_pairs"]
    block, early, stride = d["block"], d["early"], d["stride"]
    if early:
        est, land, refs = refs[0], refs[1], refs[2:]
        stage = None
    else:
        est, land, stage, refs = refs[0], refs[1], refs[2], refs[3:]
    (pack, flat, obs, lhs, pick, state, mixed, inj, ep, wm, npos, sneg, flux,
     zs, zr, hs, hr, xs, xr, os, orr, us, ur, local) = refs
    own_pairs = 2 * half
    me = lax.axis_index("tm")
    band = lax.axis_index("lon")
    core = lax.axis_index("probe")
    sides = [lax.rem(band + bands - 1, bands), lax.rem(band + 1, bands)]
    if bands == 2:
        greet = sides[:1]
    else:
        greet = sides

    def remote(src, dst, send, recv, tm, lon, probe):
        return pltpu.make_async_remote_copy(
            src_ref=src, dst_ref=dst, send_sem=send, recv_sem=recv,
            device_id={"tm": tm, "lon": lon, "probe": probe},
            device_id_type=pl.DeviceIdType.MESH,
        )

    if early:
        for t in range(1, hours):
            reach = (t + 1) // 2
            for n in range((halo - t) // WIDE * WIDE // 2, halo_pairs - reach):
                land[t, n] = jnp.zeros(land.shape[2:], land.dtype)
                land[t, 2 * halo_pairs + own_pairs - 1 - n] = jnp.zeros(land.shape[2:], land.dtype)

    barrier = pltpu.get_barrier_semaphore()

    def hello(tm, lon, probe):
        pl.semaphore_signal(
            barrier, inc=1, device_id={"tm": tm, "lon": lon, "probe": probe},
            device_id_type=pl.DeviceIdType.MESH,
        )

    for k in range(1, sections):
        hello(lax.rem(me + k, sections), band, core)
    for lon in greet:
        for q in range(2):
            hello(me, lon, q)
    hello(me, band, 1 - core)

    obs[me, 0, 0:1, :] = cell[...].astype(jnp.float32)
    for p in range(probes):
        obs[me, 0, 1 + p : 2 + p, :] = (2 * sign[p] - 1).astype(jnp.float32) * weight[...]
    lane_row = lax.broadcasted_iota(jnp.int32, (1, count), 1)
    weeks_row = jnp.zeros((1, count), jnp.float32)
    for h in range(hours_sec):
        weeks_row = jnp.where(lane_row == h, week[0:1, h : h + 1].astype(jnp.float32), weeks_row)
    obs[me, 0, 1 + probes : 2 + probes, :] = weeks_row

    if stride != levels:
        flat[...] = jnp.zeros_like(flat)
    wl = 2 * window
    lat_tiles = -(-lat_rows // 128)

    def packed_column(h, column, start):
        tiles = []
        for comp in range(2):
            row = []
            for k in range(lat_tiles):
                x = winds[comp, 0, h, column, :, k * 128 : min(k * 128 + 128, lat_rows)]
                x = x.astype(jnp.float32)
                if x.shape[1] < 128:
                    x = jnp.concatenate(
                        [x, jnp.zeros((levels, 128 - x.shape[1]), jnp.float32)], axis=1
                    )
                row.append(x)
            tiles.append(row)
        lane = lax.broadcasted_iota(jnp.int32, (levels, 128), 1)
        parts = []
        for v in range(wl // 128):
            out = jnp.zeros((levels, 128), jnp.float32)
            for comp in range(2):
                begin = comp * window - v * 128
                if begin >= 128 or begin + window <= 0:
                    continue
                shift = lax.rem(begin - start + 512, 128)
                at = lane - begin
                row = at + start
                for k in range(lat_tiles):
                    inside = (
                        (at >= 0) & (at < window) & (row >= k * 128)
                        & (row < min(k * 128 + 128, lat_rows))
                    )
                    out = jnp.where(inside, pltpu.roll(tiles[comp][k], shift, 1), out)
            parts.append(out)
        return parts[0] if len(parts) == 1 else jnp.concatenate(parts, axis=1)

    def fill(h, target, first_column, put):
        start = target * own - left

        def body(i, carry):
            for c in range(2):
                at = pl.multiple_of(i * 2 * stride, 8) + c * stride
                flat[pl.ds(at, levels), :] = packed_column(h, first_column + 2 * i + c, start)
            return carry

        lax.fori_loop(0, half, body, 0, unroll=3)

        def cast(i, carry):
            x = flat[pl.ds(pl.multiple_of(i * 2 * stride, 8), 2 * stride), :]
            put(i, x.astype(jnp.bfloat16))
            return carry

        lax.fori_loop(0, half, cast, 0, unroll=3)

    least = jnp.where(me == 0, 1, 0)
    my_pairs = halo_pairs + half * core

    def z_copy(h, target):
        t = me * hours_sec + h
        return remote(
            pack.at[h, target], land.at[t, pl.ds(my_pairs, half)], zs.at[h, target], zr.at[t],
            target, band, core,
        )

    def job(h, target):
        def put(i, x):
            pack[h, target, i] = x

        fill(h, target, 2 * half * core, put)
        z_copy(h, target).start()

    def every_job(run):
        def upper(i, carry):
            h = hours_sec - 1 - i

            def target(k, inner):
                run(h, sections - 1 - k)
                return inner

            return lax.fori_loop(0, sections - 1 - me, target, carry)

        lax.fori_loop(0, hours_sec - least, upper, 0)

        def lower(i, carry):
            h = hours_sec - 1 - i

            def target(k, inner):
                run(h, k)
                return inner

            return lax.fori_loop(0, me, target, carry)

        lax.fori_loop(0, hours_sec - least, lower, 0)

    last = hours_sec - 1
    if early:
        half_way = sections // 2
        top = me == sections - 1
        beyond = jnp.where(top, 0, me + 1)

        def put_first(i, x):
            pack[last, beyond, i] = x

        fill(last, beyond, 2 * half * core, put_first)

    pl.semaphore_wait(barrier, sections - 1 + 2 * len(greet) + 1)

    for k in range(1, sections):
        tm = lax.rem(me + k, sections)
        mine = obs.at[me, 0]
        remote(mine, mine, os.at[k], orr.at[me], tm, band, core).start()

    def batch(h, low, high):
        def body(i, carry):
            job(h, low + i)
            return carry

        lax.fori_loop(0, high - low, body, 0)

    if early:
        z_copy(last, beyond).start()
        batch(last, beyond + 1, jnp.where(top, me, sections))
        batch(0, me + 1, jnp.where(me >= half_way, sections, me + 1))
    else:
        every_job(job)

    def second():
        batch(last, 0, jnp.where((me >= half_way) & (me < sections - 1), me, 0))
        batch(0, me + 1, jnp.where((me < half_way) & (me > 0), sections, me + 1))

    def third():
        batch(last, 0, jnp.where(me < half_way, me, 0))
        batch(0, 0, jnp.where(top, me, 0))

    def fourth():
        batch(0, 0, jnp.where(top, 0, me))

    def at_home(i, carry):
        h = hours_sec - 1 - i
        t = me * hours_sec + h
        for c in range(2):
            if early:

                def put(i, x):
                    land[t, halo_pairs + half * c + i] = x

                fill(h, me, 2 * half * c, put)
            else:

                def put(i, x):
                    pack[h, me, i] = x

                fill(h, me, 2 * half * c, put)
                copy = pltpu.make_async_copy(
                    pack.at[h, me], land.at[t, pl.ds(halo_pairs + half * c, half)], local.at[0]
                )
                copy.start()
                copy.wait()
        return carry

    lax.fori_loop(0, hours_sec - least, at_home, 0)

    zero = jnp.zeros((PAD, lanes), jnp.float32)

    def clear(i, carry):
        at = pl.multiple_of(i * 8, 8)
        state[pl.ds(at, 8), :] = zero[:8]
        mixed[pl.ds(at, 8), :] = zero[:8]
        inj[0, pl.ds(at, 8), :] = zero[:8]
        return carry

    lax.fori_loop(0, d["rows"] // 8, clear, 0, unroll=8)
    flux[...] = jnp.zeros_like(flux)
    lhs[...] = jnp.zeros_like(lhs)
    lhs[0:levels, 0:levels] = mixing[...]
    turned_mix = jnp.transpose(lhs[:, 0:128])
    both = turned_mix + pltpu.roll(pltpu.roll(turned_mix, stride, 0), stride, 1)
    high = both.astype(jnp.bfloat16).astype(jnp.float32)
    low = both - high
    none = jnp.zeros_like(both)
    high = jnp.concatenate([high, none], axis=1)
    low = jnp.concatenate([low, none], axis=1)
    deep = 2 * stride
    matrix = high + pltpu.roll(low, deep, 1) + pltpu.roll(high, 2 * deep, 1)
    lhs[...] = matrix

    source = lax.broadcasted_iota(jnp.int32, (wl, lanes), 0)
    into = lax.rem(lax.broadcasted_iota(jnp.int32, (wl, lanes), 1), window)
    first_row = me * own - left
    keep = (into + first_row >= 0) & (into + first_row < lat_rows - 1)
    below = (into > 0) & (into + first_row >= 1) & (into + first_row < lat_rows)
    pick[:, :lanes] = jnp.where(source == into, 1.0, 0.0)
    pick[:, lanes : 2 * lanes] = jnp.where((source == into + window) & keep, 1.0, 0.0)
    pick[:, 2 * lanes :] = jnp.where((source == into + window - 1) & below, 1.0, 0.0)

    def obs_copy(s, n):
        return remote(
            obs.at[s, 0], obs.at[s, 1 + n], us.at[s, n], ur.at[s, n], me, sides[1 - n], core
        )

    beside = range(1 if bands == 2 else 2)

    def hand_obs(s):
        @pl.when(me != s)
        def _():
            remote(obs.at[s, 0], obs.at[s, 0], os.at[0], orr.at[s], me, sides[0], core).wait_recv()

        @pl.when(s > 0)
        def _():
            for n in beside:
                obs_copy(s, n).start()

    def half_copy(t):
        place = land.at[t, pl.ds(my_pairs, half)]
        return remote(place, place, hs.at[t], hr.at[t], me, band, 1 - core)

    def edges(depth):
        found = []
        for side in range(2):
            begin = 0 if side == 0 else own_pairs - depth
            for c in range(2):
                a, b = max(begin, half * c), min(begin + depth, half * (c + 1))
                if a < b:
                    found.append((side, c, a, b))
        return found

    def edge_copy(t, side, c, a, b, q):
        to = halo_pairs + (own_pairs if side == 0 else -own_pairs)
        return remote(
            land.at[t, pl.ds(halo_pairs + a, b - a)], land.at[t, pl.ds(to + a, b - a)],
            xs.at[t, side, q], xr.at[t, side, c], me, sides[side], q,
        )

    def with_depth(t, act):
        if early:
            for depth in range(1, halo_pairs + 1):

                @pl.when((t + 1) // 2 == depth)
                def _():
                    act(depth)

        else:

            @pl.when(t > halo // 2)
            def _():
                act(halo_pairs)

            @pl.when(t <= halo // 2)
            def _():
                act(halo_pairs // 2)

    def hand_winds(t):
        s = t // hours_sec

        @pl.when(me != s)
        def _():
            place = land.at[t, pl.ds(my_pairs, half)]
            remote(place, place, zs.at[0, 0], zr.at[t], me, sides[0], core).wait_recv()

        def act(depth):
            for c in range(2):

                @pl.when(core == c)
                def _():
                    for side, sender, a, b in edges(depth):
                        if sender == c:
                            for q in range(2):
                                edge_copy(t, side, sender, a, b, q).start()

        with_depth(t, act)

        @pl.when(me != s)
        def _():
            half_copy(t).start()

    def take_winds(t):
        s = t // hours_sec

        @pl.when(me != s)
        def _():
            place = land.at[t, pl.ds(halo_pairs + half * (1 - core), half)]
            remote(place, place, hs.at[t], hr.at[t], me, band, 1 - core).wait_recv()

        def act(depth):
            for side, sender, a, b in edges(depth):
                edge_copy(t, side, sender, a, b, 0).wait_recv()

        with_depth(t, act)

    first_row = me * own - left

    def observed(s, piece):
        place = obs[s, piece, 0:1, :].astype(jnp.int32)
        level = place // (cols * lat_rows)
        rest = place - level * (cols * lat_rows)
        column = rest // lat_rows
        row = rest - column * lat_rows - first_row
        hit = lax.broadcasted_iota(jnp.int32, (window, count), 0) == row
        parts = [
            split2(jnp.where(hit, obs[s, piece, 1 + p : 2 + p, :], 0.0)) for p in range(probes)
        ]
        rhs = jnp.concatenate([x[0] for x in parts] + [x[1] for x in parts], axis=0)
        return level, column, rhs

    def placed_sum(hot, rhs):
        got = lax.dot_general(
            hot.astype(jnp.float32).astype(jnp.bfloat16), rhs, (((1,), (1,)), ((), ())),
            preferred_element_type=jnp.float32,
        )
        return got[:, :lanes] + got[:, lanes:]

    def lowest(t):
        return (halo - t) // WIDE

    def highest(t):
        return (halo + cols + t + WIDE - 1) // WIDE

    edge_blocks = halo // WIDE
    own_blocks = cols // WIDE
    together = max(n for n in range(1, 4) if own_blocks % n == 0)

    def inject(s, slot):
        t = s * hours_sec
        for n in beside:
            remote(
                obs.at[s, 0], obs.at[s, 1 + n], us.at[s, n], ur.at[s, n], me, sides[0], core
            ).wait_recv()
        if early:
            lo, hi = lowest(t), highest(t)
            ranges = [
                (0, [(halo, edge_blocks, edge_blocks + own_blocks)]),
                (1, [(halo - cols, lo, edge_blocks)]),
                (2 if bands > 2 else 1, [(halo + cols, edge_blocks + own_blocks, hi)]),
            ]
            if bands == 2:
                ranges = [ranges[0], (1, ranges[1][1] + ranges[2][1])]
            for piece, places in ranges:
                level, column, rhs = observed(s, piece)
                hots = []
                for shift, begin, end in places:
                    place = (column + shift) * stride + level - begin * block
                    chunk = lax.broadcasted_iota(jnp.int32, ((end - begin) * block, count), 0)
                    hots.append((chunk == place).astype(jnp.float32).astype(jnp.bfloat16))
                hot = hots[0] if len(hots) == 1 else jnp.concatenate(hots, axis=0)
                got = lax.dot_general(
                    hot, rhs, (((1,), (1,)), ((), ())), preferred_element_type=jnp.float32
                )
                add = got[:, :lanes] + got[:, lanes:]
                done = 0
                for shift, begin, end in places:
                    size = (end - begin) * block
                    inj[slot, pl.ds(PAD + begin * block, size), :] = add[done : done + size]
                    done += size
            return
        for piece, shift, begin, end, step in (
            (0, halo, edge_blocks, edge_blocks + own_blocks, together),
            (1, halo - cols, lowest(t), edge_blocks, 1),
            (2 if bands > 2 else 1, halo + cols, edge_blocks + own_blocks, highest(t), 1),
        ):
            level, column, rhs = observed(s, piece)
            place = (column + shift) * stride + level
            high_rows = step * block
            chunk = lax.broadcasted_iota(jnp.int32, (high_rows, count), 0)

            def body(i, carry, begin=begin, step=step, place=place, rhs=rhs, chunk=chunk, high_rows=high_rows):
                b = begin + i * step
                add = placed_sum(chunk == place - b * block, rhs)
                inj[slot, pl.ds(pl.multiple_of(PAD + b * block, 8), high_rows), :] = add
                return carry

            lax.fori_loop(0, (end - begin) // step, body, 0)

    def ground(field=state):
        start = PAD + halo * stride
        if lanes == 128:
            return field[pl.ds(start, cols, stride=stride), :]
        rows = [state[start + c * stride : start + c * stride + 1, :] for c in range(cols)]
        return jnp.concatenate(rows, axis=0)

    def add_flux(s, h, x):
        which = obs[s, 0, 1 + probes : 2 + probes, 0:128]
        lane = lax.broadcasted_iota(jnp.int32, (1, 128), 1)
        number = jnp.sum(jnp.where(lane == h, which, 0.0), axis=1, keepdims=True)
        for w in range(d["weeks"]):
            flux[w] += jnp.where(number == w, x, 0.0)

    def surface(s, slot):
        level, column, rhs = observed(0, 0)
        tall = -(-cols // 8) * 8
        chunk = lax.broadcasted_iota(jnp.int32, (tall, count), 0)
        add = placed_sum(chunk == jnp.where(level == 0, column, -1), rhs)
        add_flux(0, 0, add[:cols])

    middle = hours // 2

    def slot_of(t):
        return jnp.where(t > middle, 0, t) if early else 0

    def prepare(t, span=None):
        slot = slot_of(t)
        if not early:
            copy = pltpu.make_async_copy(land.at[t], stage, local.at[0])
            copy.start()
            copy.wait()
        lo, hi = lowest(t), highest(t)
        wm[slot, pl.ds(pl.multiple_of(PAD + lo * block, 8), PAD), :] = jnp.zeros((PAD, lanes), jnp.float32)
        matrix = pick[...].astype(jnp.bfloat16)

        def spread(b, n):
            base = pl.multiple_of(PAD + b * block, 8)
            at = pl.ds(b * WIDE // 2, n * WIDE // 2)
            packed = land[t, at] if early else stage[at]
            packed = packed.reshape(n * block, wl)
            got = jnp.dot(packed, matrix, preferred_element_type=jnp.float32)
            east, north, south = got[:, :lanes], got[:, lanes : 2 * lanes], got[:, 2 * lanes :]
            ep[slot, pl.ds(base, n * block), :] = jnp.maximum(east, 0.0)
            wm[slot, pl.ds(base + stride, n * block), :] = jnp.minimum(east, 0.0)
            npos[slot, pl.ds(base, n * block), :] = jnp.maximum(north, 0.0)
            sneg[slot, pl.ds(base, n * block), :] = jnp.minimum(south, 0.0)

        def one(b, carry):
            spread(b, 1)
            return carry

        def many(i, carry):
            spread(edge_blocks + i * together, together)
            return carry

        if span is not None:
            b = span[0]
            while b < span[1]:
                n = min(3, span[1] - b)
                spread(b, n)
                b += n
            return
        lax.fori_loop(lo, edge_blocks, one, 0)
        lax.fori_loop(0, own_blocks // together, many, 0)
        lax.fori_loop(edge_blocks + own_blocks, hi, one, 0)

    def advance(t, slot, span=None):
        s = t // hours_sec
        h = t - s * hours_sec
        lo, hi = lowest(t), highest(t)

        if span is not None:
            slot = jnp.where(h == 0, s, 0)
        else:

            @pl.when(h == 0)
            def _():
                def body(b, carry):
                    at = pl.ds(pl.multiple_of(PAD + b * block, 8), block)
                    state[at, :] += inj[slot, at, :]
                    return carry

                lax.fori_loop(lo, hi, body, 0)

        add_flux(s, h, ground() if span is None else ground() + ground(inj.at[slot]))
        mix = lhs[0:deep, 0 : 3 * deep].astype(jnp.bfloat16)
        where = slot_of(t)

        def at_block(b):
            return PAD + b * block if span is not None else pl.multiple_of(PAD + b * block, 8)

        def mixing_of(b):
            base = at_block(b)
            parts = [state[pl.ds(base + k * deep, deep), :] for k in range(2)]
            if span is not None:
                parts = [x + inj[slot, pl.ds(base + k * deep, deep), :] for k, x in enumerate(parts)]
            x = jnp.concatenate(parts, axis=1)
            low = x - x.astype(jnp.bfloat16).astype(jnp.float32)
            stack = jnp.concatenate([x, x, low], axis=0).astype(jnp.bfloat16)
            return jnp.dot(mix, stack, preferred_element_type=jnp.float32)

        def keep_mixed(b, got):
            base = at_block(b)
            mixed[pl.ds(base, deep), :] = got[:, :lanes]
            mixed[pl.ds(base + deep, deep), :] = got[:, lanes:]

        def advect(b):
            base = at_block(b)
            at = pl.ds(base, block)
            here = mixed[at, :]
            after = mixed[pl.ds(base + stride, block), :]
            before = mixed[pl.ds(base - stride, block), :]
            g = here + ep[where, at, :] * (after - here) + wm[where, at, :] * (here - before)
            above = pltpu.roll(g, lanes - 1, 1)
            below = pltpu.roll(g, 1, 1)
            return g + npos[where, at, :] * (above - g) + sneg[where, at, :] * (g - below)

        def keep_state(b, x):
            state[pl.ds(at_block(b), block), :] = x

        def only_mix(b, carry):
            keep_mixed(b, mixing_of(b))
            return carry

        def both(b, carry):
            got = mixing_of(b)
            new = advect(b - 2)
            keep_state(b - 2, new)
            keep_mixed(b, got)
            return carry

        def only_advect(b, carry):
            keep_state(b, advect(b))
            return carry

        if span is not None:
            for b in range(span[0], span[1] + 2):
                got = mixing_of(b) if b < span[1] else None
                if b >= span[0] + 2:
                    keep_state(b - 2, advect(b - 2))
                if b < span[1]:
                    keep_mixed(b, got)
            return
        lax.fori_loop(lo, lo + 2, only_mix, 0)
        lax.fori_loop(lo + 2, hi, both, 0)
        lax.fori_loop(hi - 2, hi, only_advect, 0)

    def loop(high, low, run):
        def body(i, carry):
            run(high - i)
            return carry

        lax.fori_loop(0, high - low + 1, body, 0)

    if early:

        hand_obs(sections - 1)
        pieces = [second, third, fourth]
        for s in range(sections - 1, 0, -1):
            hand_obs(s - 1)
            inject(s, s)
            if pieces:
                pieces.pop(0)()
        while pieces:
            pieces.pop(0)()
        surface(0, 0)
        hand_winds(hours - 1)
        far = (lowest(hours - 1), highest(hours - 1))
        near = (lowest(middle), highest(middle))

        def ready(t, span):
            take_winds(t)
            prepare(t, span)

        def outer(t):
            ready(t, far)

            @pl.when(t > middle + 1)
            def _():
                hand_winds(t - 1)

            @pl.when(t == middle + 1)
            def _():
                loop(middle - 1, 1, hand_winds)
                loop(middle - 1, 1, lambda u: ready(u, near))
                hand_winds(middle)

            advance(t, 0, far)

        loop(hours - 1, middle + 1, outer)
        ready(middle, near)
        loop(middle, 1, lambda t: advance(t, 0, near))
    else:
        loop(sections - 1, 0, hand_obs)
        surface(0, 0)

        def whole(t):
            s = t // hours_sec

            @pl.when(t == s * hours_sec)
            def _():
                inject(s, 0)

            hand_winds(t)
            take_winds(t)
            prepare(t)
            advance(t, 0)

        loop(hours - 1, 1, whole)

    add_flux(0, 0, ground())
    for w in range(d["weeks"]):
        square = flux[w] * flux[w]
        est[w] = (square + pltpu.roll(square, lanes - window, 1)) * 0.5

    every_job(lambda h, target: z_copy(h, target).wait_send())
    for k in range(1, sections):
        mine = obs.at[me, 0]
        remote(mine, mine, os.at[k], orr.at[me], me, sides[0], core).wait_send()

    def sent_obs(s):
        for n in beside:
            obs_copy(s, n).wait_send()

    loop(sections - 1, 1, sent_obs)

    def sent_winds(t):
        @pl.when(me != t // hours_sec)
        def _():
            half_copy(t).wait_send()

        def act(depth):
            for c in range(2):

                @pl.when(core == c)
                def _():
                    for side, sender, a, b in edges(depth):
                        if sender == c:
                            for q in range(2):
                                edge_copy(t, side, sender, a, b, q).wait_send()

        with_depth(t, act)

    loop(hours - 1, 1, sent_winds)


def on_device(winds, mixing, obs_cell, obs_weight, probe_sign, week_map, prior_precision):
    week_count, _, own = prior_precision.shape
    d = plan(
        lax.axis_size("tm"), lax.axis_size("lon"), winds.shape[2], winds.shape[4], winds.shape[3],
        winds.shape[5], own, probe_sign.shape[0], week_count, obs_cell.shape[2],
    )
    sections, hours, hours_sec = d["sections"], d["hours"], d["hours_sec"]
    lanes, rows, cols, left = d["lanes"], d["rows"], d["cols"], d["left"]
    early = d["early"]
    wire = (d["half"], 2 * d["stride"], 2 * d["window"])
    landing = (hours, d["pairs"]) + wire[1:]
    slots = hours // 2 + 1 if early else 1
    inj_slots = sections if early else 1
    sem = pltpu.SemaphoreType.DMA
    scratch = [
        pltpu.VMEM((hours_sec, sections) + wire, jnp.bfloat16),
        pltpu.VMEM((2 * d["half"] * d["stride"], 2 * d["window"]), jnp.float32),
        pltpu.VMEM((sections, 3, 2 + d["probes"], d["count"]), jnp.float32),
        pltpu.VMEM((128, 256), jnp.float32),
        pltpu.VMEM((2 * d["window"], 3 * lanes), jnp.float32),
        pltpu.VMEM((rows, lanes), jnp.float32),
        pltpu.VMEM((rows, lanes), jnp.float32),
        pltpu.VMEM((inj_slots, rows, lanes), jnp.float32),
    ] + [pltpu.VMEM((slots, rows, lanes), jnp.float32)] * 4 + [
        pltpu.VMEM((week_count, cols, lanes), jnp.float32),
        sem((hours_sec, sections)), sem((hours,)), sem((hours,)), sem((hours,)),
        sem((hours, 2, 2)), sem((hours, 2, 2)), sem((sections,)), sem((sections,)),
        sem((sections, 2)), sem((sections, 2)), sem((1,)),
    ]
    outs = [jax.ShapeDtypeStruct((week_count, cols, lanes), jnp.float32)]
    out_specs = [pl.BlockSpec(memory_space=pltpu.VMEM)]
    if early:
        scratch = [pltpu.VMEM(landing, jnp.bfloat16)] + scratch
    else:
        outs.append(jax.ShapeDtypeStruct(landing, jnp.bfloat16))
        out_specs.append(pl.BlockSpec(memory_space=pl.ANY))
        scratch = [pltpu.VMEM(landing[1:], jnp.bfloat16)] + scratch
    got = pl.pallas_call(
        functools.partial(fused_kernel, d),
        out_shape=tuple(outs),
        in_specs=[pl.BlockSpec(memory_space=pltpu.VMEM)] * 6,
        out_specs=tuple(out_specs),
        scratch_shapes=scratch,
        compiler_params=pltpu.CompilerParams(
            collective_id=0, has_side_effects=True, vmem_limit_bytes=(38 if early else 56) << 20
        ),
    )(
        winds.transpose(0, 1, 2, 4, 3, 5), mixing, obs_cell[0], obs_weight[0],
        probe_sign[:, 0], week_map,
    )
    return (prior_precision + got[0][..., left : left + own])[None]


def solution(mesh):
    placed = (
        P(None, ("groups", "tm"), None, None, "lon", None),
        P(),
        P(("groups", "tm"), "lon", None),
        P(("groups", "tm"), "lon", None),
        P("probe", ("groups", "tm"), "lon", None),
        P(("groups", "tm"), None),
        P("groups", "lon", "tm"),
    )
    return jax.shard_map(
        on_device,
        mesh=mesh,
        in_specs=placed,
        out_specs=P("probe", "groups", "lon", "tm"),
        check_vma=False,
    )
```

```python
import functools

import jax
import jax.numpy as jnp
from jax import lax
from jax.experimental import pallas as pl
from jax.experimental.pallas import tpu as pltpu
from jax.sharding import PartitionSpec as P

WIDE = 4
PAD = 40


def split2(x):
    high = x.astype(jnp.bfloat16)
    low = (x - high.astype(jnp.float32)).astype(jnp.bfloat16)
    return high, low


def plan(sections, bands, hours_sec, cols, levels, lat_rows, own, probes, weeks, count):
    hours = sections * hours_sec
    halo = -(-hours // WIDE) * WIDE
    window = -(-(own + 2 * hours) // 64) * 64
    d = dict(
        sections=sections, bands=bands, hours_sec=hours_sec, cols=cols, levels=levels,
        lat_rows=lat_rows, own=own, probes=probes, weeks=weeks, count=count, hours=hours,
        halo=halo, left=hours, window=window, lanes=window * probes,
        half=cols // 4, halo_pairs=halo // 2, pairs=(cols + 2 * halo) // 2,
        blocks=(cols + 2 * halo) // WIDE,
    )
    d["stride"] = levels if d["lanes"] == 128 else -(-levels // 8) * 8
    d["block"] = WIDE * d["stride"]
    d["rows"] = PAD + (d["blocks"] + 1) * d["block"]
    d["early"] = hours <= 8 and hours_sec == 2 and sections % 2 == 0
    return d


def fused_kernel(d, winds, mixing, cell, weight, sign, week, *refs):
    sections, bands, hours_sec, hours = d["sections"], d["bands"], d["hours_sec"], d["hours"]
    cols, levels, lat_rows, own = d["cols"], d["levels"], d["lat_rows"], d["own"]
    probes, count, halo, left = d["probes"], d["count"], d["halo"], d["left"]
    window, lanes, half, halo_pairs = d["window"], d["lanes"], d["half"], d["halo_pairs"]
    block, early, stride = d["block"], d["early"], d["stride"]
    if early:
        est, land, refs = refs[0], refs[1], refs[2:]
        stage = None
    else:
        est, land, stage, refs = refs[0], refs[1], refs[2], refs[3:]
    (pack, flat, obs, lhs, pick, state, mixed, inj, ep, wm, npos, sneg, flux,
     zs, zr, hs, hr, xs, xr, os, orr, us, ur, local) = refs
    own_pairs = 2 * half
    me = lax.axis_index("tm")
    band = lax.axis_index("lon")
    core = lax.axis_index("probe")
    sides = [lax.rem(band + bands - 1, bands), lax.rem(band + 1, bands)]
    if bands == 2:
        greet = sides[:1]
    else:
        greet = sides

    def remote(src, dst, send, recv, tm, lon, probe):
        return pltpu.make_async_remote_copy(
            src_ref=src, dst_ref=dst, send_sem=send, recv_sem=recv,
            device_id={"tm": tm, "lon": lon, "probe": probe},
            device_id_type=pl.DeviceIdType.MESH,
        )

    if early:
        for t in range(1, hours):
            reach = (t + 1) // 2
            for n in range((halo - t) // WIDE * WIDE // 2, halo_pairs - reach):
                land[t, n] = jnp.zeros(land.shape[2:], land.dtype)
                land[t, 2 * halo_pairs + own_pairs - 1 - n] = jnp.zeros(land.shape[2:], land.dtype)

    barrier = pltpu.get_barrier_semaphore()

    def hello(tm, lon, probe):
        pl.semaphore_signal(
            barrier, inc=1, device_id={"tm": tm, "lon": lon, "probe": probe},
            device_id_type=pl.DeviceIdType.MESH,
        )

    for k in range(1, sections):
        hello(lax.rem(me + k, sections), band, core)
    for lon in greet:
        for q in range(2):
            hello(me, lon, q)
    hello(me, band, 1 - core)

    obs[me, 0, 0:1, :] = cell[...].astype(jnp.float32)
    for p in range(probes):
        obs[me, 0, 1 + p : 2 + p, :] = (2 * sign[p] - 1).astype(jnp.float32) * weight[...]
    lane_row = lax.broadcasted_iota(jnp.int32, (1, count), 1)
    weeks_row = jnp.zeros((1, count), jnp.float32)
    for h in range(hours_sec):
        weeks_row = jnp.where(lane_row == h, week[0:1, h : h + 1].astype(jnp.float32), weeks_row)
    obs[me, 0, 1 + probes : 2 + probes, :] = weeks_row

    if stride != levels:
        flat[...] = jnp.zeros_like(flat)
    wl = 2 * window
    lat_tiles = -(-lat_rows // 128)

    def packed_column(h, column, start):
        tiles = []
        for comp in range(2):
            row = []
            for k in range(lat_tiles):
                x = winds[comp, 0, h, column, :, k * 128 : min(k * 128 + 128, lat_rows)]
                x = x.astype(jnp.float32)
                if x.shape[1] < 128:
                    x = jnp.concatenate(
                        [x, jnp.zeros((levels, 128 - x.shape[1]), jnp.float32)], axis=1
                    )
                row.append(x)
            tiles.append(row)
        lane = lax.broadcasted_iota(jnp.int32, (levels, 128), 1)
        parts = []
        for v in range(wl // 128):
            out = jnp.zeros((levels, 128), jnp.float32)
            for comp in range(2):
                begin = comp * window - v * 128
                if begin >= 128 or begin + window <= 0:
                    continue
                shift = lax.rem(begin - start + 512, 128)
                at = lane - begin
                row = at + start
                for k in range(lat_tiles):
                    inside = (
                        (at >= 0) & (at < window) & (row >= k * 128)
                        & (row < min(k * 128 + 128, lat_rows))
                    )
                    out = jnp.where(inside, pltpu.roll(tiles[comp][k], shift, 1), out)
            parts.append(out)
        return parts[0] if len(parts) == 1 else jnp.concatenate(parts, axis=1)

    def fill(h, target, first_column, put):
        start = target * own - left

        def body(i, carry):
            for c in range(2):
                at = pl.multiple_of(i * 2 * stride, 8) + c * stride
                flat[pl.ds(at, levels), :] = packed_column(h, first_column + 2 * i + c, start)
            return carry

        lax.fori_loop(0, half, body, 0, unroll=3)

        def cast(i, carry):
            x = flat[pl.ds(pl.multiple_of(i * 2 * stride, 8), 2 * stride), :]
            put(i, x.astype(jnp.bfloat16))
            return carry

        lax.fori_loop(0, half, cast, 0, unroll=3)

    least = jnp.where(me == 0, 1, 0)
    my_pairs = halo_pairs + half * core

    def z_copy(h, target):
        t = me * hours_sec + h
        return remote(
            pack.at[h, target], land.at[t, pl.ds(my_pairs, half)], zs.at[h, target], zr.at[t],
            target, band, core,
        )

    def job(h, target):
        def put(i, x):
            pack[h, target, i] = x

        fill(h, target, 2 * half * core, put)
        z_copy(h, target).start()

    def every_job(run):
        def upper(i, carry):
            h = hours_sec - 1 - i

            def target(k, inner):
                run(h, sections - 1 - k)
                return inner

            return lax.fori_loop(0, sections - 1 - me, target, carry)

        lax.fori_loop(0, hours_sec - least, upper, 0)

        def lower(i, carry):
            h = hours_sec - 1 - i

            def target(k, inner):
                run(h, k)
                return inner

            return lax.fori_loop(0, me, target, carry)

        lax.fori_loop(0, hours_sec - least, lower, 0)

    last = hours_sec - 1
    if early:
        half_way = sections // 2
        top = me == sections - 1
        beyond = jnp.where(top, 0, me + 1)

        def put_first(i, x):
            pack[last, beyond, i] = x

        fill(last, beyond, 2 * half * core, put_first)

    pl.semaphore_wait(barrier, sections - 1 + 2 * len(greet) + 1)

    for k in range(1, sections):
        tm = lax.rem(me + k, sections)
        mine = obs.at[me, 0]
        remote(mine, mine, os.at[k], orr.at[me], tm, band, core).start()

    def each(run, h, low, high):
        def body(i, carry):
            run(h, low + i)
            return carry

        lax.fori_loop(0, high - low, body, 0)

    def fill_job(h, target):
        def put(i, x):
            pack[h, target, i] = x

        fill(h, target, 2 * half * core, put)

    def start(h, target):
        z_copy(h, target).start()

    def sent(h, target):
        z_copy(h, target).wait_send()

    if early:
        lower = me < half_way
        upper = (me >= half_way) & (me < sections - 1)
        z_copy(last, beyond).start()
        each(job, last, beyond + 1, jnp.where(top, half_way, sections))
        each(job, 0, me + 1, jnp.where(me >= half_way, sections, me + 1))

        def rest(run):
            each(run, 0, me + 1, jnp.where(lower & (me > 0), sections, me + 1))
            each(run, last, jnp.where(top, half_way, 0), me)
            each(run, 0, 0, me)

        rest(fill_job)

        @pl.when(lower)
        def _():
            rest(start)

    else:
        every_job(job)

    def second():
        @pl.when(upper)
        def _():
            each(sent, last, me + 1, sections)
            each(sent, 0, me + 1, sections)
            each(start, last, 0, me)

        @pl.when(top)
        def _():
            each(sent, last, 0, half_way)
            each(start, last, half_way, me)
            each(start, 0, 0, half_way)

    def third():
        @pl.when(upper)
        def _():
            each(sent, last, 0, me)
            each(start, 0, 0, me)

        @pl.when(top)
        def _():
            each(sent, last, half_way, me)
            each(start, 0, half_way, me)

    def finish_sends():
        if not early:
            every_job(sent)
            return

        @pl.when(lower)
        def _():
            each(sent, last, me + 1, sections)
            rest(sent)

        @pl.when(upper)
        def _():
            each(sent, 0, 0, me)

        @pl.when(top)
        def _():
            each(sent, 0, 0, me)

    def at_home(i, carry):
        h = hours_sec - 1 - i
        t = me * hours_sec + h
        for c in range(2):
            if early:

                def put(i, x):
                    land[t, halo_pairs + half * c + i] = x

                fill(h, me, 2 * half * c, put)
            else:

                def put(i, x):
                    pack[h, me, i] = x

                fill(h, me, 2 * half * c, put)
                copy = pltpu.make_async_copy(
                    pack.at[h, me], land.at[t, pl.ds(halo_pairs + half * c, half)], local.at[0]
                )
                copy.start()
                copy.wait()
        return carry

    lax.fori_loop(0, hours_sec - least, at_home, 0)

    zero = jnp.zeros((PAD, lanes), jnp.float32)

    def clear(i, carry):
        at = pl.multiple_of(i * 8, 8)
        state[pl.ds(at, 8), :] = zero[:8]
        mixed[pl.ds(at, 8), :] = zero[:8]
        inj[0, pl.ds(at, 8), :] = zero[:8]
        return carry

    lax.fori_loop(0, d["rows"] // 8, clear, 0, unroll=8)
    flux[...] = jnp.zeros_like(flux)
    lhs[...] = jnp.zeros_like(lhs)
    lhs[0:levels, 0:levels] = mixing[...]
    turned_mix = jnp.transpose(lhs[:, 0:128])
    both = turned_mix + pltpu.roll(pltpu.roll(turned_mix, stride, 0), stride, 1)
    high = both.astype(jnp.bfloat16).astype(jnp.float32)
    low = both - high
    none = jnp.zeros_like(both)
    high = jnp.concatenate([high, none], axis=1)
    low = jnp.concatenate([low, none], axis=1)
    deep = 2 * stride
    matrix = high + pltpu.roll(low, deep, 1) + pltpu.roll(high, 2 * deep, 1)
    lhs[...] = matrix

    source = lax.broadcasted_iota(jnp.int32, (wl, lanes), 0)
    into = lax.rem(lax.broadcasted_iota(jnp.int32, (wl, lanes), 1), window)
    first_row = me * own - left
    keep = (into + first_row >= 0) & (into + first_row < lat_rows - 1)
    below = (into > 0) & (into + first_row >= 1) & (into + first_row < lat_rows)
    pick[:, :lanes] = jnp.where(source == into, 1.0, 0.0)
    pick[:, lanes : 2 * lanes] = jnp.where((source == into + window) & keep, 1.0, 0.0)
    pick[:, 2 * lanes :] = jnp.where((source == into + window - 1) & below, 1.0, 0.0)

    def obs_copy(s, n):
        return remote(
            obs.at[s, 0], obs.at[s, 1 + n], us.at[s, n], ur.at[s, n], me, sides[1 - n], core
        )

    beside = range(1 if bands == 2 else 2)

    def hand_obs(s):
        @pl.when(me != s)
        def _():
            remote(obs.at[s, 0], obs.at[s, 0], os.at[0], orr.at[s], me, sides[0], core).wait_recv()

        @pl.when(s > 0)
        def _():
            for n in beside:
                obs_copy(s, n).start()

    def half_copy(t):
        place = land.at[t, pl.ds(my_pairs, half)]
        return remote(place, place, hs.at[t], hr.at[t], me, band, 1 - core)

    def edges(depth):
        found = []
        for side in range(2):
            begin = 0 if side == 0 else own_pairs - depth
            for c in range(2):
                a, b = max(begin, half * c), min(begin + depth, half * (c + 1))
                if a < b:
                    found.append((side, c, a, b))
        return found

    def edge_copy(t, side, c, a, b, q):
        to = halo_pairs + (own_pairs if side == 0 else -own_pairs)
        return remote(
            land.at[t, pl.ds(halo_pairs + a, b - a)], land.at[t, pl.ds(to + a, b - a)],
            xs.at[t, side, q], xr.at[t, side, c], me, sides[side], q,
        )

    def with_depth(t, act):
        if early:
            for depth in range(1, halo_pairs + 1):

                @pl.when((t + 1) // 2 == depth)
                def _():
                    act(depth)

        else:

            @pl.when(t > halo // 2)
            def _():
                act(halo_pairs)

            @pl.when(t <= halo // 2)
            def _():
                act(halo_pairs // 2)

    def hand_winds(t):
        s = t // hours_sec

        @pl.when(me != s)
        def _():
            place = land.at[t, pl.ds(my_pairs, half)]
            remote(place, place, zs.at[0, 0], zr.at[t], me, sides[0], core).wait_recv()

        def act(depth):
            for c in range(2):

                @pl.when(core == c)
                def _():
                    for side, sender, a, b in edges(depth):
                        if sender == c:
                            for q in range(2):
                                edge_copy(t, side, sender, a, b, q).start()

        with_depth(t, act)

        @pl.when(me != s)
        def _():
            half_copy(t).start()

    def take_winds(t):
        s = t // hours_sec

        @pl.when(me != s)
        def _():
            place = land.at[t, pl.ds(halo_pairs + half * (1 - core), half)]
            remote(place, place, hs.at[t], hr.at[t], me, band, 1 - core).wait_recv()

        def act(depth):
            for side, sender, a, b in edges(depth):
                edge_copy(t, side, sender, a, b, 0).wait_recv()

        with_depth(t, act)

    first_row = me * own - left

    def observed(s, piece):
        place = obs[s, piece, 0:1, :].astype(jnp.int32)
        level = place // (cols * lat_rows)
        rest = place - level * (cols * lat_rows)
        column = rest // lat_rows
        row = rest - column * lat_rows - first_row
        hit = lax.broadcasted_iota(jnp.int32, (window, count), 0) == row
        parts = [
            split2(jnp.where(hit, obs[s, piece, 1 + p : 2 + p, :], 0.0)) for p in range(probes)
        ]
        rhs = jnp.concatenate([x[0] for x in parts] + [x[1] for x in parts], axis=0)
        return level, column, rhs

    def placed_sum(hot, rhs):
        got = lax.dot_general(
            hot.astype(jnp.float32).astype(jnp.bfloat16), rhs, (((1,), (1,)), ((), ())),
            preferred_element_type=jnp.float32,
        )
        return got[:, :lanes] + got[:, lanes:]

    def lowest(t):
        return (halo - t) // WIDE

    def highest(t):
        return (halo + cols + t + WIDE - 1) // WIDE

    edge_blocks = halo // WIDE
    own_blocks = cols // WIDE
    together = max(n for n in range(1, 4) if own_blocks % n == 0)

    def inject(s, slot):
        t = s * hours_sec
        for n in beside:
            remote(
                obs.at[s, 0], obs.at[s, 1 + n], us.at[s, n], ur.at[s, n], me, sides[0], core
            ).wait_recv()
        if early:
            lo, hi = lowest(t), highest(t)
            ranges = [
                (0, [(halo, edge_blocks, edge_blocks + own_blocks)]),
                (1, [(halo - cols, lo, edge_blocks)]),
                (2 if bands > 2 else 1, [(halo + cols, edge_blocks + own_blocks, hi)]),
            ]
            if bands == 2:
                ranges = [ranges[0], (1, ranges[1][1] + ranges[2][1])]
            for piece, places in ranges:
                level, column, rhs = observed(s, piece)
                hots = []
                for shift, begin, end in places:
                    place = (column + shift) * stride + level - begin * block
                    chunk = lax.broadcasted_iota(jnp.int32, ((end - begin) * block, count), 0)
                    hots.append((chunk == place).astype(jnp.float32).astype(jnp.bfloat16))
                hot = hots[0] if len(hots) == 1 else jnp.concatenate(hots, axis=0)
                got = lax.dot_general(
                    hot, rhs, (((1,), (1,)), ((), ())), preferred_element_type=jnp.float32
                )
                add = got[:, :lanes] + got[:, lanes:]
                done = 0
                for shift, begin, end in places:
                    size = (end - begin) * block
                    inj[slot, pl.ds(PAD + begin * block, size), :] = add[done : done + size]
                    done += size
            return
        for piece, shift, begin, end, step in (
            (0, halo, edge_blocks, edge_blocks + own_blocks, together),
            (1, halo - cols, lowest(t), edge_blocks, 1),
            (2 if bands > 2 else 1, halo + cols, edge_blocks + own_blocks, highest(t), 1),
        ):
            level, column, rhs = observed(s, piece)
            place = (column + shift) * stride + level
            high_rows = step * block
            chunk = lax.broadcasted_iota(jnp.int32, (high_rows, count), 0)

            def body(i, carry, begin=begin, step=step, place=place, rhs=rhs, chunk=chunk, high_rows=high_rows):
                b = begin + i * step
                add = placed_sum(chunk == place - b * block, rhs)
                inj[slot, pl.ds(pl.multiple_of(PAD + b * block, 8), high_rows), :] = add
                return carry

            lax.fori_loop(0, (end - begin) // step, body, 0)

    def ground(field=state):
        start = PAD + halo * stride
        if lanes == 128:
            return field[pl.ds(start, cols, stride=stride), :]
        rows = [state[start + c * stride : start + c * stride + 1, :] for c in range(cols)]
        return jnp.concatenate(rows, axis=0)

    def add_flux(s, h, x):
        which = obs[s, 0, 1 + probes : 2 + probes, 0:128]
        lane = lax.broadcasted_iota(jnp.int32, (1, 128), 1)
        number = jnp.sum(jnp.where(lane == h, which, 0.0), axis=1, keepdims=True)
        for w in range(d["weeks"]):
            flux[w] += jnp.where(number == w, x, 0.0)

    def surface(s, slot):
        level, column, rhs = observed(0, 0)
        tall = -(-cols // 8) * 8
        chunk = lax.broadcasted_iota(jnp.int32, (tall, count), 0)
        add = placed_sum(chunk == jnp.where(level == 0, column, -1), rhs)
        add_flux(0, 0, add[:cols])

    middle = hours // 2

    def slot_of(t):
        return t if early else 0

    def prepare(t, span=None):
        slot = slot_of(t)
        if not early:
            copy = pltpu.make_async_copy(land.at[t], stage, local.at[0])
            copy.start()
            copy.wait()
        lo, hi = lowest(t), highest(t)
        wm[slot, pl.ds(pl.multiple_of(PAD + lo * block, 8), PAD), :] = jnp.zeros((PAD, lanes), jnp.float32)
        matrix = pick[...].astype(jnp.bfloat16)

        def spread(b, n):
            base = pl.multiple_of(PAD + b * block, 8)
            at = pl.ds(b * WIDE // 2, n * WIDE // 2)
            packed = land[t, at] if early else stage[at]
            packed = packed.reshape(n * block, wl)
            got = jnp.dot(packed, matrix, preferred_element_type=jnp.float32)
            east, north, south = got[:, :lanes], got[:, lanes : 2 * lanes], got[:, 2 * lanes :]
            ep[slot, pl.ds(base, n * block), :] = jnp.maximum(east, 0.0)
            wm[slot, pl.ds(base + stride, n * block), :] = jnp.minimum(east, 0.0)
            npos[slot, pl.ds(base, n * block), :] = jnp.maximum(north, 0.0)
            sneg[slot, pl.ds(base, n * block), :] = jnp.minimum(south, 0.0)

        def one(b, carry):
            spread(b, 1)
            return carry

        def many(i, carry):
            spread(edge_blocks + i * together, together)
            return carry

        if span is not None:
            b = span[0]
            while b < span[1]:
                n = min(3, span[1] - b)
                spread(b, n)
                b += n
            return
        lax.fori_loop(lo, edge_blocks, one, 0)
        lax.fori_loop(0, own_blocks // together, many, 0)
        lax.fori_loop(edge_blocks + own_blocks, hi, one, 0)

    def advance(t, slot, span=None):
        s = t // hours_sec
        h = t - s * hours_sec
        lo, hi = lowest(t), highest(t)

        if span is not None:
            slot = jnp.where(h == 0, s, 0)
        else:

            @pl.when(h == 0)
            def _():
                def body(b, carry):
                    at = pl.ds(pl.multiple_of(PAD + b * block, 8), block)
                    state[at, :] += inj[slot, at, :]
                    return carry

                lax.fori_loop(lo, hi, body, 0)

        add_flux(s, h, ground() if span is None else ground() + ground(inj.at[slot]))
        mix = lhs[0:deep, 0 : 3 * deep].astype(jnp.bfloat16)
        where = slot_of(t)

        def at_block(b):
            return PAD + b * block if span is not None else pl.multiple_of(PAD + b * block, 8)

        def mixing_of(b):
            base = at_block(b)
            parts = [state[pl.ds(base + k * deep, deep), :] for k in range(2)]
            if span is not None:
                parts = [x + inj[slot, pl.ds(base + k * deep, deep), :] for k, x in enumerate(parts)]
            x = jnp.concatenate(parts, axis=1)
            low = x - x.astype(jnp.bfloat16).astype(jnp.float32)
            stack = jnp.concatenate([x, x, low], axis=0).astype(jnp.bfloat16)
            return jnp.dot(mix, stack, preferred_element_type=jnp.float32)

        def keep_mixed(b, got):
            base = at_block(b)
            mixed[pl.ds(base, deep), :] = got[:, :lanes]
            mixed[pl.ds(base + deep, deep), :] = got[:, lanes:]

        def advect(b):
            base = at_block(b)
            at = pl.ds(base, block)
            here = mixed[at, :]
            after = mixed[pl.ds(base + stride, block), :]
            before = mixed[pl.ds(base - stride, block), :]
            g = here + ep[where, at, :] * (after - here) + wm[where, at, :] * (here - before)
            above = pltpu.roll(g, lanes - 1, 1)
            below = pltpu.roll(g, 1, 1)
            return g + npos[where, at, :] * (above - g) + sneg[where, at, :] * (g - below)

        def keep_state(b, x):
            state[pl.ds(at_block(b), block), :] = x

        def only_mix(b, carry):
            keep_mixed(b, mixing_of(b))
            return carry

        def both(b, carry):
            got = mixing_of(b)
            new = advect(b - 2)
            keep_state(b - 2, new)
            keep_mixed(b, got)
            return carry

        def only_advect(b, carry):
            keep_state(b, advect(b))
            return carry

        if span is not None:
            for b in range(span[0], span[1] + 2):
                got = mixing_of(b) if b < span[1] else None
                if b >= span[0] + 2:
                    keep_state(b - 2, advect(b - 2))
                if b < span[1]:
                    keep_mixed(b, got)
            return
        lax.fori_loop(lo, lo + 2, only_mix, 0)
        lax.fori_loop(lo + 2, hi, both, 0)
        lax.fori_loop(hi - 2, hi, only_advect, 0)

    def loop(high, low, run):
        def body(i, carry):
            run(high - i)
            return carry

        lax.fori_loop(0, high - low + 1, body, 0)

    if early:

        loop(hours_sec - 1, least, lambda h: hand_winds(me * hours_sec + h))
        hand_obs(sections - 1)
        second()
        for s in range(sections - 1, 0, -1):
            hand_obs(s - 1)
            inject(s, s)
        surface(0, 0)
        third()
        far = (lowest(hours - 1), highest(hours - 1))
        near = (lowest(middle), highest(middle))

        code = 0
        for z in range(sections):
            mine = [t for t in range(hours - 1, 0, -1) if t // hours_sec == z]
            low_hours = [t for t in range(middle - 1, 0, -1) if t not in mine]
            high_hours = [t for t in range(hours - 1, middle - 1, -1) if t not in mine]
            if z < half_way:
                high_hours.sort(key=lambda t: (-(t % hours_sec), -t))
                order = mine + low_hours + high_hours
            else:
                order = mine + high_hours + low_hours
            code = jnp.where(me == z, sum(t * hours**k for k, t in enumerate(order)), code)

        def ready(i, code):
            t = lax.rem(code, hours)
            code = code // hours
            after = lax.rem(code, hours)
            pl.when(me != after // hours_sec)(lambda: hand_winds(after))
            take_winds(t)
            pl.when(t >= middle + 1)(lambda: prepare(t, far))
            pl.when(t <= middle)(lambda: prepare(t, near))
            return code

        final = lax.fori_loop(0, hours - 2, ready, code)
        loop(hours - 1, middle + 1, lambda t: advance(t, 0, far))
        take_winds(final)
        prepare(final, near)
        loop(middle, 1, lambda t: advance(t, 0, near))
    else:
        loop(sections - 1, 0, hand_obs)
        surface(0, 0)

        def whole(t):
            s = t // hours_sec

            @pl.when(t == s * hours_sec)
            def _():
                inject(s, 0)

            hand_winds(t)
            take_winds(t)
            prepare(t)
            advance(t, 0)

        loop(hours - 1, 1, whole)

    add_flux(0, 0, ground())
    for w in range(d["weeks"]):
        square = flux[w] * flux[w]
        est[w] = (square + pltpu.roll(square, lanes - window, 1)) * 0.5

    finish_sends()
    for k in range(1, sections):
        mine = obs.at[me, 0]
        remote(mine, mine, os.at[k], orr.at[me], me, sides[0], core).wait_send()

    def sent_obs(s):
        for n in beside:
            obs_copy(s, n).wait_send()

    loop(sections - 1, 1, sent_obs)

    def sent_winds(t):
        @pl.when(me != t // hours_sec)
        def _():
            half_copy(t).wait_send()

        def act(depth):
            for c in range(2):

                @pl.when(core == c)
                def _():
                    for side, sender, a, b in edges(depth):
                        if sender == c:
                            for q in range(2):
                                edge_copy(t, side, sender, a, b, q).wait_send()

        with_depth(t, act)

    loop(hours - 1, 1, sent_winds)


def on_device(winds, mixing, obs_cell, obs_weight, probe_sign, week_map, prior_precision):
    week_count, _, own = prior_precision.shape
    d = plan(
        lax.axis_size("tm"), lax.axis_size("lon"), winds.shape[2], winds.shape[4], winds.shape[3],
        winds.shape[5], own, probe_sign.shape[0], week_count, obs_cell.shape[2],
    )
    sections, hours, hours_sec = d["sections"], d["hours"], d["hours_sec"]
    lanes, rows, cols, left = d["lanes"], d["rows"], d["cols"], d["left"]
    early = d["early"]
    wire = (d["half"], 2 * d["stride"], 2 * d["window"])
    landing = (hours, d["pairs"]) + wire[1:]
    slots = hours if early else 1
    inj_slots = sections if early else 1
    sem = pltpu.SemaphoreType.DMA
    scratch = [
        pltpu.VMEM((hours_sec, sections) + wire, jnp.bfloat16),
        pltpu.VMEM((2 * d["half"] * d["stride"], 2 * d["window"]), jnp.float32),
        pltpu.VMEM((sections, 3, 2 + d["probes"], d["count"]), jnp.float32),
        pltpu.VMEM((128, 256), jnp.float32),
        pltpu.VMEM((2 * d["window"], 3 * lanes), jnp.float32),
        pltpu.VMEM((rows, lanes), jnp.float32),
        pltpu.VMEM((rows, lanes), jnp.float32),
        pltpu.VMEM((inj_slots, rows, lanes), jnp.float32),
    ] + [pltpu.VMEM((slots, rows, lanes), jnp.float32)] * 4 + [
        pltpu.VMEM((week_count, cols, lanes), jnp.float32),
        sem((hours_sec, sections)), sem((hours,)), sem((hours,)), sem((hours,)),
        sem((hours, 2, 2)), sem((hours, 2, 2)), sem((sections,)), sem((sections,)),
        sem((sections, 2)), sem((sections, 2)), sem((1,)),
    ]
    outs = [jax.ShapeDtypeStruct((week_count, cols, lanes), jnp.float32)]
    out_specs = [pl.BlockSpec(memory_space=pltpu.VMEM)]
    if early:
        scratch = [pltpu.VMEM(landing, jnp.bfloat16)] + scratch
    else:
        outs.append(jax.ShapeDtypeStruct(landing, jnp.bfloat16))
        out_specs.append(pl.BlockSpec(memory_space=pl.ANY))
        scratch = [pltpu.VMEM(landing[1:], jnp.bfloat16)] + scratch
    got = pl.pallas_call(
        functools.partial(fused_kernel, d),
        out_shape=tuple(outs),
        in_specs=[pl.BlockSpec(memory_space=pltpu.VMEM)] * 6,
        out_specs=tuple(out_specs),
        scratch_shapes=scratch,
        compiler_params=pltpu.CompilerParams(
            collective_id=0, has_side_effects=True, vmem_limit_bytes=(51 if early else 56) << 20
        ),
    )(
        winds.transpose(0, 1, 2, 4, 3, 5), mixing, obs_cell[0], obs_weight[0],
        probe_sign[:, 0], week_map,
    )
    return (prior_precision + got[0][..., left : left + own])[None]


def solution(mesh):
    placed = (
        P(None, ("groups", "tm"), None, None, "lon", None),
        P(),
        P(("groups", "tm"), "lon", None),
        P(("groups", "tm"), "lon", None),
        P("probe", ("groups", "tm"), "lon", None),
        P(("groups", "tm"), None),
        P("groups", "lon", "tm"),
    )
    return jax.shard_map(
        on_device,
        mesh=mesh,
        in_specs=placed,
        out_specs=P("probe", "groups", "lon", "tm"),
        check_vma=False,
    )
```

```python
import functools

import jax
import jax.numpy as jnp
from jax import lax
from jax.experimental import pallas as pl
from jax.experimental.pallas import tpu as pltpu
from jax.sharding import PartitionSpec as P

WIDE = 4
PAD = 40


def split2(x):
    high = x.astype(jnp.bfloat16)
    low = (x - high.astype(jnp.float32)).astype(jnp.bfloat16)
    return high, low


def plan(sections, bands, hours_sec, cols, levels, lat_rows, own, probes, weeks, count):
    hours = sections * hours_sec
    halo = -(-hours // WIDE) * WIDE
    window = -(-(own + 2 * hours) // 64) * 64
    d = dict(
        sections=sections, bands=bands, hours_sec=hours_sec, cols=cols, levels=levels,
        lat_rows=lat_rows, own=own, probes=probes, weeks=weeks, count=count, hours=hours,
        halo=halo, left=hours, window=window, lanes=window * probes,
        half=cols // 4, halo_pairs=halo // 2, pairs=(cols + 2 * halo) // 2,
        blocks=(cols + 2 * halo) // WIDE,
    )
    d["stride"] = levels if d["lanes"] == 128 else -(-levels // 8) * 8
    d["block"] = WIDE * d["stride"]
    d["rows"] = PAD + (d["blocks"] + 1) * d["block"]
    d["early"] = hours <= 8 and hours_sec == 2 and sections % 2 == 0
    return d


def fused_kernel(d, winds, mixing, cell, weight, sign, week, *refs):
    sections, bands, hours_sec, hours = d["sections"], d["bands"], d["hours_sec"], d["hours"]
    cols, levels, lat_rows, own = d["cols"], d["levels"], d["lat_rows"], d["own"]
    probes, count, halo, left = d["probes"], d["count"], d["halo"], d["left"]
    window, lanes, half, halo_pairs = d["window"], d["lanes"], d["half"], d["halo_pairs"]
    block, early, stride = d["block"], d["early"], d["stride"]
    if early:
        est, land, refs = refs[0], refs[1], refs[2:]
        stage = None
    else:
        est, land, stage, refs = refs[0], refs[1], refs[2], refs[3:]
    (pack, flat, obs, lhs, pick, state, mixed, inj, ep, wm, npos, sneg, flux,
     out0, in0, lhs0, mixed0, faces0, gs, gr, zs, zr, hs, hr, xs, xr, os, orr, us, ur, local) = refs
    own_pairs = 2 * half
    me = lax.axis_index("tm")
    band = lax.axis_index("lon")
    core = lax.axis_index("probe")
    sides = [lax.rem(band + bands - 1, bands), lax.rem(band + 1, bands)]
    if bands == 2:
        greet = sides[:1]
    else:
        greet = sides

    def remote(src, dst, send, recv, tm, lon, probe):
        return pltpu.make_async_remote_copy(
            src_ref=src, dst_ref=dst, send_sem=send, recv_sem=recv,
            device_id={"tm": tm, "lon": lon, "probe": probe},
            device_id_type=pl.DeviceIdType.MESH,
        )

    if early:
        for t in range(2, hours):
            reach = (t + 1) // 2
            for n in range((halo - t) // WIDE * WIDE // 2, halo_pairs - reach):
                land[t, n] = jnp.zeros(land.shape[2:], land.dtype)
                land[t, 2 * halo_pairs + own_pairs - 1 - n] = jnp.zeros(land.shape[2:], land.dtype)

    barrier = pltpu.get_barrier_semaphore()

    def hello(tm, lon, probe):
        pl.semaphore_signal(
            barrier, inc=1, device_id={"tm": tm, "lon": lon, "probe": probe},
            device_id_type=pl.DeviceIdType.MESH,
        )

    for k in range(1, sections):
        hello(lax.rem(me + k, sections), band, core)
    for lon in greet:
        for q in range(2):
            hello(me, lon, q)
    hello(me, band, 1 - core)

    obs[me, 0, 0:1, :] = cell[...].astype(jnp.float32)
    for p in range(probes):
        obs[me, 0, 1 + p : 2 + p, :] = (2 * sign[p] - 1).astype(jnp.float32) * weight[...]
    lane_row = lax.broadcasted_iota(jnp.int32, (1, count), 1)
    weeks_row = jnp.zeros((1, count), jnp.float32)
    for h in range(hours_sec):
        weeks_row = jnp.where(lane_row == h, week[0:1, h : h + 1].astype(jnp.float32), weeks_row)
    obs[me, 0, 1 + probes : 2 + probes, :] = weeks_row

    if stride != levels:
        flat[...] = jnp.zeros_like(flat)
    wl = 2 * window
    lat_tiles = -(-lat_rows // 128)

    def packed_column(h, column, start, levels=levels):
        tiles = []
        for comp in range(2):
            row = []
            for k in range(lat_tiles):
                x = winds[comp, 0, h, column, 0:levels, k * 128 : min(k * 128 + 128, lat_rows)]
                x = x.astype(jnp.float32)
                if x.shape[1] < 128:
                    x = jnp.concatenate(
                        [x, jnp.zeros((levels, 128 - x.shape[1]), jnp.float32)], axis=1
                    )
                row.append(x)
            tiles.append(row)
        lane = lax.broadcasted_iota(jnp.int32, (levels, 128), 1)
        parts = []
        for v in range(wl // 128):
            out = jnp.zeros((levels, 128), jnp.float32)
            for comp in range(2):
                begin = comp * window - v * 128
                if begin >= 128 or begin + window <= 0:
                    continue
                shift = lax.rem(begin - start + 512, 128)
                at = lane - begin
                row = at + start
                for k in range(lat_tiles):
                    inside = (
                        (at >= 0) & (at < window) & (row >= k * 128)
                        & (row < min(k * 128 + 128, lat_rows))
                    )
                    out = jnp.where(inside, pltpu.roll(tiles[comp][k], shift, 1), out)
            parts.append(out)
        return parts[0] if len(parts) == 1 else jnp.concatenate(parts, axis=1)

    def fill(h, target, first_column, put):
        start = target * own - left

        def body(i, carry):
            for c in range(2):
                at = pl.multiple_of(i * 2 * stride, 8) + c * stride
                flat[pl.ds(at, levels), :] = packed_column(h, first_column + 2 * i + c, start)
            return carry

        lax.fori_loop(0, half, body, 0, unroll=3)

        def cast(i, carry):
            x = flat[pl.ds(pl.multiple_of(i * 2 * stride, 8), 2 * stride), :]
            put(i, x.astype(jnp.bfloat16))
            return carry

        lax.fori_loop(0, half, cast, 0, unroll=3)

    least = jnp.where(me == 0, 1, 0)
    my_pairs = halo_pairs + half * core

    if early:
        parts = [(0, half)]
    else:
        parts = [(0, half)]

    def z_copy(h, target, n):
        t = me * hours_sec + h
        begin, size = parts[n]
        return remote(
            pack.at[h, target, pl.ds(begin, size)], land.at[t, pl.ds(my_pairs + begin, size)],
            zs.at[h, target, n], zr.at[t, n], target, band, core,
        )

    def came(t, n):
        begin, size = parts[n]
        place = land.at[t, pl.ds(my_pairs + begin, size)]
        remote(place, place, zs.at[0, 0, n], zr.at[t, n], me, sides[0], core).wait_recv()

    def start(h, target):
        for n in range(len(parts)):
            z_copy(h, target, n).start()

    def sent(h, target):
        for n in range(len(parts)):
            z_copy(h, target, n).wait_send()

    def job(h, target):
        def put(i, x):
            pack[h, target, i] = x

        fill(h, target, 2 * half * core, put)
        start(h, target)

    def every_job(run):
        def upper(i, carry):
            h = hours_sec - 1 - i

            def target(k, inner):
                run(h, sections - 1 - k)
                return inner

            return lax.fori_loop(0, sections - 1 - me, target, carry)

        lax.fori_loop(0, hours_sec - least, upper, 0)

        def lower(i, carry):
            h = hours_sec - 1 - i

            def target(k, inner):
                run(h, k)
                return inner

            return lax.fori_loop(0, me, target, carry)

        lax.fori_loop(0, hours_sec - least, lower, 0)

    last = hours_sec - 1
    if early:
        half_way = sections // 2
        top = me == sections - 1
        beyond = jnp.where(top, 0, me + 1)

        def put_first(i, x):
            pack[last, beyond, i] = x

        pl.when(me > 0)(lambda: fill(last, beyond, 2 * half * core, put_first))

    pl.semaphore_wait(barrier, sections - 1 + 2 * len(greet) + 1)

    for k in range(1, sections):
        tm = lax.rem(me + k, sections)
        mine = obs.at[me, 0]
        remote(mine, mine, os.at[k], orr.at[me], tm, band, core).start()

    def each(run, h, low, high):
        def body(i, carry):
            run(h, low + i)
            return carry

        lax.fori_loop(0, high - low, body, 0)

    def fill_job(h, target):
        def put(i, x):
            pack[h, target, i] = x

        fill(h, target, 2 * half * core, put)

    if early:
        lower = me < half_way
        upper = (me >= half_way) & (me < sections - 1)
        pl.when(me > 0)(lambda: start(last, beyond))
        many = jnp.where(top, half_way, jnp.where(me > 0, sections, beyond + 1))
        each(job, last, beyond + 1, many)
        each(job, 0, me + 1, jnp.where(me >= half_way, sections, me + 1))

        def rest(run):
            each(run, 0, me + 1, jnp.where(lower & (me > 0), sections, me + 1))
            each(run, last, jnp.where(top, half_way, 0), me)
            each(run, 0, 0, me)

        rest(fill_job)

        @pl.when(lower)
        def _():
            rest(start)

    else:
        every_job(job)

    def second():
        @pl.when(upper)
        def _():
            each(start, last, 0, me)

        @pl.when(top)
        def _():
            each(sent, last, 0, half_way)
            each(start, last, half_way, me)
            each(start, 0, 0, half_way)

    def third():
        @pl.when(upper)
        def _():
            for n in range(len(parts)):
                each(lambda h, target, n=n: z_copy(h, target, n).start(), 0, 0, me)

        @pl.when(top)
        def _():
            each(sent, last, half_way, me)
            each(start, 0, half_way, me)

    def finish_lower():
        @pl.when(lower)
        def _():
            each(sent, last, me + 1, jnp.where(me > 0, sections, me + 1))
            rest(sent)

    def finish_upper():
        @pl.when(upper)
        def _():
            each(sent, last, 0, me)
            each(sent, last, me + 1, sections)
            each(sent, 0, me + 1, sections)
            each(sent, 0, 0, me)

        @pl.when(top)
        def _():
            each(sent, 0, 0, me)

    def out_copy(target):
        return remote(out0.at[target], in0.at[0], gs.at[target], gr.at[0], target, band, core)

    if early:

        @pl.when(me == 0)
        def _():
            def ground_of(target, carry):
                def body(i, inner):
                    x = packed_column(last, i, target * own - left, 16)
                    out0[target, pl.ds(i, 1), :] = x[0:1]
                    return inner

                lax.fori_loop(0, cols, body, 0, unroll=6)
                pl.when(target > 0)(lambda: out_copy(target).start())
                return carry

            lax.fori_loop(0, sections, ground_of, 0)
            in0[0] = out0[0]

    def at_home(i, carry):
        h = hours_sec - 1 - i
        t = me * hours_sec + h
        for c in range(2):
            if early:

                def put(i, x):
                    land[t, halo_pairs + half * c + i] = x

                fill(h, me, 2 * half * c, put)
            else:

                def put(i, x):
                    pack[h, me, i] = x

                fill(h, me, 2 * half * c, put)
                copy = pltpu.make_async_copy(
                    pack.at[h, me], land.at[t, pl.ds(halo_pairs + half * c, half)], local.at[0]
                )
                copy.start()
                copy.wait()
        return carry

    home = jnp.where(me == 0, hours_sec, 0) if early else least
    lax.fori_loop(0, hours_sec - home, at_home, 0)

    zero = jnp.zeros((PAD, lanes), jnp.float32)

    def clear(i, carry):
        at = pl.multiple_of(i * 8, 8)
        state[pl.ds(at, 8), :] = zero[:8]
        mixed[pl.ds(at, 8), :] = zero[:8]
        inj[0, pl.ds(at, 8), :] = zero[:8]
        return carry

    lax.fori_loop(0, d["rows"] // 8, clear, 0, unroll=8)
    flux[...] = jnp.zeros_like(flux)
    lhs[...] = jnp.zeros_like(lhs)
    lhs[0:levels, 0:levels] = mixing[...]
    turned_mix = jnp.transpose(lhs[:, 0:128])
    both = turned_mix + pltpu.roll(pltpu.roll(turned_mix, stride, 0), stride, 1)
    high = both.astype(jnp.bfloat16).astype(jnp.float32)
    low = both - high
    none = jnp.zeros_like(both)
    high = jnp.concatenate([high, none], axis=1)
    low = jnp.concatenate([low, none], axis=1)
    deep = 2 * stride
    matrix = high + pltpu.roll(low, deep, 1) + pltpu.roll(high, 2 * deep, 1)
    lhs[...] = matrix
    lhs0[...] = jnp.zeros_like(lhs0)
    for k in range(2):
        lhs0[k : k + 1, :] = matrix[k * stride : k * stride + 1]

    source = lax.broadcasted_iota(jnp.int32, (wl, lanes), 0)
    into = lax.rem(lax.broadcasted_iota(jnp.int32, (wl, lanes), 1), window)
    first_row = me * own - left
    keep = (into + first_row >= 0) & (into + first_row < lat_rows - 1)
    below = (into > 0) & (into + first_row >= 1) & (into + first_row < lat_rows)
    pick[:, :lanes] = jnp.where(source == into, 1.0, 0.0)
    pick[:, lanes : 2 * lanes] = jnp.where((source == into + window) & keep, 1.0, 0.0)
    pick[:, 2 * lanes :] = jnp.where((source == into + window - 1) & below, 1.0, 0.0)

    def obs_copy(s, n):
        return remote(
            obs.at[s, 0], obs.at[s, 1 + n], us.at[s, n], ur.at[s, n], me, sides[1 - n], core
        )

    beside = range(1 if bands == 2 else 2)

    def hand_obs(s):
        @pl.when(me != s)
        def _():
            remote(obs.at[s, 0], obs.at[s, 0], os.at[0], orr.at[s], me, sides[0], core).wait_recv()

        @pl.when(s > 0)
        def _():
            for n in beside:
                obs_copy(s, n).start()

    def half_copy(t):
        place = land.at[t, pl.ds(my_pairs, half)]
        return remote(place, place, hs.at[t], hr.at[t], me, band, 1 - core)

    def edges(depth):
        found = []
        for side in range(2):
            begin = 0 if side == 0 else own_pairs - depth
            for c in range(2):
                a, b = max(begin, half * c), min(begin + depth, half * (c + 1))
                if a < b:
                    found.append((side, c, a, b))
        return found

    def edge_copy(t, side, c, a, b, q):
        to = halo_pairs + (own_pairs if side == 0 else -own_pairs)
        return remote(
            land.at[t, pl.ds(halo_pairs + a, b - a)], land.at[t, pl.ds(to + a, b - a)],
            xs.at[t, side, q], xr.at[t, side, c], me, sides[side], q,
        )

    def with_depth(t, act):
        if early:
            for depth in range(1, halo_pairs + 1):

                @pl.when((t + 1) // 2 == depth)
                def _():
                    act(depth)

        else:

            @pl.when(t > halo // 2)
            def _():
                act(halo_pairs)

            @pl.when(t <= halo // 2)
            def _():
                act(halo_pairs // 2)

    def hand_winds(t):
        s = t // hours_sec

        pl.when(me != s)(lambda: came(t, 0))

        def act(depth):
            for c in range(2):

                @pl.when(core == c)
                def _():
                    for side, sender, a, b in edges(depth):
                        if sender == c:
                            for q in range(2):
                                edge_copy(t, side, sender, a, b, q).start()

        with_depth(t, act)

        @pl.when(me != s)
        def _():
            half_copy(t).start()

    def take_winds(t):
        s = t // hours_sec

        @pl.when(me != s)
        def _():
            place = land.at[t, pl.ds(halo_pairs + half * (1 - core), half)]
            remote(place, place, hs.at[t], hr.at[t], me, band, 1 - core).wait_recv()

        def act(depth):
            for side, sender, a, b in edges(depth):
                edge_copy(t, side, sender, a, b, 0).wait_recv()

        with_depth(t, act)

    first_row = me * own - left

    def observed(s, piece):
        place = obs[s, piece, 0:1, :].astype(jnp.int32)
        level = place // (cols * lat_rows)
        rest = place - level * (cols * lat_rows)
        column = rest // lat_rows
        row = rest - column * lat_rows - first_row
        hit = lax.broadcasted_iota(jnp.int32, (window, count), 0) == row
        parts = [
            split2(jnp.where(hit, obs[s, piece, 1 + p : 2 + p, :], 0.0)) for p in range(probes)
        ]
        rhs = jnp.concatenate([x[0] for x in parts] + [x[1] for x in parts], axis=0)
        return level, column, rhs

    def placed_sum(hot, rhs):
        got = lax.dot_general(
            hot.astype(jnp.float32).astype(jnp.bfloat16), rhs, (((1,), (1,)), ((), ())),
            preferred_element_type=jnp.float32,
        )
        return got[:, :lanes] + got[:, lanes:]

    def lowest(t):
        return (halo - t) // WIDE

    def highest(t):
        return (halo + cols + t + WIDE - 1) // WIDE

    edge_blocks = halo // WIDE
    own_blocks = cols // WIDE
    together = max(n for n in range(1, 4) if own_blocks % n == 0)

    def inject(s, slot):
        t = s * hours_sec
        for n in beside:
            remote(
                obs.at[s, 0], obs.at[s, 1 + n], us.at[s, n], ur.at[s, n], me, sides[0], core
            ).wait_recv()
        if early:
            lo, hi = lowest(t), highest(t)
            ranges = [
                (0, [(halo, edge_blocks, edge_blocks + own_blocks)]),
                (1, [(halo - cols, lo, edge_blocks)]),
                (2 if bands > 2 else 1, [(halo + cols, edge_blocks + own_blocks, hi)]),
            ]
            if bands == 2:
                ranges = [ranges[0], (1, ranges[1][1] + ranges[2][1])]
            for piece, places in ranges:
                level, column, rhs = observed(s, piece)
                hots = []
                for shift, begin, end in places:
                    place = (column + shift) * stride + level - begin * block
                    chunk = lax.broadcasted_iota(jnp.int32, ((end - begin) * block, count), 0)
                    hots.append((chunk == place).astype(jnp.float32).astype(jnp.bfloat16))
                hot = hots[0] if len(hots) == 1 else jnp.concatenate(hots, axis=0)
                got = lax.dot_general(
                    hot, rhs, (((1,), (1,)), ((), ())), preferred_element_type=jnp.float32
                )
                add = got[:, :lanes] + got[:, lanes:]
                done = 0
                for shift, begin, end in places:
                    size = (end - begin) * block
                    inj[slot, pl.ds(PAD + begin * block, size), :] = add[done : done + size]
                    done += size
            return
        for piece, shift, begin, end, step in (
            (0, halo, edge_blocks, edge_blocks + own_blocks, together),
            (1, halo - cols, lowest(t), edge_blocks, 1),
            (2 if bands > 2 else 1, halo + cols, edge_blocks + own_blocks, highest(t), 1),
        ):
            level, column, rhs = observed(s, piece)
            place = (column + shift) * stride + level
            high_rows = step * block
            chunk = lax.broadcasted_iota(jnp.int32, (high_rows, count), 0)

            def body(i, carry, begin=begin, step=step, place=place, rhs=rhs, chunk=chunk, high_rows=high_rows):
                b = begin + i * step
                add = placed_sum(chunk == place - b * block, rhs)
                inj[slot, pl.ds(pl.multiple_of(PAD + b * block, 8), high_rows), :] = add
                return carry

            lax.fori_loop(0, (end - begin) // step, body, 0)

    def ground(field=state):
        start = PAD + halo * stride
        if lanes == 128:
            return field[pl.ds(start, cols, stride=stride), :]
        rows = [state[start + c * stride : start + c * stride + 1, :] for c in range(cols)]
        return jnp.concatenate(rows, axis=0)

    def add_flux(s, h, x):
        which = obs[s, 0, 1 + probes : 2 + probes, 0:128]
        lane = lax.broadcasted_iota(jnp.int32, (1, 128), 1)
        number = jnp.sum(jnp.where(lane == h, which, 0.0), axis=1, keepdims=True)
        for w in range(d["weeks"]):
            flux[w] += jnp.where(number == w, x, 0.0)

    def surface(s, slot):
        level, column, rhs = observed(0, 0)
        tall = -(-cols // 8) * 8
        chunk = lax.broadcasted_iota(jnp.int32, (tall, count), 0)
        add = placed_sum(chunk == jnp.where(level == 0, column, -1), rhs)
        add_flux(0, 0, add[:cols])

    middle = hours // 2

    def slot_of(t):
        return t if early else 0

    def prepare(t, span=None):
        slot = slot_of(t)
        if not early:
            copy = pltpu.make_async_copy(land.at[t], stage, local.at[0])
            copy.start()
            copy.wait()
        lo, hi = lowest(t), highest(t)
        wm[slot, pl.ds(pl.multiple_of(PAD + lo * block, 8), PAD), :] = jnp.zeros((PAD, lanes), jnp.float32)
        matrix = pick[...].astype(jnp.bfloat16)

        def spread(b, n):
            base = pl.multiple_of(PAD + b * block, 8)
            at = pl.ds(b * WIDE // 2, n * WIDE // 2)
            packed = land[t, at] if early else stage[at]
            packed = packed.reshape(n * block, wl)
            got = jnp.dot(packed, matrix, preferred_element_type=jnp.float32)
            east, north, south = got[:, :lanes], got[:, lanes : 2 * lanes], got[:, 2 * lanes :]
            ep[slot, pl.ds(base, n * block), :] = jnp.maximum(east, 0.0)
            wm[slot, pl.ds(base + stride, n * block), :] = jnp.minimum(east, 0.0)
            npos[slot, pl.ds(base, n * block), :] = jnp.maximum(north, 0.0)
            sneg[slot, pl.ds(base, n * block), :] = jnp.minimum(south, 0.0)

        def one(b, carry):
            spread(b, 1)
            return carry

        def many(i, carry):
            spread(edge_blocks + i * together, together)
            return carry

        if span is not None:
            b = span[0]
            while b < span[1]:
                n = min(3, span[1] - b)
                spread(b, n)
                b += n
            return
        lax.fori_loop(lo, edge_blocks, one, 0)
        lax.fori_loop(0, own_blocks // together, many, 0)
        lax.fori_loop(edge_blocks + own_blocks, hi, one, 0)

    def advance(t, slot, span=None):
        s = t // hours_sec
        h = t - s * hours_sec
        lo, hi = lowest(t), highest(t)

        if span is not None:
            slot = jnp.where(h == 0, s, 0)
        else:

            @pl.when(h == 0)
            def _():
                def body(b, carry):
                    at = pl.ds(pl.multiple_of(PAD + b * block, 8), block)
                    state[at, :] += inj[slot, at, :]
                    return carry

                lax.fori_loop(lo, hi, body, 0)

        add_flux(s, h, ground() if span is None else ground() + ground(inj.at[slot]))
        mix = lhs[0:deep, 0 : 3 * deep].astype(jnp.bfloat16)
        where = slot_of(t)

        def at_block(b):
            return PAD + b * block if span is not None else pl.multiple_of(PAD + b * block, 8)

        def mixing_of(b):
            base = at_block(b)
            parts = [state[pl.ds(base + k * deep, deep), :] for k in range(2)]
            if span is not None:
                parts = [x + inj[slot, pl.ds(base + k * deep, deep), :] for k, x in enumerate(parts)]
            x = jnp.concatenate(parts, axis=1)
            low = x - x.astype(jnp.bfloat16).astype(jnp.float32)
            stack = jnp.concatenate([x, x, low], axis=0).astype(jnp.bfloat16)
            return jnp.dot(mix, stack, preferred_element_type=jnp.float32)

        def keep_mixed(b, got):
            base = at_block(b)
            mixed[pl.ds(base, deep), :] = got[:, :lanes]
            mixed[pl.ds(base + deep, deep), :] = got[:, lanes:]

        def advect(b):
            base = at_block(b)
            at = pl.ds(base, block)
            here = mixed[at, :]
            after = mixed[pl.ds(base + stride, block), :]
            before = mixed[pl.ds(base - stride, block), :]
            g = here + ep[where, at, :] * (after - here) + wm[where, at, :] * (here - before)
            above = pltpu.roll(g, lanes - 1, 1)
            below = pltpu.roll(g, 1, 1)
            return g + npos[where, at, :] * (above - g) + sneg[where, at, :] * (g - below)

        def keep_state(b, x):
            state[pl.ds(at_block(b), block), :] = x

        def only_mix(b, carry):
            keep_mixed(b, mixing_of(b))
            return carry

        def both(b, carry):
            got = mixing_of(b)
            new = advect(b - 2)
            keep_state(b - 2, new)
            keep_mixed(b, got)
            return carry

        def only_advect(b, carry):
            keep_state(b, advect(b))
            return carry

        if span is not None:
            for b in range(span[0], span[1] + 2):
                got = mixing_of(b) if b < span[1] else None
                if b >= span[0] + 2:
                    keep_state(b - 2, advect(b - 2))
                if b < span[1]:
                    keep_mixed(b, got)
            return
        lax.fori_loop(lo, lo + 2, only_mix, 0)
        lax.fori_loop(lo + 2, hi, both, 0)
        lax.fori_loop(hi - 2, hi, only_advect, 0)

    def ground_copy():
        return remote(in0.at[0], in0.at[1], gs.at[0], gr.at[1], me, sides[1], core)

    def hand_ground():
        @pl.when(me > 0)
        def _():
            remote(in0.at[0], in0.at[0], gs.at[0], gr.at[0], me, sides[0], core).wait_recv()

        ground_copy().start()

    def prepare_ground():
        remote(in0.at[1], in0.at[1], gs.at[0], gr.at[1], me, sides[0], core).wait_recv()
        matrix = pick[...].astype(jnp.bfloat16)
        got = jnp.dot(in0[0].astype(jnp.bfloat16), matrix, preferred_element_type=jnp.float32)
        west = jnp.dot(
            in0[1].astype(jnp.bfloat16), matrix[:, :lanes], preferred_element_type=jnp.float32
        )
        east, north, south = got[:, :lanes], got[:, lanes : 2 * lanes], got[:, 2 * lanes :]
        faces0[0, 0:cols, :] = jnp.maximum(east, 0.0)
        faces0[1, 1 : cols + 1, :] = jnp.minimum(east, 0.0)
        faces0[1, 0:1, :] = jnp.minimum(west[cols - 1 : cols], 0.0)
        faces0[2, 0:cols, :] = jnp.maximum(north, 0.0)
        faces0[3, 0:cols, :] = jnp.minimum(south, 0.0)

    def last_step(span):
        add_flux(0, 1, ground())
        mix = lhs0[:, 0 : 3 * deep].astype(jnp.bfloat16)
        for b in range(*span):
            base = PAD + b * block
            x = jnp.concatenate([state[pl.ds(base + k * deep, deep), :] for k in range(2)], axis=1)
            low = x - x.astype(jnp.bfloat16).astype(jnp.float32)
            stack = jnp.concatenate([x, x, low], axis=0).astype(jnp.bfloat16)
            got = jnp.dot(mix, stack, preferred_element_type=jnp.float32)
            mixed0[b * WIDE : b * WIDE + 2, :] = got[0:2, :lanes]
            mixed0[b * WIDE + 2 : b * WIDE + 4, :] = got[0:2, lanes:]
        here = mixed0[halo : halo + cols, :]
        after = mixed0[halo + 1 : halo + cols + 1, :]
        before = mixed0[halo - 1 : halo + cols - 1, :]
        faces = [faces0[k, 0:cols, :] for k in range(4)]
        g = here + faces[0] * (after - here) + faces[1] * (here - before)
        above = pltpu.roll(g, lanes - 1, 1)
        below = pltpu.roll(g, 1, 1)
        add_flux(0, 0, g + faces[2] * (above - g) + faces[3] * (g - below))

    def finish_obs():
        for k in range(1, sections):
            mine = obs.at[me, 0]
            remote(mine, mine, os.at[k], orr.at[me], me, sides[0], core).wait_send()

        def sent_obs(s):
            for n in beside:
                obs_copy(s, n).wait_send()

        loop(sections - 1, 1, sent_obs)
        if early:
            ground_copy().wait_send()

            @pl.when(me == 0)
            def _():
                for target in range(1, sections):
                    out_copy(target).wait_send()

    def sent_winds(t):
        @pl.when(me != t // hours_sec)
        def _():
            half_copy(t).wait_send()

        def act(depth):
            for c in range(2):

                @pl.when(core == c)
                def _():
                    for side, sender, a, b in edges(depth):
                        if sender == c:
                            for q in range(2):
                                edge_copy(t, side, sender, a, b, q).wait_send()

        with_depth(t, act)

    def loop(high, low, run):
        def body(i, carry):
            run(high - i)
            return carry

        lax.fori_loop(0, high - low + 1, body, 0)

    if early:

        loop(hours_sec - 1, home, lambda h: hand_winds(me * hours_sec + h))
        hand_obs(sections - 1)
        second()
        for s in range(sections - 1, 0, -1):
            hand_obs(s - 1)
            inject(s, s)
        surface(0, 0)
        third()
        far = (lowest(hours - 1), highest(hours - 1))
        near = (lowest(middle), highest(middle))

        code = 0
        for z in range(sections):
            mine = [t for t in range(hours - 1, 1, -1) if t // hours_sec == z]
            low_hours = [t for t in range(middle - 1, 1, -1) if t not in mine]
            high_hours = [t for t in range(hours - 1, middle - 1, -1) if t not in mine]
            if z < half_way:
                high_hours.sort(key=lambda t: (-(t % hours_sec), -t))
                order = mine + low_hours + high_hours
            else:
                order = mine + high_hours + low_hours
            code = jnp.where(me == z, sum(t * hours**k for k, t in enumerate(order)), code)

        def ready(i, code):
            t = lax.rem(code, hours)
            code = code // hours
            after = lax.rem(code, hours)
            pl.when(me != after // hours_sec)(lambda: hand_winds(after))
            take_winds(t)
            pl.when(t >= middle + 1)(lambda: prepare(t, far))
            pl.when(t <= middle)(lambda: prepare(t, near))
            sent_winds(t)
            return code

        foremost = lax.rem(code, hours)
        pl.when(me != foremost // hours_sec)(lambda: hand_winds(foremost))
        final = lax.fori_loop(0, hours - 3, ready, code)
        hand_ground()
        loop(hours - 1, middle + 1, lambda t: advance(t, 0, far))
        prepare_ground()
        take_winds(final)
        prepare(final, near)
        loop(middle, 2, lambda t: advance(t, 0, near))
        last_step(near)
    else:
        loop(sections - 1, 0, hand_obs)
        surface(0, 0)

        def whole(t):
            s = t // hours_sec

            @pl.when(t == s * hours_sec)
            def _():
                inject(s, 0)

            hand_winds(t)
            take_winds(t)
            prepare(t)
            advance(t, 0)

        loop(hours - 1, 1, whole)

    if not early:
        add_flux(0, 0, ground())
    for w in range(d["weeks"]):
        square = flux[w] * flux[w]
        est[w] = (square + pltpu.roll(square, lanes - window, 1)) * 0.5

    if early:
        finish_lower()
        finish_upper()
        finish_obs()
        sent_winds(final)
    else:
        every_job(sent)
        finish_obs()
        loop(hours - 1, 1, sent_winds)


def on_device(winds, mixing, obs_cell, obs_weight, probe_sign, week_map, prior_precision):
    week_count, _, own = prior_precision.shape
    d = plan(
        lax.axis_size("tm"), lax.axis_size("lon"), winds.shape[2], winds.shape[4], winds.shape[3],
        winds.shape[5], own, probe_sign.shape[0], week_count, obs_cell.shape[2],
    )
    sections, hours, hours_sec = d["sections"], d["hours"], d["hours_sec"]
    lanes, rows, cols, left = d["lanes"], d["rows"], d["cols"], d["left"]
    early = d["early"]
    wire = (d["half"], 2 * d["stride"], 2 * d["window"])
    landing = (hours, d["pairs"]) + wire[1:]
    slots = hours if early else 1
    inj_slots = sections if early else 1
    sem = pltpu.SemaphoreType.DMA
    scratch = [
        pltpu.VMEM((hours_sec, sections) + wire, jnp.bfloat16),
        pltpu.VMEM((2 * d["half"] * d["stride"], 2 * d["window"]), jnp.float32),
        pltpu.VMEM((sections, 3, 2 + d["probes"], d["count"]), jnp.float32),
        pltpu.VMEM((128, 256), jnp.float32),
        pltpu.VMEM((2 * d["window"], 3 * lanes), jnp.float32),
        pltpu.VMEM((rows, lanes), jnp.float32),
        pltpu.VMEM((rows, lanes), jnp.float32),
        pltpu.VMEM((inj_slots, rows, lanes), jnp.float32),
    ] + [pltpu.VMEM((slots, rows, lanes), jnp.float32)] * 4 + [
        pltpu.VMEM((week_count, cols, lanes), jnp.float32),
        pltpu.VMEM((sections, cols, 2 * d["window"]), jnp.float32),
        pltpu.VMEM((2, cols, 2 * d["window"]), jnp.float32),
        pltpu.VMEM((8, 256), jnp.float32),
        pltpu.VMEM((d["blocks"] * WIDE, lanes), jnp.float32),
        pltpu.VMEM((4, cols + 4, lanes), jnp.float32),
        sem((sections + 1,)), sem((2,)),
        sem((hours_sec, sections, 2)), sem((hours, 2)), sem((hours,)), sem((hours,)),
        sem((hours, 2, 2)), sem((hours, 2, 2)), sem((sections,)), sem((sections,)),
        sem((sections, 2)), sem((sections, 2)), sem((1,)),
    ]
    outs = [jax.ShapeDtypeStruct((week_count, cols, lanes), jnp.float32)]
    out_specs = [pl.BlockSpec(memory_space=pltpu.VMEM)]
    if early:
        scratch = [pltpu.VMEM(landing, jnp.bfloat16)] + scratch
    else:
        outs.append(jax.ShapeDtypeStruct(landing, jnp.bfloat16))
        out_specs.append(pl.BlockSpec(memory_space=pl.ANY))
        scratch = [pltpu.VMEM(landing[1:], jnp.bfloat16)] + scratch
    got = pl.pallas_call(
        functools.partial(fused_kernel, d),
        out_shape=tuple(outs),
        in_specs=[pl.BlockSpec(memory_space=pltpu.VMEM)] * 6,
        out_specs=tuple(out_specs),
        scratch_shapes=scratch,
        compiler_params=pltpu.CompilerParams(
            collective_id=0, has_side_effects=True, vmem_limit_bytes=(51 if early else 56) << 20
        ),
    )(
        winds.transpose(0, 1, 2, 4, 3, 5), mixing, obs_cell[0], obs_weight[0],
        probe_sign[:, 0], week_map,
    )
    return (prior_precision + got[0][..., left : left + own])[None]


def solution(mesh):
    placed = (
        P(None, ("groups", "tm"), None, None, "lon", None),
        P(),
        P(("groups", "tm"), "lon", None),
        P(("groups", "tm"), "lon", None),
        P("probe", ("groups", "tm"), "lon", None),
        P(("groups", "tm"), None),
        P("groups", "lon", "tm"),
    )
    return jax.shard_map(
        on_device,
        mesh=mesh,
        in_specs=placed,
        out_specs=P("probe", "groups", "lon", "tm"),
        check_vma=False,
    )
```

```python
import functools

import jax
import jax.numpy as jnp
from jax import lax
from jax.experimental import pallas as pl
from jax.experimental.pallas import tpu as pltpu
from jax.sharding import PartitionSpec as P

WIDE = 4
PAD = 40


def split2(x):
    high = x.astype(jnp.bfloat16)
    low = (x - high.astype(jnp.float32)).astype(jnp.bfloat16)
    return high, low


def plan(sections, bands, hours_sec, cols, levels, lat_rows, own, probes, weeks, count):
    hours = sections * hours_sec
    halo = -(-hours // WIDE) * WIDE
    window = -(-(own + 2 * hours) // 64) * 64
    d = dict(
        sections=sections, bands=bands, hours_sec=hours_sec, cols=cols, levels=levels,
        lat_rows=lat_rows, own=own, probes=probes, weeks=weeks, count=count, hours=hours,
        halo=halo, left=hours, window=window, lanes=window * probes,
        half=cols // 4, halo_pairs=halo // 2, pairs=(cols + 2 * halo) // 2,
        blocks=(cols + 2 * halo) // WIDE,
    )
    d["stride"] = levels if d["lanes"] == 128 else -(-levels // 8) * 8
    d["block"] = WIDE * d["stride"]
    d["rows"] = PAD + (d["blocks"] + 1) * d["block"]
    d["early"] = hours <= 8 and hours_sec == 2 and sections % 2 == 0
    return d


def fused_kernel(d, winds, mixing, cell, weight, sign, week, *refs):
    sections, bands, hours_sec, hours = d["sections"], d["bands"], d["hours_sec"], d["hours"]
    cols, levels, lat_rows, own = d["cols"], d["levels"], d["lat_rows"], d["own"]
    probes, count, halo, left = d["probes"], d["count"], d["halo"], d["left"]
    window, lanes, half, halo_pairs = d["window"], d["lanes"], d["half"], d["halo_pairs"]
    block, early, stride = d["block"], d["early"], d["stride"]
    if early:
        est, land, refs = refs[0], refs[1], refs[2:]
        stage = None
    else:
        est, land, stage, refs = refs[0], refs[1], refs[2], refs[3:]
    (pack, flat, obs, lhs, pick, state, mixed, inj, ep, wm, npos, sneg, flux,
     out0, in0, lhs0, mixed0, faces0, gs, gr, zs, zr, hs, hr, xs, xr, os, orr, us, ur, local) = refs
    own_pairs = 2 * half
    me = lax.axis_index("tm")
    band = lax.axis_index("lon")
    core = lax.axis_index("probe")
    sides = [lax.rem(band + bands - 1, bands), lax.rem(band + 1, bands)]
    if bands == 2:
        greet = sides[:1]
    else:
        greet = sides

    def remote(src, dst, send, recv, tm, lon, probe):
        return pltpu.make_async_remote_copy(
            src_ref=src, dst_ref=dst, send_sem=send, recv_sem=recv,
            device_id={"tm": tm, "lon": lon, "probe": probe},
            device_id_type=pl.DeviceIdType.MESH,
        )

    if early:
        for t in range(2, hours):
            reach = (t + 1) // 2
            for n in range((halo - t) // WIDE * WIDE // 2, halo_pairs - reach):
                land[t, n] = jnp.zeros(land.shape[2:], land.dtype)
                land[t, 2 * halo_pairs + own_pairs - 1 - n] = jnp.zeros(land.shape[2:], land.dtype)

    barrier = pltpu.get_barrier_semaphore()

    def hello(tm, lon, probe):
        pl.semaphore_signal(
            barrier, inc=1, device_id={"tm": tm, "lon": lon, "probe": probe},
            device_id_type=pl.DeviceIdType.MESH,
        )

    for k in range(1, sections):
        hello(lax.rem(me + k, sections), band, core)
    for lon in greet:
        for q in range(2):
            hello(me, lon, q)
    hello(me, band, 1 - core)

    obs[me, 0, 0, :, 0:count] = cell[...].astype(jnp.float32)
    for p in range(probes):
        obs[me, 0, 1 + p, :, 0:count] = (2 * sign[p] - 1).astype(jnp.float32) * weight[...]
        obs[me, 0, 1 + p, :, count:] = jnp.zeros((1, 128), jnp.float32)
    lane_row = lax.broadcasted_iota(jnp.int32, (1, 128), 1)
    weeks_row = jnp.zeros((1, 128), jnp.float32)
    for h in range(hours_sec):
        weeks_row = jnp.where(lane_row == h, week[0:1, h : h + 1].astype(jnp.float32), weeks_row)
    obs[me, 0, 0, :, count:] = weeks_row

    if stride != levels:
        flat[...] = jnp.zeros_like(flat)
    wl = 2 * window
    lat_tiles = -(-lat_rows // 128)

    def packed_column(h, column, start, levels=levels):
        tiles = []
        for comp in range(2):
            row = []
            for k in range(lat_tiles):
                x = winds[comp, 0, h, column, 0:levels, k * 128 : min(k * 128 + 128, lat_rows)]
                x = x.astype(jnp.float32)
                if x.shape[1] < 128:
                    x = jnp.concatenate(
                        [x, jnp.zeros((levels, 128 - x.shape[1]), jnp.float32)], axis=1
                    )
                row.append(x)
            tiles.append(row)
        lane = lax.broadcasted_iota(jnp.int32, (levels, 128), 1)
        parts = []
        for v in range(wl // 128):
            out = jnp.zeros((levels, 128), jnp.float32)
            for comp in range(2):
                begin = comp * window - v * 128
                if begin >= 128 or begin + window <= 0:
                    continue
                shift = lax.rem(begin - start + 512, 128)
                at = lane - begin
                row = at + start
                for k in range(lat_tiles):
                    inside = (
                        (at >= 0) & (at < window) & (row >= k * 128)
                        & (row < min(k * 128 + 128, lat_rows))
                    )
                    out = jnp.where(inside, pltpu.roll(tiles[comp][k], shift, 1), out)
            parts.append(out)
        return parts[0] if len(parts) == 1 else jnp.concatenate(parts, axis=1)

    def fill(h, target, first_column, put):
        start = target * own - left

        def body(i, carry):
            for c in range(2):
                at = pl.multiple_of(i * 2 * stride, 8) + c * stride
                flat[pl.ds(at, levels), :] = packed_column(h, first_column + 2 * i + c, start)
            return carry

        lax.fori_loop(0, half, body, 0, unroll=3)

        def cast(i, carry):
            x = flat[pl.ds(pl.multiple_of(i * 2 * stride, 8), 2 * stride), :]
            put(i, x.astype(jnp.bfloat16))
            return carry

        lax.fori_loop(0, half, cast, 0, unroll=3)

    least = jnp.where(me == 0, 1, 0)
    my_pairs = halo_pairs + half * core

    if early:
        parts = [((half - halo_pairs) * core, halo_pairs), (halo_pairs * (1 - core), half - halo_pairs)]
    else:
        parts = [(0, half)]

    def z_copy(h, target, n):
        t = me * hours_sec + h
        begin, size = parts[n]
        return remote(
            pack.at[h, target, pl.ds(begin, size)], land.at[t, pl.ds(my_pairs + begin, size)],
            zs.at[h, target, n], zr.at[t, n], target, band, core,
        )

    def came(t, n):
        begin, size = parts[n]
        place = land.at[t, pl.ds(my_pairs + begin, size)]
        remote(place, place, zs.at[0, 0, n], zr.at[t, n], me, sides[0], core).wait_recv()

    def start(h, target):
        for n in range(len(parts)):
            z_copy(h, target, n).start()

    def sent(h, target):
        for n in range(len(parts)):
            z_copy(h, target, n).wait_send()

    def job(h, target):
        def put(i, x):
            pack[h, target, i] = x

        fill(h, target, 2 * half * core, put)
        start(h, target)

    def every_job(run):
        def upper(i, carry):
            h = hours_sec - 1 - i

            def target(k, inner):
                run(h, sections - 1 - k)
                return inner

            return lax.fori_loop(0, sections - 1 - me, target, carry)

        lax.fori_loop(0, hours_sec - least, upper, 0)

        def lower(i, carry):
            h = hours_sec - 1 - i

            def target(k, inner):
                run(h, k)
                return inner

            return lax.fori_loop(0, me, target, carry)

        lax.fori_loop(0, hours_sec - least, lower, 0)

    last = hours_sec - 1
    if early:
        half_way = sections // 2
        top = me == sections - 1
        beyond = jnp.where(top, 0, me + 1)

        def put_first(i, x):
            pack[last, beyond, i] = x

        pl.when(me > 0)(lambda: fill(last, beyond, 2 * half * core, put_first))

    pl.semaphore_wait(barrier, sections - 1 + 2 * len(greet) + 1)

    def obs_send(s, tm):
        mine = obs.at[s, 0]
        return remote(mine, mine, os.at[s, tm], orr.at[s], tm, band, core)

    def obs_targets(act):
        for k in range(1, sections):
            act(me, lax.rem(me + k, sections))

    obs_targets(lambda s, tm: obs_send(s, tm).start())

    def each(run, h, low, high):
        def body(i, carry):
            run(h, low + i)
            return carry

        lax.fori_loop(0, high - low, body, 0)

    def fill_job(h, target):
        def put(i, x):
            pack[h, target, i] = x

        fill(h, target, 2 * half * core, put)

    if early:
        lower = me < half_way
        upper = (me >= half_way) & (me < sections - 1)
        pl.when(me > 0)(lambda: start(last, beyond))
        many = jnp.where(top, half_way, jnp.where(me > 0, sections, beyond + 1))
        each(job, last, beyond + 1, many)
        each(job, 0, me + 1, jnp.where(me >= half_way, sections, me + 1))

        def rest(run):
            each(run, 0, me + 1, jnp.where(lower & (me > 0), sections, me + 1))
            each(run, last, jnp.where(top, half_way, 0), me)
            each(run, 0, 0, me)

        rest(fill_job)

        @pl.when(lower)
        def _():
            rest(start)

    else:
        every_job(job)

    def second():
        @pl.when(upper)
        def _():
            each(start, last, 0, me)

        @pl.when(top)
        def _():
            each(sent, last, 0, half_way)
            each(start, last, half_way, me)
            each(start, 0, 0, half_way)

    def third():
        @pl.when(upper)
        def _():
            for n in range(len(parts)):
                each(lambda h, target, n=n: z_copy(h, target, n).start(), 0, 0, me)

        @pl.when(top)
        def _():
            each(sent, last, half_way, me)
            each(start, 0, half_way, me)

    def finish_lower():
        @pl.when(lower)
        def _():
            each(sent, last, me + 1, jnp.where(me > 0, sections, me + 1))
            rest(sent)

    def finish_upper():
        @pl.when(upper)
        def _():
            each(sent, last, 0, me)
            each(sent, last, me + 1, sections)
            each(sent, 0, me + 1, sections)
            each(sent, 0, 0, me)

        @pl.when(top)
        def _():
            each(sent, 0, 0, me)

    def out_copy(target):
        return remote(out0.at[target], in0.at[0], gs.at[target], gr.at[0], target, band, core)

    if early:

        @pl.when(me == 0)
        def _():
            def ground_of(target, carry):
                def body(i, inner):
                    x = packed_column(last, i, target * own - left, 16)
                    out0[target, pl.ds(i, 1), :] = x[0:1]
                    return inner

                lax.fori_loop(0, cols, body, 0, unroll=6)
                pl.when(target > 0)(lambda: out_copy(target).start())
                return carry

            lax.fori_loop(0, sections, ground_of, 0)
            in0[0] = out0[0]

    def at_home(i, carry):
        h = hours_sec - 1 - i
        t = me * hours_sec + h
        for c in range(2):
            if early:

                def put(i, x):
                    land[t, halo_pairs + half * c + i] = x

                fill(h, me, 2 * half * c, put)
            else:

                def put(i, x):
                    pack[h, me, i] = x

                fill(h, me, 2 * half * c, put)
                copy = pltpu.make_async_copy(
                    pack.at[h, me], land.at[t, pl.ds(halo_pairs + half * c, half)], local.at[0]
                )
                copy.start()
                copy.wait()
        return carry

    home = jnp.where(me == 0, hours_sec, 0) if early else least
    lax.fori_loop(0, hours_sec - home, at_home, 0)

    zero = jnp.zeros((PAD, lanes), jnp.float32)

    def clear(i, carry):
        at = pl.multiple_of(i * 8, 8)
        state[pl.ds(at, 8), :] = zero[:8]
        mixed[pl.ds(at, 8), :] = zero[:8]
        inj[0, pl.ds(at, 8), :] = zero[:8]
        return carry

    lax.fori_loop(0, d["rows"] // 8, clear, 0, unroll=8)
    flux[...] = jnp.zeros_like(flux)
    lhs[...] = jnp.zeros_like(lhs)
    lhs[0:levels, 0:levels] = mixing[...]
    turned_mix = jnp.transpose(lhs[:, 0:128])
    both = turned_mix + pltpu.roll(pltpu.roll(turned_mix, stride, 0), stride, 1)
    high = both.astype(jnp.bfloat16).astype(jnp.float32)
    low = both - high
    none = jnp.zeros_like(both)
    high = jnp.concatenate([high, none], axis=1)
    low = jnp.concatenate([low, none], axis=1)
    deep = 2 * stride
    matrix = high + pltpu.roll(low, deep, 1) + pltpu.roll(high, 2 * deep, 1)
    lhs[...] = matrix
    lhs0[...] = jnp.zeros_like(lhs0)
    for k in range(2):
        lhs0[k : k + 1, :] = matrix[k * stride : k * stride + 1]

    source = lax.broadcasted_iota(jnp.int32, (wl, lanes), 0)
    into = lax.rem(lax.broadcasted_iota(jnp.int32, (wl, lanes), 1), window)
    first_row = me * own - left
    keep = (into + first_row >= 0) & (into + first_row < lat_rows - 1)
    below = (into > 0) & (into + first_row >= 1) & (into + first_row < lat_rows)
    pick[:, :lanes] = jnp.where(source == into, 1.0, 0.0)
    pick[:, lanes : 2 * lanes] = jnp.where((source == into + window) & keep, 1.0, 0.0)
    pick[:, 2 * lanes :] = jnp.where((source == into + window - 1) & below, 1.0, 0.0)

    def obs_copy(s, n):
        return remote(
            obs.at[s, 0], obs.at[s, 1 + n], us.at[s, n], ur.at[s, n], me, sides[1 - n], core
        )

    beside = range(1 if bands == 2 else 2)

    def hand_obs(s):
        @pl.when(me != s)
        def _():
            remote(obs.at[s, 0], obs.at[s, 0], os.at[0, 0], orr.at[s], me, sides[0], core).wait_recv()

        @pl.when(s > 0)
        def _():
            for n in beside:
                obs_copy(s, n).start()

    def half_copy(t):
        place = land.at[t, pl.ds(my_pairs, half)]
        return remote(place, place, hs.at[t], hr.at[t], me, band, 1 - core)

    def edges(depth):
        found = []
        for side in range(2):
            begin = 0 if side == 0 else own_pairs - depth
            for c in range(2):
                a, b = max(begin, half * c), min(begin + depth, half * (c + 1))
                if a < b:
                    found.append((side, c, a, b))
        return found

    def edge_copy(t, side, c, a, b, q):
        to = halo_pairs + (own_pairs if side == 0 else -own_pairs)
        return remote(
            land.at[t, pl.ds(halo_pairs + a, b - a)], land.at[t, pl.ds(to + a, b - a)],
            xs.at[t, side, q], xr.at[t, side, c], me, sides[side], q,
        )

    def with_depth(t, act):
        if early:
            for depth in range(1, halo_pairs + 1):

                @pl.when((t + 1) // 2 == depth)
                def _():
                    act(depth)

        else:

            @pl.when(t > halo // 2)
            def _():
                act(halo_pairs)

            @pl.when(t <= halo // 2)
            def _():
                act(halo_pairs // 2)

    def hand_winds(t):
        s = t // hours_sec

        pl.when(me != s)(lambda: came(t, 0))

        def act(depth):
            for c in range(2):

                @pl.when(core == c)
                def _():
                    for side, sender, a, b in edges(depth):
                        if sender == c:
                            for q in range(2):
                                edge_copy(t, side, sender, a, b, q).start()

        with_depth(t, act)

        @pl.when(me != s)
        def _():
            if early:
                came(t, 1)
            half_copy(t).start()

    def take_winds(t):
        s = t // hours_sec

        @pl.when(me != s)
        def _():
            place = land.at[t, pl.ds(halo_pairs + half * (1 - core), half)]
            remote(place, place, hs.at[t], hr.at[t], me, band, 1 - core).wait_recv()

        def act(depth):
            for side, sender, a, b in edges(depth):
                edge_copy(t, side, sender, a, b, 0).wait_recv()

        with_depth(t, act)

    first_row = me * own - left

    def observed(s, piece):
        place = obs[s, piece, 0, :, 0:count].astype(jnp.int32)
        level = place // (cols * lat_rows)
        rest = place - level * (cols * lat_rows)
        column = rest // lat_rows
        row = rest - column * lat_rows - first_row
        hit = lax.broadcasted_iota(jnp.int32, (window, count), 0) == row
        parts = [
            split2(jnp.where(hit, obs[s, piece, 1 + p, :, 0:count], 0.0)) for p in range(probes)
        ]
        rhs = jnp.concatenate([x[0] for x in parts] + [x[1] for x in parts], axis=0)
        return level, column, rhs

    def placed_sum(hot, rhs):
        got = lax.dot_general(
            hot.astype(jnp.float32).astype(jnp.bfloat16), rhs, (((1,), (1,)), ((), ())),
            preferred_element_type=jnp.float32,
        )
        return got[:, :lanes] + got[:, lanes:]

    def lowest(t):
        return (halo - t) // WIDE

    def highest(t):
        return (halo + cols + t + WIDE - 1) // WIDE

    edge_blocks = halo // WIDE
    own_blocks = cols // WIDE
    together = max(n for n in range(1, 4) if own_blocks % n == 0)

    def inject(s, slot):
        t = s * hours_sec
        for n in beside:
            remote(
                obs.at[s, 0], obs.at[s, 1 + n], us.at[s, n], ur.at[s, n], me, sides[0], core
            ).wait_recv()
        if early:
            lo, hi = lowest(t), highest(t)
            ranges = [
                (0, [(halo, edge_blocks, edge_blocks + own_blocks)]),
                (1, [(halo - cols, lo, edge_blocks)]),
                (2 if bands > 2 else 1, [(halo + cols, edge_blocks + own_blocks, hi)]),
            ]
            if bands == 2:
                ranges = [ranges[0], (1, ranges[1][1] + ranges[2][1])]
            for piece, places in ranges:
                level, column, rhs = observed(s, piece)
                hots = []
                for shift, begin, end in places:
                    place = (column + shift) * stride + level - begin * block
                    chunk = lax.broadcasted_iota(jnp.int32, ((end - begin) * block, count), 0)
                    hots.append((chunk == place).astype(jnp.float32).astype(jnp.bfloat16))
                hot = hots[0] if len(hots) == 1 else jnp.concatenate(hots, axis=0)
                got = lax.dot_general(
                    hot, rhs, (((1,), (1,)), ((), ())), preferred_element_type=jnp.float32
                )
                add = got[:, :lanes] + got[:, lanes:]
                done = 0
                for shift, begin, end in places:
                    size = (end - begin) * block
                    inj[slot, pl.ds(PAD + begin * block, size), :] = add[done : done + size]
                    done += size
            return
        for piece, shift, begin, end, step in (
            (0, halo, edge_blocks, edge_blocks + own_blocks, together),
            (1, halo - cols, lowest(t), edge_blocks, 1),
            (2 if bands > 2 else 1, halo + cols, edge_blocks + own_blocks, highest(t), 1),
        ):
            level, column, rhs = observed(s, piece)
            place = (column + shift) * stride + level
            high_rows = step * block
            chunk = lax.broadcasted_iota(jnp.int32, (high_rows, count), 0)

            def body(i, carry, begin=begin, step=step, place=place, rhs=rhs, chunk=chunk, high_rows=high_rows):
                b = begin + i * step
                add = placed_sum(chunk == place - b * block, rhs)
                inj[slot, pl.ds(pl.multiple_of(PAD + b * block, 8), high_rows), :] = add
                return carry

            lax.fori_loop(0, (end - begin) // step, body, 0)

    def ground(field=state):
        start = PAD + halo * stride
        if lanes == 128:
            return field[pl.ds(start, cols, stride=stride), :]
        rows = [state[start + c * stride : start + c * stride + 1, :] for c in range(cols)]
        return jnp.concatenate(rows, axis=0)

    def add_flux(s, h, x):
        which = obs[s, 0, 0, :, count:]
        lane = lax.broadcasted_iota(jnp.int32, (1, 128), 1)
        number = jnp.sum(jnp.where(lane == h, which, 0.0), axis=1, keepdims=True)
        for w in range(d["weeks"]):
            flux[w] += jnp.where(number == w, x, 0.0)

    def surface(s, slot):
        level, column, rhs = observed(0, 0)
        tall = -(-cols // 8) * 8
        chunk = lax.broadcasted_iota(jnp.int32, (tall, count), 0)
        add = placed_sum(chunk == jnp.where(level == 0, column, -1), rhs)
        add_flux(0, 0, add[:cols])

    middle = hours // 2

    def slot_of(t):
        return t if early else 0

    def prepare(t, span=None):
        slot = slot_of(t)
        if not early:
            copy = pltpu.make_async_copy(land.at[t], stage, local.at[0])
            copy.start()
            copy.wait()
        lo, hi = lowest(t), highest(t)
        wm[slot, pl.ds(pl.multiple_of(PAD + lo * block, 8), PAD), :] = jnp.zeros((PAD, lanes), jnp.float32)
        matrix = pick[...].astype(jnp.bfloat16)

        def spread(b, n):
            base = pl.multiple_of(PAD + b * block, 8)
            at = pl.ds(b * WIDE // 2, n * WIDE // 2)
            packed = land[t, at] if early else stage[at]
            packed = packed.reshape(n * block, wl)
            got = jnp.dot(packed, matrix, preferred_element_type=jnp.float32)
            east, north, south = got[:, :lanes], got[:, lanes : 2 * lanes], got[:, 2 * lanes :]
            ep[slot, pl.ds(base, n * block), :] = jnp.maximum(east, 0.0)
            wm[slot, pl.ds(base + stride, n * block), :] = jnp.minimum(east, 0.0)
            npos[slot, pl.ds(base, n * block), :] = jnp.maximum(north, 0.0)
            sneg[slot, pl.ds(base, n * block), :] = jnp.minimum(south, 0.0)

        def one(b, carry):
            spread(b, 1)
            return carry

        def many(i, carry):
            spread(edge_blocks + i * together, together)
            return carry

        if span is not None:
            b = span[0]
            while b < span[1]:
                n = min(3, span[1] - b)
                spread(b, n)
                b += n
            return
        lax.fori_loop(lo, edge_blocks, one, 0)
        lax.fori_loop(0, own_blocks // together, many, 0)
        lax.fori_loop(edge_blocks + own_blocks, hi, one, 0)

    def advance(t, slot, span=None):
        s = t // hours_sec
        h = t - s * hours_sec
        lo, hi = lowest(t), highest(t)

        if span is not None:
            slot = jnp.where(h == 0, s, 0)
        else:

            @pl.when(h == 0)
            def _():
                def body(b, carry):
                    at = pl.ds(pl.multiple_of(PAD + b * block, 8), block)
                    state[at, :] += inj[slot, at, :]
                    return carry

                lax.fori_loop(lo, hi, body, 0)

        add_flux(s, h, ground() if span is None else ground() + ground(inj.at[slot]))
        mix = lhs[0:deep, 0 : 3 * deep].astype(jnp.bfloat16)
        where = slot_of(t)

        def at_block(b):
            return PAD + b * block if span is not None else pl.multiple_of(PAD + b * block, 8)

        def mixing_of(b):
            base = at_block(b)
            parts = [state[pl.ds(base + k * deep, deep), :] for k in range(2)]
            if span is not None:
                parts = [x + inj[slot, pl.ds(base + k * deep, deep), :] for k, x in enumerate(parts)]
            x = jnp.concatenate(parts, axis=1)
            low = x - x.astype(jnp.bfloat16).astype(jnp.float32)
            stack = jnp.concatenate([x, x, low], axis=0).astype(jnp.bfloat16)
            return jnp.dot(mix, stack, preferred_element_type=jnp.float32)

        def keep_mixed(b, got):
            base = at_block(b)
            mixed[pl.ds(base, deep), :] = got[:, :lanes]
            mixed[pl.ds(base + deep, deep), :] = got[:, lanes:]

        def advect(b):
            base = at_block(b)
            at = pl.ds(base, block)
            here = mixed[at, :]
            after = mixed[pl.ds(base + stride, block), :]
            before = mixed[pl.ds(base - stride, block), :]
            g = here + ep[where, at, :] * (after - here) + wm[where, at, :] * (here - before)
            above = pltpu.roll(g, lanes - 1, 1)
            below = pltpu.roll(g, 1, 1)
            return g + npos[where, at, :] * (above - g) + sneg[where, at, :] * (g - below)

        def keep_state(b, x):
            state[pl.ds(at_block(b), block), :] = x

        def only_mix(b, carry):
            keep_mixed(b, mixing_of(b))
            return carry

        def both(b, carry):
            got = mixing_of(b)
            new = advect(b - 2)
            keep_state(b - 2, new)
            keep_mixed(b, got)
            return carry

        def only_advect(b, carry):
            keep_state(b, advect(b))
            return carry

        if span is not None:
            for b in range(span[0], span[1] + 2):
                got = mixing_of(b) if b < span[1] else None
                if b >= span[0] + 2:
                    keep_state(b - 2, advect(b - 2))
                if b < span[1]:
                    keep_mixed(b, got)
            return
        lax.fori_loop(lo, lo + 2, only_mix, 0)
        lax.fori_loop(lo + 2, hi, both, 0)
        lax.fori_loop(hi - 2, hi, only_advect, 0)

    def ground_copy():
        return remote(in0.at[0], in0.at[1], gs.at[0], gr.at[1], me, sides[1], core)

    def hand_ground():
        @pl.when(me > 0)
        def _():
            remote(in0.at[0], in0.at[0], gs.at[0], gr.at[0], me, sides[0], core).wait_recv()

        ground_copy().start()

    def prepare_ground():
        remote(in0.at[1], in0.at[1], gs.at[0], gr.at[1], me, sides[0], core).wait_recv()
        matrix = pick[...].astype(jnp.bfloat16)
        got = jnp.dot(in0[0].astype(jnp.bfloat16), matrix, preferred_element_type=jnp.float32)
        west = jnp.dot(
            in0[1].astype(jnp.bfloat16), matrix[:, :lanes], preferred_element_type=jnp.float32
        )
        east, north, south = got[:, :lanes], got[:, lanes : 2 * lanes], got[:, 2 * lanes :]
        faces0[0, 0:cols, :] = jnp.maximum(east, 0.0)
        faces0[1, 1 : cols + 1, :] = jnp.minimum(east, 0.0)
        faces0[1, 0:1, :] = jnp.minimum(west[cols - 1 : cols], 0.0)
        faces0[2, 0:cols, :] = jnp.maximum(north, 0.0)
        faces0[3, 0:cols, :] = jnp.minimum(south, 0.0)

    def last_step(span):
        add_flux(0, 1, ground())
        mix = lhs0[:, 0 : 3 * deep].astype(jnp.bfloat16)
        for b in range(*span):
            base = PAD + b * block
            x = jnp.concatenate([state[pl.ds(base + k * deep, deep), :] for k in range(2)], axis=1)
            low = x - x.astype(jnp.bfloat16).astype(jnp.float32)
            stack = jnp.concatenate([x, x, low], axis=0).astype(jnp.bfloat16)
            got = jnp.dot(mix, stack, preferred_element_type=jnp.float32)
            mixed0[b * WIDE : b * WIDE + 2, :] = got[0:2, :lanes]
            mixed0[b * WIDE + 2 : b * WIDE + 4, :] = got[0:2, lanes:]
        here = mixed0[halo : halo + cols, :]
        after = mixed0[halo + 1 : halo + cols + 1, :]
        before = mixed0[halo - 1 : halo + cols - 1, :]
        faces = [faces0[k, 0:cols, :] for k in range(4)]
        g = here + faces[0] * (after - here) + faces[1] * (here - before)
        above = pltpu.roll(g, lanes - 1, 1)
        below = pltpu.roll(g, 1, 1)
        add_flux(0, 0, g + faces[2] * (above - g) + faces[3] * (g - below))

    def finish_obs():
        obs_targets(lambda s, tm: obs_send(s, tm).wait_send())

        def sent_obs(s):
            for n in beside:
                obs_copy(s, n).wait_send()

        loop(sections - 1, 1, sent_obs)
        if early:
            ground_copy().wait_send()

            @pl.when(me == 0)
            def _():
                for target in range(1, sections):
                    out_copy(target).wait_send()

    def sent_winds(t):
        @pl.when(me != t // hours_sec)
        def _():
            half_copy(t).wait_send()

        def act(depth):
            for c in range(2):

                @pl.when(core == c)
                def _():
                    for side, sender, a, b in edges(depth):
                        if sender == c:
                            for q in range(2):
                                edge_copy(t, side, sender, a, b, q).wait_send()

        with_depth(t, act)

    def loop(high, low, run):
        def body(i, carry):
            run(high - i)
            return carry

        lax.fori_loop(0, high - low + 1, body, 0)

    if early:

        loop(hours_sec - 1, home, lambda h: hand_winds(me * hours_sec + h))
        hand_obs(sections - 1)
        second()
        for s in range(sections - 1, 0, -1):
            hand_obs(s - 1)
            inject(s, s)
        surface(0, 0)
        third()
        far = (lowest(hours - 1), highest(hours - 1))
        near = (lowest(middle), highest(middle))

        code = 0
        for z in range(sections):
            mine = [t for t in range(hours - 1, 1, -1) if t // hours_sec == z]
            low_hours = [t for t in range(middle - 1, 1, -1) if t not in mine]
            high_hours = [t for t in range(hours - 1, middle - 1, -1) if t not in mine]
            if z < half_way:
                high_hours.sort(key=lambda t: (-(t % hours_sec), -t))
                order = mine + low_hours + high_hours
            else:
                order = mine + high_hours + low_hours
            code = jnp.where(me == z, sum(t * hours**k for k, t in enumerate(order)), code)

        def ready(i, code):
            t = lax.rem(code, hours)
            code = code // hours
            after = lax.rem(code, hours)
            pl.when(me != after // hours_sec)(lambda: hand_winds(after))
            take_winds(t)
            pl.when(t >= middle + 1)(lambda: prepare(t, far))
            pl.when(t <= middle)(lambda: prepare(t, near))
            sent_winds(t)
            pl.when(i == hours - 5)(lambda: advance(hours - 1, 0, far))
            return code

        foremost = lax.rem(code, hours)
        pl.when(me != foremost // hours_sec)(lambda: hand_winds(foremost))
        final = lax.fori_loop(0, hours - 3, ready, code)
        hand_ground()
        loop(hours - 2, middle + 1, lambda t: advance(t, 0, far))
        prepare_ground()
        take_winds(final)
        prepare(final, near)
        loop(middle, 2, lambda t: advance(t, 0, near))
        last_step(near)
    else:
        loop(sections - 1, 0, hand_obs)
        surface(0, 0)

        def whole(t):
            s = t // hours_sec

            @pl.when(t == s * hours_sec)
            def _():
                inject(s, 0)

            hand_winds(t)
            take_winds(t)
            prepare(t)
            advance(t, 0)

        loop(hours - 1, 1, whole)

    if not early:
        add_flux(0, 0, ground())
    for w in range(d["weeks"]):
        square = flux[w] * flux[w]
        est[w] = (square + pltpu.roll(square, lanes - window, 1)) * 0.5

    if early:
        finish_lower()
        finish_upper()
        finish_obs()
        sent_winds(final)
    else:
        every_job(sent)
        finish_obs()
        loop(hours - 1, 1, sent_winds)


def on_device(winds, mixing, obs_cell, obs_weight, probe_sign, week_map, prior_precision):
    week_count, _, own = prior_precision.shape
    d = plan(
        lax.axis_size("tm"), lax.axis_size("lon"), winds.shape[2], winds.shape[4], winds.shape[3],
        winds.shape[5], own, probe_sign.shape[0], week_count, obs_cell.shape[2],
    )
    sections, hours, hours_sec = d["sections"], d["hours"], d["hours_sec"]
    lanes, rows, cols, left = d["lanes"], d["rows"], d["cols"], d["left"]
    early = d["early"]
    wire = (d["half"], 2 * d["stride"], 2 * d["window"])
    landing = (hours, d["pairs"]) + wire[1:]
    slots = hours if early else 1
    inj_slots = sections if early else 1
    sem = pltpu.SemaphoreType.DMA
    scratch = [
        pltpu.VMEM((hours_sec, sections) + wire, jnp.bfloat16),
        pltpu.VMEM((2 * d["half"] * d["stride"], 2 * d["window"]), jnp.float32),
        pltpu.VMEM((sections, 3, 1 + d["probes"], 1, d["count"] + 128), jnp.float32),
        pltpu.VMEM((128, 256), jnp.float32),
        pltpu.VMEM((2 * d["window"], 3 * lanes), jnp.float32),
        pltpu.VMEM((rows, lanes), jnp.float32),
        pltpu.VMEM((rows, lanes), jnp.float32),
        pltpu.VMEM((inj_slots, rows, lanes), jnp.float32),
    ] + [pltpu.VMEM((slots, rows, lanes), jnp.float32)] * 4 + [
        pltpu.VMEM((week_count, cols, lanes), jnp.float32),
        pltpu.VMEM((sections, cols, 2 * d["window"]), jnp.float32),
        pltpu.VMEM((2, cols, 2 * d["window"]), jnp.float32),
        pltpu.VMEM((8, 256), jnp.float32),
        pltpu.VMEM((d["blocks"] * WIDE, lanes), jnp.float32),
        pltpu.VMEM((4, cols + 4, lanes), jnp.float32),
        sem((sections + 1,)), sem((2,)),
        sem((hours_sec, sections, 2)), sem((hours, 2)), sem((hours,)), sem((hours,)),
        sem((hours, 2, 2)), sem((hours, 2, 2)), sem((sections, sections)), sem((sections,)),
        sem((sections, 2)), sem((sections, 2)), sem((1,)),
    ]
    outs = [jax.ShapeDtypeStruct((week_count, cols, lanes), jnp.float32)]
    out_specs = [pl.BlockSpec(memory_space=pltpu.VMEM)]
    if early:
        scratch = [pltpu.VMEM(landing, jnp.bfloat16)] + scratch
    else:
        outs.append(jax.ShapeDtypeStruct(landing, jnp.bfloat16))
        out_specs.append(pl.BlockSpec(memory_space=pl.ANY))
        scratch = [pltpu.VMEM(landing[1:], jnp.bfloat16)] + scratch
    got = pl.pallas_call(
        functools.partial(fused_kernel, d),
        out_shape=tuple(outs),
        in_specs=[pl.BlockSpec(memory_space=pltpu.VMEM)] * 6,
        out_specs=tuple(out_specs),
        scratch_shapes=scratch,
        compiler_params=pltpu.CompilerParams(
            collective_id=0, has_side_effects=True, vmem_limit_bytes=(51 if early else 56) << 20
        ),
    )(
        winds.transpose(0, 1, 2, 4, 3, 5), mixing, obs_cell[0], obs_weight[0],
        probe_sign[:, 0], week_map,
    )
    return (prior_precision + got[0][..., left : left + own])[None]


def solution(mesh):
    placed = (
        P(None, ("groups", "tm"), None, None, "lon", None),
        P(),
        P(("groups", "tm"), "lon", None),
        P(("groups", "tm"), "lon", None),
        P("probe", ("groups", "tm"), "lon", None),
        P(("groups", "tm"), None),
        P("groups", "lon", "tm"),
    )
    return jax.shard_map(
        on_device,
        mesh=mesh,
        in_specs=placed,
        out_specs=P("probe", "groups", "lon", "tm"),
        check_vma=False,
    )
```

```python
import functools

import jax
import jax.numpy as jnp
from jax import lax
from jax.experimental import pallas as pl
from jax.experimental.pallas import tpu as pltpu
from jax.sharding import PartitionSpec as P

WIDE = 4
PAD = 40


def split2(x):
    high = x.astype(jnp.bfloat16)
    low = (x - high.astype(jnp.float32)).astype(jnp.bfloat16)
    return high, low


def plan(sections, bands, hours_sec, cols, levels, lat_rows, own, probes, weeks, count):
    hours = sections * hours_sec
    halo = -(-hours // WIDE) * WIDE
    window = -(-(own + 2 * hours) // 64) * 64
    d = dict(
        sections=sections, bands=bands, hours_sec=hours_sec, cols=cols, levels=levels,
        lat_rows=lat_rows, own=own, probes=probes, weeks=weeks, count=count, hours=hours,
        halo=halo, left=hours, window=window, lanes=window * probes,
        half=cols // 4, halo_pairs=halo // 2, pairs=(cols + 2 * halo) // 2,
        blocks=(cols + 2 * halo) // WIDE,
    )
    d["stride"] = levels if d["lanes"] == 128 else -(-levels // 8) * 8
    d["block"] = WIDE * d["stride"]
    d["rows"] = PAD + (d["blocks"] + 1) * d["block"]
    d["early"] = hours <= 8 and hours_sec == 2 and sections % 2 == 0
    return d


def fused_kernel(d, winds, mixing, cell, weight, sign, week, *refs):
    sections, bands, hours_sec, hours = d["sections"], d["bands"], d["hours_sec"], d["hours"]
    cols, levels, lat_rows, own = d["cols"], d["levels"], d["lat_rows"], d["own"]
    probes, count, halo, left = d["probes"], d["count"], d["halo"], d["left"]
    window, lanes, half, halo_pairs = d["window"], d["lanes"], d["half"], d["halo_pairs"]
    block, early, stride = d["block"], d["early"], d["stride"]
    if early:
        est, land, refs = refs[0], refs[1], refs[2:]
        stage = None
    else:
        est, land, stage, refs = refs[0], refs[1], refs[2], refs[3:]
    (pack, flat, obs, lhs, pick, state, mixed, inj, ep, wm, npos, sneg, flux,
     out0, in0, lhs0, mixed0, faces0, gs, gr, zs, zr, hs, hr, xs, xr, os, orr, us, ur, local) = refs
    own_pairs = 2 * half
    me = lax.axis_index("tm")
    band = lax.axis_index("lon")
    core = lax.axis_index("probe")
    sides = [lax.rem(band + bands - 1, bands), lax.rem(band + 1, bands)]
    if bands == 2:
        greet = sides[:1]
    else:
        greet = sides

    def remote(src, dst, send, recv, tm, lon, probe):
        return pltpu.make_async_remote_copy(
            src_ref=src, dst_ref=dst, send_sem=send, recv_sem=recv,
            device_id={"tm": tm, "lon": lon, "probe": probe},
            device_id_type=pl.DeviceIdType.MESH,
        )

    if early:
        for t in range(2, hours):
            reach = (t + 1) // 2
            for n in range((halo - t) // WIDE * WIDE // 2, halo_pairs - reach):
                land[t, n] = jnp.zeros(land.shape[2:], land.dtype)
                land[t, 2 * halo_pairs + own_pairs - 1 - n] = jnp.zeros(land.shape[2:], land.dtype)

    barrier = pltpu.get_barrier_semaphore()

    def hello(tm, lon, probe):
        pl.semaphore_signal(
            barrier, inc=1, device_id={"tm": tm, "lon": lon, "probe": probe},
            device_id_type=pl.DeviceIdType.MESH,
        )

    for k in range(1, sections):
        hello(lax.rem(me + k, sections), band, core)
    for lon in greet:
        for q in range(2):
            hello(me, lon, q)
    hello(me, band, 1 - core)

    obs[me, 0, 0, :, 0:count] = cell[...].astype(jnp.float32)
    for p in range(probes):
        obs[me, 0, 1 + p, :, 0:count] = (2 * sign[p] - 1).astype(jnp.float32) * weight[...]
        obs[me, 0, 1 + p, :, count:] = jnp.zeros((1, 128), jnp.float32)
    lane_row = lax.broadcasted_iota(jnp.int32, (1, 128), 1)
    weeks_row = jnp.zeros((1, 128), jnp.float32)
    for h in range(hours_sec):
        weeks_row = jnp.where(lane_row == h, week[0:1, h : h + 1].astype(jnp.float32), weeks_row)
    obs[me, 0, 0, :, count:] = weeks_row

    if stride != levels:
        flat[...] = jnp.zeros_like(flat)
    wl = 2 * window
    lat_tiles = -(-lat_rows // 128)

    def packed_column(h, column, start, levels=levels):
        tiles = []
        for comp in range(2):
            row = []
            for k in range(lat_tiles):
                x = winds[comp, 0, h, column, 0:levels, k * 128 : min(k * 128 + 128, lat_rows)]
                x = x.astype(jnp.float32)
                if x.shape[1] < 128:
                    x = jnp.concatenate(
                        [x, jnp.zeros((levels, 128 - x.shape[1]), jnp.float32)], axis=1
                    )
                row.append(x)
            tiles.append(row)
        lane = lax.broadcasted_iota(jnp.int32, (levels, 128), 1)
        parts = []
        for v in range(wl // 128):
            out = jnp.zeros((levels, 128), jnp.float32)
            for comp in range(2):
                begin = comp * window - v * 128
                if begin >= 128 or begin + window <= 0:
                    continue
                shift = lax.rem(begin - start + 512, 128)
                at = lane - begin
                row = at + start
                for k in range(lat_tiles):
                    inside = (
                        (at >= 0) & (at < window) & (row >= k * 128)
                        & (row < min(k * 128 + 128, lat_rows))
                    )
                    out = jnp.where(inside, pltpu.roll(tiles[comp][k], shift, 1), out)
            parts.append(out)
        return parts[0] if len(parts) == 1 else jnp.concatenate(parts, axis=1)

    def fill(h, target, first_column, put):
        start = target * own - left

        def body(i, carry):
            for c in range(2):
                at = pl.multiple_of(i * 2 * stride, 8) + c * stride
                flat[pl.ds(at, levels), :] = packed_column(h, first_column + 2 * i + c, start)
            return carry

        lax.fori_loop(0, half, body, 0, unroll=3)

        def cast(i, carry):
            x = flat[pl.ds(pl.multiple_of(i * 2 * stride, 8), 2 * stride), :]
            put(i, x.astype(jnp.bfloat16))
            return carry

        lax.fori_loop(0, half, cast, 0, unroll=3)

    least = jnp.where(me == 0, 1, 0)
    my_pairs = halo_pairs + half * core

    if early:
        parts = [((half - halo_pairs) * core, halo_pairs), (halo_pairs * (1 - core), half - halo_pairs)]
    else:
        parts = [(0, half)]

    def z_copy(h, target, n):
        t = me * hours_sec + h
        begin, size = parts[n]
        return remote(
            pack.at[h, target, pl.ds(begin, size)], land.at[t, pl.ds(my_pairs + begin, size)],
            zs.at[h, target, n], zr.at[t, n], target, band, core,
        )

    def came(t, n):
        begin, size = parts[n]
        place = land.at[t, pl.ds(my_pairs + begin, size)]
        remote(place, place, zs.at[0, 0, n], zr.at[t, n], me, sides[0], core).wait_recv()

    def start(h, target):
        for n in range(len(parts)):
            z_copy(h, target, n).start()

    def sent(h, target):
        for n in range(len(parts)):
            z_copy(h, target, n).wait_send()

    def job(h, target):
        def put(i, x):
            pack[h, target, i] = x

        fill(h, target, 2 * half * core, put)
        start(h, target)

    def every_job(run):
        def upper(i, carry):
            h = hours_sec - 1 - i

            def target(k, inner):
                run(h, sections - 1 - k)
                return inner

            return lax.fori_loop(0, sections - 1 - me, target, carry)

        lax.fori_loop(0, hours_sec - least, upper, 0)

        def lower(i, carry):
            h = hours_sec - 1 - i

            def target(k, inner):
                run(h, k)
                return inner

            return lax.fori_loop(0, me, target, carry)

        lax.fori_loop(0, hours_sec - least, lower, 0)

    last = hours_sec - 1
    if early:
        half_way = sections // 2
        top = me == sections - 1
        beyond = jnp.where(top, 0, me + 1)

        def put_first(i, x):
            pack[last, beyond, i] = x

        pl.when(me > 0)(lambda: fill(last, beyond, 2 * half * core, put_first))

    pl.semaphore_wait(barrier, sections - 1 + 2 * len(greet) + 1)

    def obs_send(s, tm):
        mine = obs.at[s, 0]
        return remote(mine, mine, os.at[s, tm], orr.at[s], tm, band, core)

    def obs_targets(act):
        for k in range(1, sections):
            act(me, lax.rem(me + k, sections))

    obs_targets(lambda s, tm: obs_send(s, tm).start())

    def each(run, h, low, high):
        def body(i, carry):
            run(h, low + i)
            return carry

        lax.fori_loop(0, high - low, body, 0)

    def fill_job(h, target):
        def put(i, x):
            pack[h, target, i] = x

        fill(h, target, 2 * half * core, put)

    if early:
        lower = me < half_way
        upper = (me >= half_way) & (me < sections - 1)
        pl.when(me > 0)(lambda: start(last, beyond))
        many = jnp.where(top, half_way, jnp.where(me > 0, sections, beyond + 1))
        each(job, last, beyond + 1, many)
        each(job, 0, me + 1, jnp.where(me >= half_way, sections, me + 1))

        def rest(run):
            each(run, 0, me + 1, jnp.where(lower & (me > 0), sections, me + 1))
            each(run, last, jnp.where(top, half_way, 0), me)
            each(run, 0, 0, me)

        rest(fill_job)

        @pl.when(lower)
        def _():
            rest(start)

    else:
        every_job(job)

    def second():
        @pl.when(upper)
        def _():
            each(start, last, 0, me)

        @pl.when(top)
        def _():
            each(start, 0, 0, half_way)
            each(start, last, half_way, me)

    def third():
        @pl.when(upper)
        def _():
            for n in range(len(parts)):
                each(lambda h, target, n=n: z_copy(h, target, n).start(), 0, 0, me)

        @pl.when(top)
        def _():
            each(start, 0, half_way, me)

    def finish_lower():
        @pl.when(lower)
        def _():
            each(sent, last, me + 1, jnp.where(me > 0, sections, me + 1))
            rest(sent)

    def finish_upper():
        @pl.when(upper)
        def _():
            each(sent, last, 0, me)
            each(sent, last, me + 1, sections)
            each(sent, 0, me + 1, sections)
            each(sent, 0, 0, me)

        @pl.when(top)
        def _():
            each(sent, last, 0, me)
            each(sent, 0, 0, me)

    def out_copy(target):
        return remote(out0.at[target], in0.at[0], gs.at[target], gr.at[0], target, band, core)

    if early:

        @pl.when(me == 0)
        def _():
            def ground_of(target, carry):
                def body(i, inner):
                    x = packed_column(last, i, target * own - left, 16)
                    out0[target, pl.ds(i, 1), :] = x[0:1]
                    return inner

                lax.fori_loop(0, cols, body, 0, unroll=6)
                pl.when(target > 0)(lambda: out_copy(target).start())
                return carry

            lax.fori_loop(0, sections, ground_of, 0)
            in0[0] = out0[0]

    def at_home(i, carry):
        h = hours_sec - 1 - i
        t = me * hours_sec + h
        for c in range(2):
            if early:

                def put(i, x):
                    land[t, halo_pairs + half * c + i] = x

                fill(h, me, 2 * half * c, put)
            else:

                def put(i, x):
                    pack[h, me, i] = x

                fill(h, me, 2 * half * c, put)
                copy = pltpu.make_async_copy(
                    pack.at[h, me], land.at[t, pl.ds(halo_pairs + half * c, half)], local.at[0]
                )
                copy.start()
                copy.wait()
        return carry

    home = jnp.where(me == 0, hours_sec, 0) if early else least
    lax.fori_loop(0, hours_sec - home, at_home, 0)

    zero = jnp.zeros((PAD, lanes), jnp.float32)

    def clear(i, carry):
        at = pl.multiple_of(i * 8, 8)
        state[pl.ds(at, 8), :] = zero[:8]
        mixed[pl.ds(at, 8), :] = zero[:8]
        inj[0, pl.ds(at, 8), :] = zero[:8]
        return carry

    lax.fori_loop(0, d["rows"] // 8, clear, 0, unroll=8)
    flux[...] = jnp.zeros_like(flux)
    lhs[...] = jnp.zeros_like(lhs)
    lhs[0:levels, 0:levels] = mixing[...]
    turned_mix = jnp.transpose(lhs[:, 0:128])
    both = turned_mix + pltpu.roll(pltpu.roll(turned_mix, stride, 0), stride, 1)
    high = both.astype(jnp.bfloat16).astype(jnp.float32)
    low = both - high
    none = jnp.zeros_like(both)
    high = jnp.concatenate([high, none], axis=1)
    low = jnp.concatenate([low, none], axis=1)
    deep = 2 * stride
    matrix = high + pltpu.roll(low, deep, 1) + pltpu.roll(high, 2 * deep, 1)
    lhs[...] = matrix
    lhs0[...] = jnp.zeros_like(lhs0)
    for k in range(2):
        lhs0[k : k + 1, :] = matrix[k * stride : k * stride + 1]

    source = lax.broadcasted_iota(jnp.int32, (wl, lanes), 0)
    into = lax.rem(lax.broadcasted_iota(jnp.int32, (wl, lanes), 1), window)
    first_row = me * own - left
    keep = (into + first_row >= 0) & (into + first_row < lat_rows - 1)
    below = (into > 0) & (into + first_row >= 1) & (into + first_row < lat_rows)
    pick[:, :lanes] = jnp.where(source == into, 1.0, 0.0)
    pick[:, lanes : 2 * lanes] = jnp.where((source == into + window) & keep, 1.0, 0.0)
    pick[:, 2 * lanes :] = jnp.where((source == into + window - 1) & below, 1.0, 0.0)

    def obs_copy(s, n):
        return remote(
            obs.at[s, 0], obs.at[s, 1 + n], us.at[s, n], ur.at[s, n], me, sides[1 - n], core
        )

    beside = range(1 if bands == 2 else 2)

    def hand_obs(s):
        @pl.when(me != s)
        def _():
            remote(obs.at[s, 0], obs.at[s, 0], os.at[0, 0], orr.at[s], me, sides[0], core).wait_recv()

        @pl.when(s > 0)
        def _():
            for n in beside:
                obs_copy(s, n).start()

    def half_copy(t):
        place = land.at[t, pl.ds(my_pairs, half)]
        return remote(place, place, hs.at[t], hr.at[t], me, band, 1 - core)

    def edges(depth):
        found = []
        for side in range(2):
            begin = 0 if side == 0 else own_pairs - depth
            for c in range(2):
                a, b = max(begin, half * c), min(begin + depth, half * (c + 1))
                if a < b:
                    found.append((side, c, a, b))
        return found

    def edge_copy(t, side, c, a, b, q):
        to = halo_pairs + (own_pairs if side == 0 else -own_pairs)
        return remote(
            land.at[t, pl.ds(halo_pairs + a, b - a)], land.at[t, pl.ds(to + a, b - a)],
            xs.at[t, side, q], xr.at[t, side, c], me, sides[side], q,
        )

    def with_depth(t, act):
        if early:
            for depth in range(1, halo_pairs + 1):

                @pl.when((t + 1) // 2 == depth)
                def _():
                    act(depth)

        else:

            @pl.when(t > halo // 2)
            def _():
                act(halo_pairs)

            @pl.when(t <= halo // 2)
            def _():
                act(halo_pairs // 2)

    def hand_winds(t):
        s = t // hours_sec

        pl.when(me != s)(lambda: came(t, 0))

        def act(depth):
            for c in range(2):

                @pl.when(core == c)
                def _():
                    for side, sender, a, b in edges(depth):
                        if sender == c:
                            for q in range(2):
                                edge_copy(t, side, sender, a, b, q).start()

        with_depth(t, act)

        @pl.when(me != s)
        def _():
            if early:
                came(t, 1)
            half_copy(t).start()

    def take_winds(t):
        s = t // hours_sec

        @pl.when(me != s)
        def _():
            place = land.at[t, pl.ds(halo_pairs + half * (1 - core), half)]
            remote(place, place, hs.at[t], hr.at[t], me, band, 1 - core).wait_recv()

        def act(depth):
            for side, sender, a, b in edges(depth):
                edge_copy(t, side, sender, a, b, 0).wait_recv()

        with_depth(t, act)

    first_row = me * own - left

    def observed(s, piece):
        place = obs[s, piece, 0, :, 0:count].astype(jnp.int32)
        level = place // (cols * lat_rows)
        rest = place - level * (cols * lat_rows)
        column = rest // lat_rows
        row = rest - column * lat_rows - first_row
        hit = lax.broadcasted_iota(jnp.int32, (window, count), 0) == row
        parts = [
            split2(jnp.where(hit, obs[s, piece, 1 + p, :, 0:count], 0.0)) for p in range(probes)
        ]
        rhs = jnp.concatenate([x[0] for x in parts] + [x[1] for x in parts], axis=0)
        return level, column, rhs

    def placed_sum(hot, rhs):
        got = lax.dot_general(
            hot.astype(jnp.float32).astype(jnp.bfloat16), rhs, (((1,), (1,)), ((), ())),
            preferred_element_type=jnp.float32,
        )
        return got[:, :lanes] + got[:, lanes:]

    def lowest(t):
        return (halo - t) // WIDE

    def highest(t):
        return (halo + cols + t + WIDE - 1) // WIDE

    edge_blocks = halo // WIDE
    own_blocks = cols // WIDE
    together = max(n for n in range(1, 4) if own_blocks % n == 0)

    def inject(s, slot):
        t = s * hours_sec
        for n in beside:
            remote(
                obs.at[s, 0], obs.at[s, 1 + n], us.at[s, n], ur.at[s, n], me, sides[0], core
            ).wait_recv()
        if early:
            lo, hi = lowest(t), highest(t)
            ranges = [
                (0, [(halo, edge_blocks, edge_blocks + own_blocks)]),
                (1, [(halo - cols, lo, edge_blocks)]),
                (2 if bands > 2 else 1, [(halo + cols, edge_blocks + own_blocks, hi)]),
            ]
            if bands == 2:
                ranges = [ranges[0], (1, ranges[1][1] + ranges[2][1])]
            for piece, places in ranges:
                level, column, rhs = observed(s, piece)
                hots = []
                for shift, begin, end in places:
                    place = (column + shift) * stride + level - begin * block
                    chunk = lax.broadcasted_iota(jnp.int32, ((end - begin) * block, count), 0)
                    hots.append((chunk == place).astype(jnp.float32).astype(jnp.bfloat16))
                hot = hots[0] if len(hots) == 1 else jnp.concatenate(hots, axis=0)
                got = lax.dot_general(
                    hot, rhs, (((1,), (1,)), ((), ())), preferred_element_type=jnp.float32
                )
                add = got[:, :lanes] + got[:, lanes:]
                done = 0
                for shift, begin, end in places:
                    size = (end - begin) * block
                    inj[slot, pl.ds(PAD + begin * block, size), :] = add[done : done + size]
                    done += size
            return
        for piece, shift, begin, end, step in (
            (0, halo, edge_blocks, edge_blocks + own_blocks, together),
            (1, halo - cols, lowest(t), edge_blocks, 1),
            (2 if bands > 2 else 1, halo + cols, edge_blocks + own_blocks, highest(t), 1),
        ):
            level, column, rhs = observed(s, piece)
            place = (column + shift) * stride + level
            high_rows = step * block
            chunk = lax.broadcasted_iota(jnp.int32, (high_rows, count), 0)

            def body(i, carry, begin=begin, step=step, place=place, rhs=rhs, chunk=chunk, high_rows=high_rows):
                b = begin + i * step
                add = placed_sum(chunk == place - b * block, rhs)
                inj[slot, pl.ds(pl.multiple_of(PAD + b * block, 8), high_rows), :] = add
                return carry

            lax.fori_loop(0, (end - begin) // step, body, 0)

    def ground(field=state):
        start = PAD + halo * stride
        if lanes == 128:
            return field[pl.ds(start, cols, stride=stride), :]
        rows = [state[start + c * stride : start + c * stride + 1, :] for c in range(cols)]
        return jnp.concatenate(rows, axis=0)

    def add_flux(s, h, x):
        which = obs[s, 0, 0, :, count:]
        lane = lax.broadcasted_iota(jnp.int32, (1, 128), 1)
        number = jnp.sum(jnp.where(lane == h, which, 0.0), axis=1, keepdims=True)
        for w in range(d["weeks"]):
            flux[w] += jnp.where(number == w, x, 0.0)

    def surface(s, slot):
        level, column, rhs = observed(0, 0)
        tall = -(-cols // 8) * 8
        chunk = lax.broadcasted_iota(jnp.int32, (tall, count), 0)
        add = placed_sum(chunk == jnp.where(level == 0, column, -1), rhs)
        add_flux(0, 0, add[:cols])

    middle = hours // 2

    def slot_of(t):
        return t if early else 0

    def prepare(t, span=None):
        slot = slot_of(t)
        if not early:
            copy = pltpu.make_async_copy(land.at[t], stage, local.at[0])
            copy.start()
            copy.wait()
        lo, hi = lowest(t), highest(t)
        wm[slot, pl.ds(pl.multiple_of(PAD + lo * block, 8), PAD), :] = jnp.zeros((PAD, lanes), jnp.float32)
        matrix = pick[...].astype(jnp.bfloat16)

        def spread(b, n):
            base = pl.multiple_of(PAD + b * block, 8)
            at = pl.ds(b * WIDE // 2, n * WIDE // 2)
            packed = land[t, at] if early else stage[at]
            packed = packed.reshape(n * block, wl)
            got = jnp.dot(packed, matrix, preferred_element_type=jnp.float32)
            east, north, south = got[:, :lanes], got[:, lanes : 2 * lanes], got[:, 2 * lanes :]
            ep[slot, pl.ds(base, n * block), :] = jnp.maximum(east, 0.0)
            wm[slot, pl.ds(base + stride, n * block), :] = jnp.minimum(east, 0.0)
            npos[slot, pl.ds(base, n * block), :] = jnp.maximum(north, 0.0)
            sneg[slot, pl.ds(base, n * block), :] = jnp.minimum(south, 0.0)

        def one(b, carry):
            spread(b, 1)
            return carry

        def many(i, carry):
            spread(edge_blocks + i * together, together)
            return carry

        if span is not None:
            b = span[0]
            while b < span[1]:
                n = min(3, span[1] - b)
                spread(b, n)
                b += n
            return
        lax.fori_loop(lo, edge_blocks, one, 0)
        lax.fori_loop(0, own_blocks // together, many, 0)
        lax.fori_loop(edge_blocks + own_blocks, hi, one, 0)

    def advance(t, slot, span=None):
        s = t // hours_sec
        h = t - s * hours_sec
        lo, hi = lowest(t), highest(t)

        if span is not None:
            slot = jnp.where(h == 0, s, 0)
        else:

            @pl.when(h == 0)
            def _():
                def body(b, carry):
                    at = pl.ds(pl.multiple_of(PAD + b * block, 8), block)
                    state[at, :] += inj[slot, at, :]
                    return carry

                lax.fori_loop(lo, hi, body, 0)

        add_flux(s, h, ground() if span is None else ground() + ground(inj.at[slot]))
        mix = lhs[0:deep, 0 : 3 * deep].astype(jnp.bfloat16)
        where = slot_of(t)

        def at_block(b):
            return PAD + b * block if span is not None else pl.multiple_of(PAD + b * block, 8)

        def mixing_of(b):
            base = at_block(b)
            parts = [state[pl.ds(base + k * deep, deep), :] for k in range(2)]
            if span is not None:
                parts = [x + inj[slot, pl.ds(base + k * deep, deep), :] for k, x in enumerate(parts)]
            x = jnp.concatenate(parts, axis=1)
            low = x - x.astype(jnp.bfloat16).astype(jnp.float32)
            stack = jnp.concatenate([x, x, low], axis=0).astype(jnp.bfloat16)
            return jnp.dot(mix, stack, preferred_element_type=jnp.float32)

        def keep_mixed(b, got):
            base = at_block(b)
            mixed[pl.ds(base, deep), :] = got[:, :lanes]
            mixed[pl.ds(base + deep, deep), :] = got[:, lanes:]

        def advect(b):
            base = at_block(b)
            at = pl.ds(base, block)
            here = mixed[at, :]
            after = mixed[pl.ds(base + stride, block), :]
            before = mixed[pl.ds(base - stride, block), :]
            g = here + ep[where, at, :] * (after - here) + wm[where, at, :] * (here - before)
            above = pltpu.roll(g, lanes - 1, 1)
            below = pltpu.roll(g, 1, 1)
            return g + npos[where, at, :] * (above - g) + sneg[where, at, :] * (g - below)

        def keep_state(b, x):
            state[pl.ds(at_block(b), block), :] = x

        def only_mix(b, carry):
            keep_mixed(b, mixing_of(b))
            return carry

        def both(b, carry):
            got = mixing_of(b)
            new = advect(b - 2)
            keep_state(b - 2, new)
            keep_mixed(b, got)
            return carry

        def only_advect(b, carry):
            keep_state(b, advect(b))
            return carry

        if span is not None:
            for b in range(span[0], span[1] + 2):
                got = mixing_of(b) if b < span[1] else None
                if b >= span[0] + 2:
                    keep_state(b - 2, advect(b - 2))
                if b < span[1]:
                    keep_mixed(b, got)
            return
        lax.fori_loop(lo, lo + 2, only_mix, 0)
        lax.fori_loop(lo + 2, hi, both, 0)
        lax.fori_loop(hi - 2, hi, only_advect, 0)

    def ground_copy():
        return remote(in0.at[0], in0.at[1], gs.at[0], gr.at[1], me, sides[1], core)

    def hand_ground():
        @pl.when(me > 0)
        def _():
            remote(in0.at[0], in0.at[0], gs.at[0], gr.at[0], me, sides[0], core).wait_recv()

        ground_copy().start()

    def prepare_ground():
        remote(in0.at[1], in0.at[1], gs.at[0], gr.at[1], me, sides[0], core).wait_recv()
        matrix = pick[...].astype(jnp.bfloat16)
        got = jnp.dot(in0[0].astype(jnp.bfloat16), matrix, preferred_element_type=jnp.float32)
        west = jnp.dot(
            in0[1].astype(jnp.bfloat16), matrix[:, :lanes], preferred_element_type=jnp.float32
        )
        east, north, south = got[:, :lanes], got[:, lanes : 2 * lanes], got[:, 2 * lanes :]
        faces0[0, 0:cols, :] = jnp.maximum(east, 0.0)
        faces0[1, 1 : cols + 1, :] = jnp.minimum(east, 0.0)
        faces0[1, 0:1, :] = jnp.minimum(west[cols - 1 : cols], 0.0)
        faces0[2, 0:cols, :] = jnp.maximum(north, 0.0)
        faces0[3, 0:cols, :] = jnp.minimum(south, 0.0)

    def last_step(span):
        add_flux(0, 1, ground())
        mix = lhs0[:, 0 : 3 * deep].astype(jnp.bfloat16)
        for b in range(*span):
            base = PAD + b * block
            x = jnp.concatenate([state[pl.ds(base + k * deep, deep), :] for k in range(2)], axis=1)
            low = x - x.astype(jnp.bfloat16).astype(jnp.float32)
            stack = jnp.concatenate([x, x, low], axis=0).astype(jnp.bfloat16)
            got = jnp.dot(mix, stack, preferred_element_type=jnp.float32)
            mixed0[b * WIDE : b * WIDE + 2, :] = got[0:2, :lanes]
            mixed0[b * WIDE + 2 : b * WIDE + 4, :] = got[0:2, lanes:]
        here = mixed0[halo : halo + cols, :]
        after = mixed0[halo + 1 : halo + cols + 1, :]
        before = mixed0[halo - 1 : halo + cols - 1, :]
        faces = [faces0[k, 0:cols, :] for k in range(4)]
        g = here + faces[0] * (after - here) + faces[1] * (here - before)
        above = pltpu.roll(g, lanes - 1, 1)
        below = pltpu.roll(g, 1, 1)
        add_flux(0, 0, g + faces[2] * (above - g) + faces[3] * (g - below))

    def finish_obs():
        obs_targets(lambda s, tm: obs_send(s, tm).wait_send())

        def sent_obs(s):
            for n in beside:
                obs_copy(s, n).wait_send()

        loop(sections - 1, 1, sent_obs)
        if early:
            ground_copy().wait_send()

            @pl.when(me == 0)
            def _():
                for target in range(1, sections):
                    out_copy(target).wait_send()

    def sent_winds(t):
        @pl.when(me != t // hours_sec)
        def _():
            half_copy(t).wait_send()

        def act(depth):
            for c in range(2):

                @pl.when(core == c)
                def _():
                    for side, sender, a, b in edges(depth):
                        if sender == c:
                            for q in range(2):
                                edge_copy(t, side, sender, a, b, q).wait_send()

        with_depth(t, act)

    def loop(high, low, run):
        def body(i, carry):
            run(high - i)
            return carry

        lax.fori_loop(0, high - low + 1, body, 0)

    if early:

        loop(hours_sec - 1, home, lambda h: hand_winds(me * hours_sec + h))
        hand_obs(sections - 1)
        second()
        for s in range(sections - 1, 0, -1):
            hand_obs(s - 1)
            inject(s, s)
        surface(0, 0)
        third()
        far = (lowest(hours - 1), highest(hours - 1))
        near = (lowest(middle), highest(middle))

        code = 0
        for z in range(sections):
            mine = [t for t in range(hours - 1, 1, -1) if t // hours_sec == z]
            low_hours = [t for t in range(middle - 1, 1, -1) if t not in mine]
            high_hours = [t for t in range(hours - 1, middle - 1, -1) if t not in mine]
            if z < half_way:
                high_hours.sort(key=lambda t: (-(t % hours_sec), -t))
                order = mine + low_hours + high_hours
            else:
                order = mine + high_hours + low_hours
            code = jnp.where(me == z, sum(t * hours**k for k, t in enumerate(order)), code)

        def ready(i, code):
            t = lax.rem(code, hours)
            code = code // hours
            after = lax.rem(code, hours)
            pl.when(me != after // hours_sec)(lambda: hand_winds(after))
            take_winds(t)
            pl.when(t >= middle + 1)(lambda: prepare(t, far))
            pl.when(t <= middle)(lambda: prepare(t, near))
            sent_winds(t)
            pl.when(i == hours - 5)(lambda: advance(hours - 1, 0, far))
            return code

        foremost = lax.rem(code, hours)
        pl.when(me != foremost // hours_sec)(lambda: hand_winds(foremost))
        final = lax.fori_loop(0, hours - 3, ready, code)
        hand_ground()
        loop(hours - 2, middle + 1, lambda t: advance(t, 0, far))
        prepare_ground()
        take_winds(final)
        prepare(final, near)
        loop(middle, 2, lambda t: advance(t, 0, near))
        last_step(near)
    else:
        loop(sections - 1, 0, hand_obs)
        surface(0, 0)

        def whole(t):
            s = t // hours_sec

            @pl.when(t == s * hours_sec)
            def _():
                inject(s, 0)

            hand_winds(t)
            take_winds(t)
            prepare(t)
            advance(t, 0)

        loop(hours - 1, 1, whole)

    if not early:
        add_flux(0, 0, ground())
    for w in range(d["weeks"]):
        square = flux[w] * flux[w]
        est[w] = (square + pltpu.roll(square, lanes - window, 1)) * 0.5

    if early:
        finish_lower()
        finish_upper()
        finish_obs()
        sent_winds(final)
    else:
        every_job(sent)
        finish_obs()
        loop(hours - 1, 1, sent_winds)


def on_device(winds, mixing, obs_cell, obs_weight, probe_sign, week_map, prior_precision):
    week_count, _, own = prior_precision.shape
    d = plan(
        lax.axis_size("tm"), lax.axis_size("lon"), winds.shape[2], winds.shape[4], winds.shape[3],
        winds.shape[5], own, probe_sign.shape[0], week_count, obs_cell.shape[2],
    )
    sections, hours, hours_sec = d["sections"], d["hours"], d["hours_sec"]
    lanes, rows, cols, left = d["lanes"], d["rows"], d["cols"], d["left"]
    early = d["early"]
    wire = (d["half"], 2 * d["stride"], 2 * d["window"])
    landing = (hours, d["pairs"]) + wire[1:]
    slots = hours if early else 1
    inj_slots = sections if early else 1
    sem = pltpu.SemaphoreType.DMA
    scratch = [
        pltpu.VMEM((hours_sec, sections) + wire, jnp.bfloat16),
        pltpu.VMEM((2 * d["half"] * d["stride"], 2 * d["window"]), jnp.float32),
        pltpu.VMEM((sections, 3, 1 + d["probes"], 1, d["count"] + 128), jnp.float32),
        pltpu.VMEM((128, 256), jnp.float32),
        pltpu.VMEM((2 * d["window"], 3 * lanes), jnp.float32),
        pltpu.VMEM((rows, lanes), jnp.float32),
        pltpu.VMEM((rows, lanes), jnp.float32),
        pltpu.VMEM((inj_slots, rows, lanes), jnp.float32),
    ] + [pltpu.VMEM((slots, rows, lanes), jnp.float32)] * 4 + [
        pltpu.VMEM((week_count, cols, lanes), jnp.float32),
        pltpu.VMEM((sections, cols, 2 * d["window"]), jnp.float32),
        pltpu.VMEM((2, cols, 2 * d["window"]), jnp.float32),
        pltpu.VMEM((8, 256), jnp.float32),
        pltpu.VMEM((d["blocks"] * WIDE, lanes), jnp.float32),
        pltpu.VMEM((4, cols + 4, lanes), jnp.float32),
        sem((sections + 1,)), sem((2,)),
        sem((hours_sec, sections, 2)), sem((hours, 2)), sem((hours,)), sem((hours,)),
        sem((hours, 2, 2)), sem((hours, 2, 2)), sem((sections, sections)), sem((sections,)),
        sem((sections, 2)), sem((sections, 2)), sem((1,)),
    ]
    outs = [jax.ShapeDtypeStruct((week_count, cols, lanes), jnp.float32)]
    out_specs = [pl.BlockSpec(memory_space=pltpu.VMEM)]
    if early:
        scratch = [pltpu.VMEM(landing, jnp.bfloat16)] + scratch
    else:
        outs.append(jax.ShapeDtypeStruct(landing, jnp.bfloat16))
        out_specs.append(pl.BlockSpec(memory_space=pl.ANY))
        scratch = [pltpu.VMEM(landing[1:], jnp.bfloat16)] + scratch
    got = pl.pallas_call(
        functools.partial(fused_kernel, d),
        out_shape=tuple(outs),
        in_specs=[pl.BlockSpec(memory_space=pltpu.VMEM)] * 6,
        out_specs=tuple(out_specs),
        scratch_shapes=scratch,
        compiler_params=pltpu.CompilerParams(
            collective_id=0, has_side_effects=True, vmem_limit_bytes=(51 if early else 56) << 20
        ),
    )(
        winds.transpose(0, 1, 2, 4, 3, 5), mixing, obs_cell[0], obs_weight[0],
        probe_sign[:, 0], week_map,
    )
    return (prior_precision + got[0][..., left : left + own])[None]


def solution(mesh):
    placed = (
        P(None, ("groups", "tm"), None, None, "lon", None),
        P(),
        P(("groups", "tm"), "lon", None),
        P(("groups", "tm"), "lon", None),
        P("probe", ("groups", "tm"), "lon", None),
        P(("groups", "tm"), None),
        P("groups", "lon", "tm"),
    )
    return jax.shard_map(
        on_device,
        mesh=mesh,
        in_specs=placed,
        out_specs=P("probe", "groups", "lon", "tm"),
        check_vma=False,
    )
```

```python
import functools

import jax
import jax.numpy as jnp
from jax import lax
from jax.experimental import pallas as pl
from jax.experimental.pallas import tpu as pltpu
from jax.sharding import PartitionSpec as P

WIDE = 4
PAD = 40


def split2(x):
    high = x.astype(jnp.bfloat16)
    low = (x - high.astype(jnp.float32)).astype(jnp.bfloat16)
    return high, low


def plan(sections, bands, hours_sec, cols, levels, lat_rows, own, probes, weeks, count):
    hours = sections * hours_sec
    halo = -(-hours // WIDE) * WIDE
    window = -(-(own + 2 * hours) // 64) * 64
    d = dict(
        sections=sections, bands=bands, hours_sec=hours_sec, cols=cols, levels=levels,
        lat_rows=lat_rows, own=own, probes=probes, weeks=weeks, count=count, hours=hours,
        halo=halo, left=hours, window=window, lanes=window * probes,
        half=cols // 4, halo_pairs=halo // 2, pairs=(cols + 2 * halo) // 2,
        blocks=(cols + 2 * halo) // WIDE,
    )
    d["stride"] = levels if d["lanes"] == 128 else -(-levels // 8) * 8
    d["block"] = WIDE * d["stride"]
    d["rows"] = PAD + (d["blocks"] + 1) * d["block"]
    d["early"] = hours <= 8 and hours_sec == 2 and sections % 2 == 0
    return d


def fused_kernel(d, winds, mixing, cell, weight, sign, week, *refs):
    sections, bands, hours_sec, hours = d["sections"], d["bands"], d["hours_sec"], d["hours"]
    cols, levels, lat_rows, own = d["cols"], d["levels"], d["lat_rows"], d["own"]
    probes, count, halo, left = d["probes"], d["count"], d["halo"], d["left"]
    window, lanes, half, halo_pairs = d["window"], d["lanes"], d["half"], d["halo_pairs"]
    block, early, stride = d["block"], d["early"], d["stride"]
    if early:
        est, land, refs = refs[0], refs[1], refs[2:]
        stage = None
    else:
        est, land, stage, refs = refs[0], refs[1], refs[2], refs[3:]
    (pack, flat, obs, lhs, pick, state, mixed, inj, ep, wm, npos, sneg, flux,
     out0, in0, lhs0, mixed0, faces0, gs, gr, zs, zr, hs, hr, xs, xr, os, orr, us, ur, local) = refs
    own_pairs = 2 * half
    me = lax.axis_index("tm")
    band = lax.axis_index("lon")
    core = lax.axis_index("probe")
    sides = [lax.rem(band + bands - 1, bands), lax.rem(band + 1, bands)]
    if bands == 2:
        greet = sides[:1]
    else:
        greet = sides

    def remote(src, dst, send, recv, tm, lon, probe):
        return pltpu.make_async_remote_copy(
            src_ref=src, dst_ref=dst, send_sem=send, recv_sem=recv,
            device_id={"tm": tm, "lon": lon, "probe": probe},
            device_id_type=pl.DeviceIdType.MESH,
        )

    if early:
        for t in range(2, hours):
            reach = (t + 1) // 2
            for n in range((halo - t) // WIDE * WIDE // 2, halo_pairs - reach):
                land[t, n] = jnp.zeros(land.shape[2:], land.dtype)
                land[t, 2 * halo_pairs + own_pairs - 1 - n] = jnp.zeros(land.shape[2:], land.dtype)

    barrier = pltpu.get_barrier_semaphore()

    def hello(tm, lon, probe):
        pl.semaphore_signal(
            barrier, inc=1, device_id={"tm": tm, "lon": lon, "probe": probe},
            device_id_type=pl.DeviceIdType.MESH,
        )

    for k in range(1, sections):
        hello(lax.rem(me + k, sections), band, core)
    for lon in greet:
        for q in range(2):
            hello(me, lon, q)
    hello(me, band, 1 - core)

    obs[me, 0, 0, :, 0:count] = cell[...].astype(jnp.float32)
    for p in range(probes):
        obs[me, 0, 1 + p, :, 0:count] = (2 * sign[p] - 1).astype(jnp.float32) * weight[...]
        obs[me, 0, 1 + p, :, count:] = jnp.zeros((1, 128), jnp.float32)
    lane_row = lax.broadcasted_iota(jnp.int32, (1, 128), 1)
    weeks_row = jnp.zeros((1, 128), jnp.float32)
    for h in range(hours_sec):
        weeks_row = jnp.where(lane_row == h, week[0:1, h : h + 1].astype(jnp.float32), weeks_row)
    obs[me, 0, 0, :, count:] = weeks_row

    if stride != levels:
        flat[...] = jnp.zeros_like(flat)
    wl = 2 * window
    lat_tiles = -(-lat_rows // 128)

    def packed_column(h, column, start, levels=levels):
        tiles = []
        for comp in range(2):
            row = []
            for k in range(lat_tiles):
                x = winds[comp, 0, h, column, 0:levels, k * 128 : min(k * 128 + 128, lat_rows)]
                x = x.astype(jnp.float32)
                if x.shape[1] < 128:
                    x = jnp.concatenate(
                        [x, jnp.zeros((levels, 128 - x.shape[1]), jnp.float32)], axis=1
                    )
                row.append(x)
            tiles.append(row)
        lane = lax.broadcasted_iota(jnp.int32, (levels, 128), 1)
        parts = []
        for v in range(wl // 128):
            out = jnp.zeros((levels, 128), jnp.float32)
            for comp in range(2):
                begin = comp * window - v * 128
                if begin >= 128 or begin + window <= 0:
                    continue
                shift = lax.rem(begin - start + 512, 128)
                at = lane - begin
                row = at + start
                for k in range(lat_tiles):
                    inside = (
                        (at >= 0) & (at < window) & (row >= k * 128)
                        & (row < min(k * 128 + 128, lat_rows))
                    )
                    out = jnp.where(inside, pltpu.roll(tiles[comp][k], shift, 1), out)
            parts.append(out)
        return parts[0] if len(parts) == 1 else jnp.concatenate(parts, axis=1)

    def fill(h, target, first_column, put):
        start = target * own - left

        def body(i, carry):
            for c in range(2):
                at = pl.multiple_of(i * 2 * stride, 8) + c * stride
                flat[pl.ds(at, levels), :] = packed_column(h, first_column + 2 * i + c, start)
            return carry

        lax.fori_loop(0, half, body, 0, unroll=3)

        def cast(i, carry):
            x = flat[pl.ds(pl.multiple_of(i * 2 * stride, 8), 2 * stride), :]
            put(i, x.astype(jnp.bfloat16))
            return carry

        lax.fori_loop(0, half, cast, 0, unroll=3)

    least = jnp.where(me == 0, 1, 0)
    my_pairs = halo_pairs + half * core

    if early:
        parts = [((half - halo_pairs) * core, halo_pairs), (halo_pairs * (1 - core), half - halo_pairs)]
    else:
        parts = [(0, half)]

    def z_copy(h, target, n):
        t = me * hours_sec + h
        begin, size = parts[n]
        return remote(
            pack.at[h, target, pl.ds(begin, size)], land.at[t, pl.ds(my_pairs + begin, size)],
            zs.at[h, target, n], zr.at[t, n], target, band, core,
        )

    def came(t, n):
        begin, size = parts[n]
        place = land.at[t, pl.ds(my_pairs + begin, size)]
        remote(place, place, zs.at[0, 0, n], zr.at[t, n], me, sides[0], core).wait_recv()

    def start(h, target):
        for n in range(len(parts)):
            z_copy(h, target, n).start()

    def sent(h, target):
        for n in range(len(parts)):
            z_copy(h, target, n).wait_send()

    def job(h, target):
        def put(i, x):
            pack[h, target, i] = x

        fill(h, target, 2 * half * core, put)
        start(h, target)

    def every_job(run):
        def upper(i, carry):
            h = hours_sec - 1 - i

            def target(k, inner):
                run(h, sections - 1 - k)
                return inner

            return lax.fori_loop(0, sections - 1 - me, target, carry)

        lax.fori_loop(0, hours_sec - least, upper, 0)

        def lower(i, carry):
            h = hours_sec - 1 - i

            def target(k, inner):
                run(h, k)
                return inner

            return lax.fori_loop(0, me, target, carry)

        lax.fori_loop(0, hours_sec - least, lower, 0)

    last = hours_sec - 1
    if early:
        half_way = sections // 2
        top = me == sections - 1
        beyond = jnp.where(top, 0, me + 1)

        def put_first(i, x):
            pack[last, beyond, i] = x

        pl.when(me > 0)(lambda: fill(last, beyond, 2 * half * core, put_first))

    pl.semaphore_wait(barrier, sections - 1 + 2 * len(greet) + 1)

    def obs_send(s, tm):
        mine = obs.at[s, 0]
        return remote(mine, mine, os.at[s, tm], orr.at[s], tm, band, core)

    def obs_targets(act):
        for k in range(1, sections):
            act(me, lax.rem(me + k, sections))

    obs_targets(lambda s, tm: obs_send(s, tm).start())

    def each(run, h, low, high):
        def body(i, carry):
            run(h, low + i)
            return carry

        lax.fori_loop(0, high - low, body, 0)

    def fill_job(h, target):
        def put(i, x):
            pack[h, target, i] = x

        fill(h, target, 2 * half * core, put)

    if early:
        lower = me < half_way
        upper = (me >= half_way) & (me < sections - 1)
        pl.when(me > 0)(lambda: start(last, beyond))
        many = jnp.where(top, half_way, jnp.where(me > 0, sections, beyond + 1))
        each(job, last, beyond + 1, many)
        each(job, 0, me + 1, jnp.where(me >= half_way, sections, me + 1))

        def rest(run):
            each(run, 0, me + 1, jnp.where(lower & (me > 0), sections, me + 1))
            each(run, last, jnp.where(top, half_way, 0), me)
            each(run, 0, 0, me)

        rest(fill_job)

        @pl.when(lower)
        def _():
            rest(start)

    else:
        every_job(job)

    def second():
        @pl.when(upper)
        def _():
            each(start, last, 0, me)

        @pl.when(top)
        def _():
            each(start, 0, 0, half_way)
            each(start, last, half_way, me)

    def third():
        @pl.when(upper)
        def _():
            for n in range(len(parts)):
                each(lambda h, target, n=n: z_copy(h, target, n).start(), 0, 0, me)

        @pl.when(top)
        def _():
            each(start, 0, half_way, me)

    def finish_lower():
        @pl.when(lower)
        def _():
            each(sent, last, me + 1, jnp.where(me > 0, sections, me + 1))
            rest(sent)

    def finish_upper():
        @pl.when(upper)
        def _():
            each(sent, last, 0, me)
            each(sent, last, me + 1, sections)
            each(sent, 0, me + 1, sections)
            each(sent, 0, 0, me)

        @pl.when(top)
        def _():
            each(sent, last, 0, me)
            each(sent, 0, 0, me)

    def out_copy(target):
        return remote(out0.at[target], in0.at[0], gs.at[target], gr.at[0], target, band, core)

    if early:

        @pl.when(me == 0)
        def _():
            def ground_of(target, carry):
                def body(i, inner):
                    x = packed_column(last, i, target * own - left, 16)
                    out0[target, pl.ds(i, 1), :] = x[0:1]
                    return inner

                lax.fori_loop(0, cols, body, 0, unroll=6)
                pl.when(target > 0)(lambda: out_copy(target).start())
                return carry

            lax.fori_loop(0, sections, ground_of, 0)
            in0[0] = out0[0]

    def at_home(i, carry):
        h = hours_sec - 1 - i
        t = me * hours_sec + h
        for c in range(2):
            if early:

                def put(i, x):
                    land[t, halo_pairs + half * c + i] = x

                fill(h, me, 2 * half * c, put)
            else:

                def put(i, x):
                    pack[h, me, i] = x

                fill(h, me, 2 * half * c, put)
                copy = pltpu.make_async_copy(
                    pack.at[h, me], land.at[t, pl.ds(halo_pairs + half * c, half)], local.at[0]
                )
                copy.start()
                copy.wait()
        return carry

    home = jnp.where(me == 0, hours_sec, 0) if early else least
    lax.fori_loop(0, hours_sec - home, at_home, 0)

    zero = jnp.zeros((PAD, lanes), jnp.float32)

    def clear(i, carry):
        at = pl.multiple_of(i * 8, 8)
        state[pl.ds(at, 8), :] = zero[:8]
        mixed[pl.ds(at, 8), :] = zero[:8]
        inj[0, pl.ds(at, 8), :] = zero[:8]
        return carry

    lax.fori_loop(0, d["rows"] // 8, clear, 0, unroll=8)
    flux[...] = jnp.zeros_like(flux)
    lhs[...] = jnp.zeros_like(lhs)
    lhs[0:levels, 0:levels] = mixing[...]
    turned_mix = jnp.transpose(lhs[:, 0:128])
    both = turned_mix + pltpu.roll(pltpu.roll(turned_mix, stride, 0), stride, 1)
    high = both.astype(jnp.bfloat16).astype(jnp.float32)
    low = both - high
    none = jnp.zeros_like(both)
    high = jnp.concatenate([high, none], axis=1)
    low = jnp.concatenate([low, none], axis=1)
    deep = 2 * stride
    matrix = high + pltpu.roll(low, deep, 1) + pltpu.roll(high, 2 * deep, 1)
    lhs[...] = matrix
    lhs0[...] = jnp.zeros_like(lhs0)
    for k in range(2):
        lhs0[k : k + 1, :] = matrix[k * stride : k * stride + 1]

    source = lax.broadcasted_iota(jnp.int32, (wl, lanes), 0)
    into = lax.rem(lax.broadcasted_iota(jnp.int32, (wl, lanes), 1), window)
    first_row = me * own - left
    keep = (into + first_row >= 0) & (into + first_row < lat_rows - 1)
    below = (into > 0) & (into + first_row >= 1) & (into + first_row < lat_rows)
    pick[:, :lanes] = jnp.where(source == into, 1.0, 0.0)
    pick[:, lanes : 2 * lanes] = jnp.where((source == into + window) & keep, 1.0, 0.0)
    pick[:, 2 * lanes :] = jnp.where((source == into + window - 1) & below, 1.0, 0.0)

    def obs_copy(s, n):
        return remote(
            obs.at[s, 0], obs.at[s, 1 + n], us.at[s, n], ur.at[s, n], me, sides[1 - n], core
        )

    beside = range(1 if bands == 2 else 2)

    def hand_obs(s):
        @pl.when(me != s)
        def _():
            remote(obs.at[s, 0], obs.at[s, 0], os.at[0, 0], orr.at[s], me, sides[0], core).wait_recv()

        @pl.when(s > 0)
        def _():
            for n in beside:
                obs_copy(s, n).start()

    def half_copy(t):
        place = land.at[t, pl.ds(my_pairs, half)]
        return remote(place, place, hs.at[t], hr.at[t], me, band, 1 - core)

    def edges(depth):
        found = []
        for side in range(2):
            begin = 0 if side == 0 else own_pairs - depth
            for c in range(2):
                a, b = max(begin, half * c), min(begin + depth, half * (c + 1))
                if a < b:
                    found.append((side, c, a, b))
        return found

    def edge_copy(t, side, c, a, b, q):
        to = halo_pairs + (own_pairs if side == 0 else -own_pairs)
        return remote(
            land.at[t, pl.ds(halo_pairs + a, b - a)], land.at[t, pl.ds(to + a, b - a)],
            xs.at[t, side, q], xr.at[t, side, c], me, sides[side], q,
        )

    def with_depth(t, act):
        if early:
            for depth in range(1, halo_pairs + 1):

                @pl.when((t + 1) // 2 == depth)
                def _():
                    act(depth)

        else:

            @pl.when(t > halo // 2)
            def _():
                act(halo_pairs)

            @pl.when(t <= halo // 2)
            def _():
                act(halo_pairs // 2)

    def hand_winds(t):
        s = t // hours_sec

        pl.when(me != s)(lambda: came(t, 0))

        def act(depth):
            for c in range(2):

                @pl.when(core == c)
                def _():
                    for side, sender, a, b in edges(depth):
                        if sender == c:
                            for q in range(2):
                                edge_copy(t, side, sender, a, b, q).start()

        with_depth(t, act)

        @pl.when(me != s)
        def _():
            if early:
                came(t, 1)
            half_copy(t).start()

    def take_winds(t):
        s = t // hours_sec

        @pl.when(me != s)
        def _():
            place = land.at[t, pl.ds(halo_pairs + half * (1 - core), half)]
            remote(place, place, hs.at[t], hr.at[t], me, band, 1 - core).wait_recv()

        def act(depth):
            for side, sender, a, b in edges(depth):
                edge_copy(t, side, sender, a, b, 0).wait_recv()

        with_depth(t, act)

    first_row = me * own - left

    def observed(s, piece):
        place = obs[s, piece, 0, :, 0:count].astype(jnp.int32)
        level = place // (cols * lat_rows)
        rest = place - level * (cols * lat_rows)
        column = rest // lat_rows
        row = rest - column * lat_rows - first_row
        hit = lax.broadcasted_iota(jnp.int32, (window, count), 0) == row
        parts = [
            split2(jnp.where(hit, obs[s, piece, 1 + p, :, 0:count], 0.0)) for p in range(probes)
        ]
        rhs = jnp.concatenate([x[0] for x in parts] + [x[1] for x in parts], axis=0)
        return level, column, rhs

    def placed_sum(hot, rhs):
        got = lax.dot_general(
            hot.astype(jnp.float32).astype(jnp.bfloat16), rhs, (((1,), (1,)), ((), ())),
            preferred_element_type=jnp.float32,
        )
        return got[:, :lanes] + got[:, lanes:]

    def lowest(t):
        return (halo - t) // WIDE

    def highest(t):
        return (halo + cols + t + WIDE - 1) // WIDE

    edge_blocks = halo // WIDE
    own_blocks = cols // WIDE
    together = max(n for n in range(1, 4) if own_blocks % n == 0)

    def inject(s, slot):
        t = s * hours_sec
        for n in beside:
            remote(
                obs.at[s, 0], obs.at[s, 1 + n], us.at[s, n], ur.at[s, n], me, sides[0], core
            ).wait_recv()
        if early:
            lo, hi = lowest(t), highest(t)
            ranges = [
                (0, [(halo, edge_blocks, edge_blocks + own_blocks)]),
                (1, [(halo - cols, lo, edge_blocks)]),
                (2 if bands > 2 else 1, [(halo + cols, edge_blocks + own_blocks, hi)]),
            ]
            if bands == 2:
                ranges = [ranges[0], (1, ranges[1][1] + ranges[2][1])]
            for piece, places in ranges:
                level, column, rhs = observed(s, piece)
                hots = []
                for shift, begin, end in places:
                    place = (column + shift) * stride + level - begin * block
                    chunk = lax.broadcasted_iota(jnp.int32, ((end - begin) * block, count), 0)
                    hots.append((chunk == place).astype(jnp.float32).astype(jnp.bfloat16))
                hot = hots[0] if len(hots) == 1 else jnp.concatenate(hots, axis=0)
                got = lax.dot_general(
                    hot, rhs, (((1,), (1,)), ((), ())), preferred_element_type=jnp.float32
                )
                add = got[:, :lanes] + got[:, lanes:]
                done = 0
                for shift, begin, end in places:
                    size = (end - begin) * block
                    inj[slot, pl.ds(PAD + begin * block, size), :] = add[done : done + size]
                    done += size
            return
        for piece, shift, begin, end, step in (
            (0, halo, edge_blocks, edge_blocks + own_blocks, together),
            (1, halo - cols, lowest(t), edge_blocks, 1),
            (2 if bands > 2 else 1, halo + cols, edge_blocks + own_blocks, highest(t), 1),
        ):
            level, column, rhs = observed(s, piece)
            place = (column + shift) * stride + level
            high_rows = step * block
            chunk = lax.broadcasted_iota(jnp.int32, (high_rows, count), 0)

            def body(i, carry, begin=begin, step=step, place=place, rhs=rhs, chunk=chunk, high_rows=high_rows):
                b = begin + i * step
                add = placed_sum(chunk == place - b * block, rhs)
                inj[slot, pl.ds(pl.multiple_of(PAD + b * block, 8), high_rows), :] = add
                return carry

            lax.fori_loop(0, (end - begin) // step, body, 0)

    def ground(field=state):
        start = PAD + halo * stride
        if lanes == 128:
            return field[pl.ds(start, cols, stride=stride), :]
        rows = [state[start + c * stride : start + c * stride + 1, :] for c in range(cols)]
        return jnp.concatenate(rows, axis=0)

    def add_flux(s, h, x):
        which = obs[s, 0, 0, :, count:]
        lane = lax.broadcasted_iota(jnp.int32, (1, 128), 1)
        number = jnp.sum(jnp.where(lane == h, which, 0.0), axis=1, keepdims=True)
        for w in range(d["weeks"]):
            flux[w] += jnp.where(number == w, x, 0.0)

    def surface(s, slot):
        level, column, rhs = observed(0, 0)
        tall = -(-cols // 8) * 8
        chunk = lax.broadcasted_iota(jnp.int32, (tall, count), 0)
        add = placed_sum(chunk == jnp.where(level == 0, column, -1), rhs)
        add_flux(0, 0, add[:cols])

    middle = hours // 2

    def slot_of(t):
        return t if early else 0

    def prepare(t, span=None):
        slot = slot_of(t)
        if not early:
            copy = pltpu.make_async_copy(land.at[t], stage, local.at[0])
            copy.start()
            copy.wait()
        lo, hi = lowest(t), highest(t)
        wm[slot, pl.ds(pl.multiple_of(PAD + lo * block, 8), PAD), :] = jnp.zeros((PAD, lanes), jnp.float32)
        matrix = pick[...].astype(jnp.bfloat16)

        def spread(b, n):
            base = pl.multiple_of(PAD + b * block, 8)
            at = pl.ds(b * WIDE // 2, n * WIDE // 2)
            packed = land[t, at] if early else stage[at]
            packed = packed.reshape(n * block, wl)
            got = jnp.dot(packed, matrix, preferred_element_type=jnp.float32)
            east, north, south = got[:, :lanes], got[:, lanes : 2 * lanes], got[:, 2 * lanes :]
            ep[slot, pl.ds(base, n * block), :] = jnp.maximum(east, 0.0)
            wm[slot, pl.ds(base + stride, n * block), :] = jnp.minimum(east, 0.0)
            npos[slot, pl.ds(base, n * block), :] = jnp.maximum(north, 0.0)
            sneg[slot, pl.ds(base, n * block), :] = jnp.minimum(south, 0.0)

        def one(b, carry):
            spread(b, 1)
            return carry

        def many(i, carry):
            spread(edge_blocks + i * together, together)
            return carry

        if span is not None:
            b = span[0]
            while b < span[1]:
                n = min(3, span[1] - b)
                spread(b, n)
                b += n
            return
        lax.fori_loop(lo, edge_blocks, one, 0)
        lax.fori_loop(0, own_blocks // together, many, 0)
        lax.fori_loop(edge_blocks + own_blocks, hi, one, 0)

    def advance(t, slot, span=None):
        s = t // hours_sec
        h = t - s * hours_sec
        lo, hi = lowest(t), highest(t)

        if span is not None:
            slot = jnp.where(h == 0, s, 0)
        else:

            @pl.when(h == 0)
            def _():
                def body(b, carry):
                    at = pl.ds(pl.multiple_of(PAD + b * block, 8), block)
                    state[at, :] += inj[slot, at, :]
                    return carry

                lax.fori_loop(lo, hi, body, 0)

        add_flux(s, h, ground() if span is None else ground() + ground(inj.at[slot]))
        mix = lhs[0:deep, 0 : 3 * deep].astype(jnp.bfloat16)
        where = slot_of(t)

        def at_block(b):
            return PAD + b * block if span is not None else pl.multiple_of(PAD + b * block, 8)

        def mixing_of(b):
            base = at_block(b)
            parts = [state[pl.ds(base + k * deep, deep), :] for k in range(2)]
            if span is not None:
                parts = [x + inj[slot, pl.ds(base + k * deep, deep), :] for k, x in enumerate(parts)]
            x = jnp.concatenate(parts, axis=1)
            low = x - x.astype(jnp.bfloat16).astype(jnp.float32)
            stack = jnp.concatenate([x, x, low], axis=0).astype(jnp.bfloat16)
            return jnp.dot(mix, stack, preferred_element_type=jnp.float32)

        def keep_mixed(b, got):
            base = at_block(b)
            mixed[pl.ds(base, deep), :] = got[:, :lanes]
            mixed[pl.ds(base + deep, deep), :] = got[:, lanes:]

        def advect(b):
            base = at_block(b)
            at = pl.ds(base, block)
            here = mixed[at, :]
            after = mixed[pl.ds(base + stride, block), :]
            before = mixed[pl.ds(base - stride, block), :]
            g = here + ep[where, at, :] * (after - here) + wm[where, at, :] * (here - before)
            above = pltpu.roll(g, lanes - 1, 1)
            below = pltpu.roll(g, 1, 1)
            return g + npos[where, at, :] * (above - g) + sneg[where, at, :] * (g - below)

        def keep_state(b, x):
            state[pl.ds(at_block(b), block), :] = x

        def only_mix(b, carry):
            keep_mixed(b, mixing_of(b))
            return carry

        def both(b, carry):
            got = mixing_of(b)
            new = advect(b - 2)
            keep_state(b - 2, new)
            keep_mixed(b, got)
            return carry

        def only_advect(b, carry):
            keep_state(b, advect(b))
            return carry

        if span is not None:
            for b in range(span[0], span[1] + 2):
                got = mixing_of(b) if b < span[1] else None
                if b >= span[0] + 2:
                    keep_state(b - 2, advect(b - 2))
                if b < span[1]:
                    keep_mixed(b, got)
            return
        lax.fori_loop(lo, lo + 2, only_mix, 0)
        lax.fori_loop(lo + 2, hi, both, 0)
        lax.fori_loop(hi - 2, hi, only_advect, 0)

    def ground_copy():
        return remote(in0.at[0], in0.at[1], gs.at[0], gr.at[1], me, sides[1], core)

    def hand_ground():
        @pl.when(me > 0)
        def _():
            remote(in0.at[0], in0.at[0], gs.at[0], gr.at[0], me, sides[0], core).wait_recv()

        ground_copy().start()

    def prepare_ground():
        remote(in0.at[1], in0.at[1], gs.at[0], gr.at[1], me, sides[0], core).wait_recv()
        matrix = pick[...].astype(jnp.bfloat16)
        got = jnp.dot(in0[0].astype(jnp.bfloat16), matrix, preferred_element_type=jnp.float32)
        west = jnp.dot(
            in0[1].astype(jnp.bfloat16), matrix[:, :lanes], preferred_element_type=jnp.float32
        )
        east, north, south = got[:, :lanes], got[:, lanes : 2 * lanes], got[:, 2 * lanes :]
        faces0[0, 0:cols, :] = jnp.maximum(east, 0.0)
        faces0[1, 1 : cols + 1, :] = jnp.minimum(east, 0.0)
        faces0[1, 0:1, :] = jnp.minimum(west[cols - 1 : cols], 0.0)
        faces0[2, 0:cols, :] = jnp.maximum(north, 0.0)
        faces0[3, 0:cols, :] = jnp.minimum(south, 0.0)

    def last_step(span):
        add_flux(0, 1, ground())
        mix = lhs0[:, 0 : 3 * deep].astype(jnp.bfloat16)
        for b in range(*span):
            base = PAD + b * block
            x = jnp.concatenate([state[pl.ds(base + k * deep, deep), :] for k in range(2)], axis=1)
            low = x - x.astype(jnp.bfloat16).astype(jnp.float32)
            stack = jnp.concatenate([x, x, low], axis=0).astype(jnp.bfloat16)
            got = jnp.dot(mix, stack, preferred_element_type=jnp.float32)
            mixed0[b * WIDE : b * WIDE + 2, :] = got[0:2, :lanes]
            mixed0[b * WIDE + 2 : b * WIDE + 4, :] = got[0:2, lanes:]
        here = mixed0[halo : halo + cols, :]
        after = mixed0[halo + 1 : halo + cols + 1, :]
        before = mixed0[halo - 1 : halo + cols - 1, :]
        faces = [faces0[k, 0:cols, :] for k in range(4)]
        g = here + faces[0] * (after - here) + faces[1] * (here - before)
        above = pltpu.roll(g, lanes - 1, 1)
        below = pltpu.roll(g, 1, 1)
        add_flux(0, 0, g + faces[2] * (above - g) + faces[3] * (g - below))

    def finish_obs():
        obs_targets(lambda s, tm: obs_send(s, tm).wait_send())

        def sent_obs(s):
            for n in beside:
                obs_copy(s, n).wait_send()

        loop(sections - 1, 1, sent_obs)
        if early:
            ground_copy().wait_send()

            @pl.when(me == 0)
            def _():
                for target in range(1, sections):
                    out_copy(target).wait_send()

    def sent_winds(t):
        @pl.when(me != t // hours_sec)
        def _():
            half_copy(t).wait_send()

        def act(depth):
            for c in range(2):

                @pl.when(core == c)
                def _():
                    for side, sender, a, b in edges(depth):
                        if sender == c:
                            for q in range(2):
                                edge_copy(t, side, sender, a, b, q).wait_send()

        with_depth(t, act)

    def loop(high, low, run):
        def body(i, carry):
            run(high - i)
            return carry

        lax.fori_loop(0, high - low + 1, body, 0)

    if early:

        loop(hours_sec - 1, home, lambda h: hand_winds(me * hours_sec + h))
        hand_obs(sections - 1)
        second()
        for s in range(sections - 1, 0, -1):
            hand_obs(s - 1)
            inject(s, s)
        surface(0, 0)
        third()
        far = (lowest(hours - 1), highest(hours - 1))
        near = (lowest(middle), highest(middle))

        code = 0
        for z in range(sections):
            mine = [t for t in range(hours - 1, 1, -1) if t // hours_sec == z]
            low_hours = [t for t in range(middle - 1, 1, -1) if t not in mine]
            high_hours = [t for t in range(hours - 1, middle - 1, -1) if t not in mine]
            if z < half_way:
                order = mine + low_hours + high_hours
            else:
                order = mine + high_hours + low_hours
            code = jnp.where(me == z, sum(t * hours**k for k, t in enumerate(order)), code)

        def ready(i, code):
            t = lax.rem(code, hours)
            code = code // hours
            after = lax.rem(code, hours)
            pl.when(me != after // hours_sec)(lambda: hand_winds(after))
            take_winds(t)
            pl.when(t >= middle + 1)(lambda: prepare(t, far))
            pl.when(t <= middle)(lambda: prepare(t, near))
            sent_winds(t)
            pl.when(i == hours - 5)(
                lambda: loop(hours - 1, middle + 2, lambda t: advance(t, 0, far))
            )
            return code

        foremost = lax.rem(code, hours)
        pl.when(me != foremost // hours_sec)(lambda: hand_winds(foremost))
        final = lax.fori_loop(0, hours - 3, ready, code)
        hand_ground()
        advance(middle + 1, 0, far)
        prepare_ground()
        take_winds(final)
        prepare(final, near)
        loop(middle, 2, lambda t: advance(t, 0, near))
        last_step(near)
    else:
        loop(sections - 1, 0, hand_obs)
        surface(0, 0)

        def whole(t):
            s = t // hours_sec

            @pl.when(t == s * hours_sec)
            def _():
                inject(s, 0)

            hand_winds(t)
            take_winds(t)
            prepare(t)
            advance(t, 0)

        loop(hours - 1, 1, whole)

    if not early:
        add_flux(0, 0, ground())
    for w in range(d["weeks"]):
        square = flux[w] * flux[w]
        est[w] = (square + pltpu.roll(square, lanes - window, 1)) * 0.5

    if early:
        finish_lower()
        finish_upper()
        finish_obs()
        sent_winds(final)
    else:
        every_job(sent)
        finish_obs()
        loop(hours - 1, 1, sent_winds)


def on_device(winds, mixing, obs_cell, obs_weight, probe_sign, week_map, prior_precision):
    week_count, _, own = prior_precision.shape
    d = plan(
        lax.axis_size("tm"), lax.axis_size("lon"), winds.shape[2], winds.shape[4], winds.shape[3],
        winds.shape[5], own, probe_sign.shape[0], week_count, obs_cell.shape[2],
    )
    sections, hours, hours_sec = d["sections"], d["hours"], d["hours_sec"]
    lanes, rows, cols, left = d["lanes"], d["rows"], d["cols"], d["left"]
    early = d["early"]
    wire = (d["half"], 2 * d["stride"], 2 * d["window"])
    landing = (hours, d["pairs"]) + wire[1:]
    slots = hours if early else 1
    inj_slots = sections if early else 1
    sem = pltpu.SemaphoreType.DMA
    scratch = [
        pltpu.VMEM((hours_sec, sections) + wire, jnp.bfloat16),
        pltpu.VMEM((2 * d["half"] * d["stride"], 2 * d["window"]), jnp.float32),
        pltpu.VMEM((sections, 3, 1 + d["probes"], 1, d["count"] + 128), jnp.float32),
        pltpu.VMEM((128, 256), jnp.float32),
        pltpu.VMEM((2 * d["window"], 3 * lanes), jnp.float32),
        pltpu.VMEM((rows, lanes), jnp.float32),
        pltpu.VMEM((rows, lanes), jnp.float32),
        pltpu.VMEM((inj_slots, rows, lanes), jnp.float32),
    ] + [pltpu.VMEM((slots, rows, lanes), jnp.float32)] * 4 + [
        pltpu.VMEM((week_count, cols, lanes), jnp.float32),
        pltpu.VMEM((sections, cols, 2 * d["window"]), jnp.float32),
        pltpu.VMEM((2, cols, 2 * d["window"]), jnp.float32),
        pltpu.VMEM((8, 256), jnp.float32),
        pltpu.VMEM((d["blocks"] * WIDE, lanes), jnp.float32),
        pltpu.VMEM((4, cols + 4, lanes), jnp.float32),
        sem((sections + 1,)), sem((2,)),
        sem((hours_sec, sections, 2)), sem((hours, 2)), sem((hours,)), sem((hours,)),
        sem((hours, 2, 2)), sem((hours, 2, 2)), sem((sections, sections)), sem((sections,)),
        sem((sections, 2)), sem((sections, 2)), sem((1,)),
    ]
    outs = [jax.ShapeDtypeStruct((week_count, cols, lanes), jnp.float32)]
    out_specs = [pl.BlockSpec(memory_space=pltpu.VMEM)]
    if early:
        scratch = [pltpu.VMEM(landing, jnp.bfloat16)] + scratch
    else:
        outs.append(jax.ShapeDtypeStruct(landing, jnp.bfloat16))
        out_specs.append(pl.BlockSpec(memory_space=pl.ANY))
        scratch = [pltpu.VMEM(landing[1:], jnp.bfloat16)] + scratch
    got = pl.pallas_call(
        functools.partial(fused_kernel, d),
        out_shape=tuple(outs),
        in_specs=[pl.BlockSpec(memory_space=pltpu.VMEM)] * 6,
        out_specs=tuple(out_specs),
        scratch_shapes=scratch,
        compiler_params=pltpu.CompilerParams(
            collective_id=0, has_side_effects=True, vmem_limit_bytes=(51 if early else 56) << 20
        ),
    )(
        winds.transpose(0, 1, 2, 4, 3, 5), mixing, obs_cell[0], obs_weight[0],
        probe_sign[:, 0], week_map,
    )
    return (prior_precision + got[0][..., left : left + own])[None]


def solution(mesh):
    placed = (
        P(None, ("groups", "tm"), None, None, "lon", None),
        P(),
        P(("groups", "tm"), "lon", None),
        P(("groups", "tm"), "lon", None),
        P("probe", ("groups", "tm"), "lon", None),
        P(("groups", "tm"), None),
        P("groups", "lon", "tm"),
    )
    return jax.shard_map(
        on_device,
        mesh=mesh,
        in_specs=placed,
        out_specs=P("probe", "groups", "lon", "tm"),
        check_vma=False,
    )
```
